32 devices in a mesh: blk: 8 (over z, y), head: 4 (over x, core).
Axes of the slice: x: 2, y: 2, z: 4, core: 2. Of those that a mesh axis runs over, the one named last changes fastest.
Arguments:
- hidden_in: bfloat16 [2048, 768], P('blk'), may hold values from -6 to 6
- query_w: bfloat16 [768, 768], P('blk', 'head'), may hold values from -0.21875 to 0.21875
- key_w: bfloat16 [768, 768], P('blk', 'head'), may hold values from -0.21875 to 0.21875
- value_w: bfloat16 [768, 768], P('blk', 'head'), may hold values from -0.21875 to 0.21875
- output_w: bfloat16 [768, 768], P('blk', 'head'), may hold values from -1.75 to 1.75
- inner_w: bfloat16 [768, 3072], P('blk', 'head'), may hold values from -0.21875 to 0.21875
- outer_w: bfloat16 [768, 3072], P('blk', 'head'), may hold values from -0.109375 to 0.109375
- query_b: float32 [768], P('head'), may hold values from -3 to 3
- value_b: float32 [768], P('head'), may hold values from -3 to 3
- output_b: float32 [768], replicated, may hold values from -3 to 3
- inner_b: float32 [3072], P('head'), may hold values from -3 to 3
- outer_b: float32 [768], replicated, may hold values from -3 to 3
- first_gain: float32 [768], replicated, may hold values from 0.5 to 1.5
- first_shift: float32 [768], replicated, may hold values from -1.75 to 1.75
- second_gain: float32 [768], replicated, may hold values from 0.5 to 1.5
- second_shift: float32 [768], replicated, may hold values from -1.75 to 1.75
- key_cluster: int32 [2048], P('blk'), may hold values from 0 to 15, as said below
- document: int32 [2048], P('blk'), may hold values from 0 to 1
- cotangent: bfloat16 [2048, 768], P('blk'), may hold values from -6 to 6
Outputs:
- layer_out: bfloat16 [2048, 768], P('blk')
- grad_input: float32 [2048, 768], P('blk')
- grad_query_w: float32 [768, 768], P('blk', 'head')
- grad_key_w: float32 [768, 768], P('blk', 'head')
- grad_value_w: float32 [768, 768], P('blk', 'head')
- grad_output_w: float32 [768, 768], P('blk', 'head')
- grad_inner_w: float32 [768, 3072], P('blk', 'head')
- grad_outer_w: float32 [768, 3072], P('blk', 'head')
- grad_query_b: float32 [768], P('head')
- grad_value_b: float32 [768], P('head')
- grad_output_b: float32 [768], replicated
- grad_inner_b: float32 [3072], P('head')
- grad_outer_b: float32 [768], replicated
- grad_first_gain: float32 [768], replicated
- grad_first_shift: float32 [768], replicated
- grad_second_gain: float32 [768], replicated
- grad_second_shift: float32 [768], replicated
The draws below stay inside these ranges and needn't reach their ends.
Inputs may be any that keep to these rules, and one draw needn't show every extreme that they name: `key_cluster`: each cluster number is held by exactly 128 tokens; the clusters of device d are those from d * 2 on; of the 256 keys of one device at most 64 have clusters of any one device, and some device sends exactly 64 to one device.
All inputs are finite; a program needn't handle non-finite values.
Results may differ from the reference program's by a relative error of at most 0.02.
Values may be sent and summed in bfloat16 or wider, within the bound.
No kernel may reach another device: no remote copies, remote signals or barrier semaphores. Data moves between devices by JAX's collectives and lax.ppermute only.
A program may use at most 64 MiB of HBM per device.

```python
import jax
import jax.numpy as jnp
from jax import lax

D = 768
HEADS = 12
DH = 64
FF = 3072
TOK = 256
CLUSTER = 128
SOURCES = 2
TOKENS = 2048


def draw_key_cluster(key, part):
    blocks = TOKENS // TOK
    base = TOK // blocks
    per_device = TOK // CLUSTER
    key_first, key_offset, key_tokens, key_spread = jax.random.split(key, 4)
    first = jax.random.permutation(key_first, blocks).astype(jnp.int32)
    offset = jax.random.randint(key_offset, (), 1, blocks).astype(jnp.int32)
    second = (first + offset) % blocks
    targets = jnp.arange(blocks, dtype=jnp.int32)
    counts = base + base * (first[:, None] == targets[None, :]).astype(jnp.int32) - base * (second[:, None] == targets[None, :]).astype(jnp.int32)
    bounds = jnp.cumsum(counts, axis=1)
    place = jnp.arange(TOK, dtype=jnp.int32)
    sorted_dest = jnp.sum((place[None, :, None] >= bounds[:, None, :]).astype(jnp.int32), axis=2)
    shuffles = jax.vmap(lambda sub: jax.random.permutation(sub, TOK))(jax.random.split(key_tokens, blocks)).astype(jnp.int32)
    token_dest = jnp.take_along_axis(sorted_dest, shuffles, axis=1).reshape(TOKENS)
    onehot = (token_dest[:, None] == targets[None, :]).astype(jnp.int32)
    rank = jnp.sum(jnp.cumsum(onehot, axis=0) * onehot, axis=1) - 1
    spreads = jax.vmap(lambda sub: jax.random.permutation(sub, TOK))(jax.random.split(key_spread, blocks)).astype(jnp.int32)
    within = spreads[token_dest, rank]
    return (token_dest * per_device + within // CLUSTER).astype(jnp.int32)


def plant(values, own_key, least, top_value):
    index_at = [jax.random.randint(jax.random.fold_in(own_key, axis), (), 0, length) for axis, length in enumerate(values.shape)]
    main_axis = values.shape.index(max(values.shape))
    next_to = index_at[:main_axis] + [(index_at[main_axis] + 1) % values.shape[main_axis]] + index_at[main_axis + 1:]
    return values.at[tuple(index_at)].set(least).at[tuple(next_to)].set(top_value)


def raised(entries, stream_key, source, target, blocks, factor):
    owner, partner = [(jnp.arange(entries.shape[position]) // (entries.shape[position] // blocks)).reshape([-1 if axis == position else 1 for axis in range(entries.ndim)]) for position in (source, target)]
    chosen = jax.random.permutation(stream_key, blocks)[partner]
    strong = (owner == chosen) | (owner == (partner + blocks // 2) % blocks)
    return jnp.where(strong, factor * entries, entries)


def level_of(stream_key, dims, cuts, least, largest):
    def one(dim, shards_of):
        steps = jax.random.uniform(jax.random.fold_in(jax.random.fold_in(stream_key, 6), dim), (shards_of,), jnp.float32, least / len(cuts), largest / len(cuts))
        return jnp.repeat(jnp.exp(steps), dims[dim] // shards_of).reshape((-1,) + (1,) * (len(dims) - dim - 1))

    level = one(*cuts[0])
    for cut in cuts[1:]:
        level = level * one(*cut)
    return level


def centred(key, extent, scale, most, pieces=(), kind=jnp.bfloat16):
    level = level_of(key, extent, pieces, -0.22, 0.18) if pieces else 1.0
    drawn = jax.random.normal(key, extent, jnp.float32) * scale * level
    return jnp.minimum(jnp.maximum(drawn, -most), most).astype(kind)


def noise_with(key, shape, scale, most, shards, heavy, kind=jnp.bfloat16):
    values = scale * jax.random.normal(key, shape, jnp.float32)
    if shards:
        values = values * level_of(key, shape, shards, -0.22, 0.18)
    return jnp.clip(raised(values, jax.random.fold_in(key, 3), *heavy), -most, most).astype(kind)


def setup_inputs(seed: int = 0) -> dict:
    seeds = jax.random.split(jax.random.key(seed), 20)
    return {
        "hidden_in": noise_with(seeds[0], (TOKENS, D), 1.0, 6.0, ((0, 8),), (0, 1, 8, 2.0)),
        "query_w": centred(seeds[1], (D, D), D ** -0.5, 0.21875, ((0, 8), (1, 4))),
        "key_w": centred(seeds[2], (D, D), D ** -0.5, 0.21875, ((0, 8), (1, 4))),
        "value_w": centred(seeds[3], (D, D), D ** -0.5, 0.21875, ((0, 8), (1, 4))),
        "output_w": centred(seeds[4], (D, D), (D // 64) ** -0.5, 1.75, ((0, 8), (1, 4))),
        "inner_w": centred(seeds[5], (D, FF), D ** -0.5, 0.21875, ((0, 8), (1, 4))),
        "outer_w": centred(seeds[6], (D, FF), FF ** -0.5, 0.109375, ((0, 8), (1, 4))),
        "query_b": centred(seeds[7], (D,), 0.5, 3.0, ((0, 4),), jnp.float32),
        "value_b": centred(seeds[8], (D,), 0.5, 3.0, ((0, 4),), jnp.float32),
        "output_b": centred(seeds[9], (D,), 0.5, 3.0, (), jnp.float32),
        "inner_b": centred(seeds[10], (FF,), 0.5, 3.0, ((0, 4),), jnp.float32),
        "outer_b": centred(seeds[11], (D,), 0.5, 3.0, (), jnp.float32),
        "first_gain": jnp.clip(1.0 + 0.1 * jax.random.normal(seeds[12], (D,), jnp.float32), 0.5, 1.5),
        "first_shift": centred(seeds[13], (D,), 0.3, 1.75, (), jnp.float32),
        "second_gain": jnp.clip(1.0 + 0.1 * jax.random.normal(seeds[14], (D,), jnp.float32), 0.5, 1.5),
        "second_shift": centred(seeds[15], (D,), 0.3, 1.75, (), jnp.float32),
        "key_cluster": draw_key_cluster(jax.random.fold_in(seeds[19], 71), 0),
        "document": plant(jax.random.randint(seeds[17], (TOKENS,), 0, SOURCES), jax.random.fold_in(seeds[17], 1), 0, SOURCES - 1).astype(jnp.int32),
        "cotangent": centred(seeds[18], (TOKENS, D), 1.0, 6.0, ((0, 8),)),
    }


EPS = 1e-06
NEG = -1e+30
HIGH = lax.Precision.HIGHEST

@jax.custom_vjp
def low(v):
    return lax.optimization_barrier(v.astype(jnp.bfloat16)).astype(jnp.float32)

@jax.custom_vjp
def low_back(v):
    return v

def low_keep(v):
    return (low(v), None)

def low_pass(kept, grad):
    return (grad,)

def back_keep(v):
    return (v, None)

def back_low(kept, grad):
    return (low(grad),)
low.defvjp(low_keep, low_pass)
low_back.defvjp(back_keep, back_low)

def matmul(left, right):
    return jnp.dot(left, right, precision=HIGH)

def normalize(value, gain, shift):
    centered = value - lax.optimization_barrier(jnp.mean(value, axis=-1, keepdims=True))
    variance = lax.optimization_barrier(jnp.mean(centered * centered, axis=-1, keepdims=True))
    return centered * lax.rsqrt(variance + EPS) * gain + shift

def forward(hidden, query_w, key_w, value_w, output_w, inner_w, outer_w, query_b, value_b, output_b, inner_b, outer_b, first_gain, first_shift, second_gain, second_shift, key_cluster, document):
    scale = DH ** (-0.5)
    rows = hidden.shape[0]
    queries = low(low_back(matmul(hidden, query_w) + query_b))
    keys = low(low_back(matmul(hidden, key_w)))
    values = low(low_back(matmul(hidden, value_w) + value_b))
    head_keys = keys.reshape(rows, HEADS, DH).transpose(1, 0, 2)
    head_values = values.reshape(rows, HEADS, DH).transpose(1, 0, 2)
    positions = jnp.arange(rows, dtype=jnp.int32)
    width = min(512, rows)
    count = rows // width
    query_blocks = queries.reshape(count, width, HEADS, DH).transpose(0, 2, 1, 3)
    position_blocks = positions.reshape(count, width)

    def attend(pair):
        query_block, position_block = pair
        scores = low_back(jnp.einsum('hqd,hkd->hqk', query_block, head_keys, precision=HIGH) * scale)
        query_cluster = position_block // CLUSTER
        query_doc = jnp.take(document, position_block)
        allowed = (query_cluster[:, None] == key_cluster[None, :]) & (query_doc[:, None] == document[None, :]) | (position_block[:, None] == positions[None, :])
        scores = jnp.where(allowed[None], scores, NEG)
        weights = low(jax.nn.softmax(scores, axis=-1))
        return jnp.einsum('hqk,hkd->hqd', weights, head_values, precision=HIGH)
    mixed = lax.map(jax.checkpoint(attend), (query_blocks, position_blocks))
    mixed = mixed.transpose(0, 2, 1, 3).reshape(rows, D)
    attended = low(low_back(mixed))
    branch = low_back(jnp.dot(attended, output_w.T, precision=HIGH) + output_b)
    normed = normalize(hidden + branch, first_gain, first_shift)
    inner = low_back(matmul(low(normed), inner_w) + inner_b)
    active = low(low_back(jax.nn.gelu(inner, approximate=False)))
    outer = low_back(jnp.dot(active, outer_w.T, precision=HIGH) + outer_b)
    return normalize(normed + outer, second_gain, second_shift)

def reference(hidden_in, query_w, key_w, value_w, output_w, inner_w, outer_w, query_b, value_b, output_b, inner_b, outer_b, first_gain, first_shift, second_gain, second_shift, key_cluster, document, cotangent):
    floats = [item.astype(jnp.float32) for item in (hidden_in, query_w, key_w, value_w, output_w, inner_w, outer_w, query_b, value_b, output_b, inner_b, outer_b, first_gain, first_shift, second_gain, second_shift)]

    def apply(*params):
        return forward(*params, key_cluster, document)
    result, pullback = jax.vjp(apply, *floats)
    grads = pullback(cotangent.astype(jnp.float32))
    return (result.astype(jnp.bfloat16), grads[0], grads[1], grads[2], grads[3], grads[4], grads[5], grads[6], grads[7], grads[8], grads[9], grads[10], grads[11], grads[12], grads[13], grads[14], grads[15])
```

```python
import math

import jax
import jax.numpy as jnp
from jax import lax
from jax.sharding import PartitionSpec as P

DH = 64
CLUSTER = 128
EPS = 1e-06
NEG = -1e30
BF = jnp.bfloat16
F32 = jnp.float32


def swap(value, axis, bits):
    return lax.ppermute(value, axis, [(i, i ^ bits) for i in range(lax.axis_size(axis))])


def dot(left, right):
    return jnp.dot(left, right, preferred_element_type=F32)


def dot_last(left, right):
    return lax.dot_general(left, right, (((1,), (1,)), ((), ())), preferred_element_type=F32)


def dot_first(left, right):
    return lax.dot_general(left, right, (((0,), (0,)), ((), ())), preferred_element_type=F32)


def norm_forward(value, gain, shift):
    centered = value - jnp.mean(value, axis=-1, keepdims=True)
    variance = jnp.mean(centered * centered, axis=-1, keepdims=True)
    inv_std = lax.rsqrt(variance + EPS)
    normal_part = centered * inv_std
    return (normal_part * gain + shift, normal_part, inv_std)


def norm_backward(grad_out, normal_part, inv_std, gain):
    scaled = grad_out * gain
    mean_one = jnp.mean(scaled, axis=-1, keepdims=True)
    mean_two = jnp.mean(scaled * normal_part, axis=-1, keepdims=True)
    grad_in = inv_std * (scaled - mean_one - normal_part * mean_two)
    return (grad_in, jnp.sum(grad_out * normal_part, axis=0), jnp.sum(grad_out, axis=0))


def gather_rows(value):
    n = lax.axis_size("blk")
    if n != 8:
        return lax.all_gather(value, "blk", axis=0, tiled=True)
    me = lax.axis_index("blk")
    column = jnp.stack([value] + [swap(value, "blk", bits) for bits in (2, 4, 6)])
    other = swap(column, "blk", 1)
    held = jnp.stack([column, other], axis=1).reshape((8,) + value.shape)
    full = jnp.concatenate([lax.dynamic_index_in_dim(held, s ^ me, 0, False) for s in range(8)])
    return full


def scatter_sum(value):
    n = lax.axis_size("blk")
    me = lax.axis_index("blk")
    if n != 8:
        return lax.psum_scatter(value, "blk", scatter_dimension=0, tiled=True)
    rows = value.shape[0] // 8
    parts = value.reshape(4, 2, rows, value.shape[1])
    odd = me % 2
    mine = lax.dynamic_index_in_dim(parts, odd, 1, False)
    theirs = lax.dynamic_index_in_dim(parts, 1 - odd, 1, False).astype(BF)
    mine = mine + swap(theirs, "blk", 1).astype(F32)
    level = me // 2
    total = lax.dynamic_index_in_dim(mine, level, 0, False)
    for bits in (1, 2, 3):
        piece = lax.dynamic_index_in_dim(mine, level ^ bits, 0, False).astype(BF)
        total = total + swap(piece, "blk", 2 * bits).astype(F32)
    return total


def sum_blk(value):
    n = lax.axis_size("blk")
    if n != 8:
        return lax.psum(value, "blk")
    for bits in (1, 2, 4):
        value = value + swap(value, "blk", bits)
    return value


def sum_head(value):
    if lax.axis_size("head") != 4:
        return lax.psum(value.astype(BF), "head").astype(F32)
    half = value.shape[0] // 2
    core = lax.axis_index("head") % 2
    mine = lax.dynamic_slice_in_dim(value, core * half, half)
    theirs = lax.dynamic_slice_in_dim(value, (1 - core) * half, half).astype(BF)
    chip = (mine + swap(theirs, "head", 1).astype(F32)).astype(BF)
    total = (chip.astype(F32) + swap(chip, "head", 2).astype(F32)).astype(BF)
    other = swap(total, "head", 1)
    low = jnp.where(core == 0, total, other)
    high = jnp.where(core == 0, other, total)
    return jnp.concatenate([low, high]).astype(F32)


def gather_columns(value):
    if lax.axis_size("head") != 4:
        return lax.all_gather(value, "head", axis=1, tiled=True)
    me = lax.axis_index("head")
    pair = jnp.stack([value, swap(value, "head", 2)])
    other = swap(pair, "head", 1)
    held = jnp.stack([pair[0], other[0], pair[1], other[1]])
    return jnp.concatenate(
        [lax.dynamic_index_in_dim(held, s ^ me, 0, False) for s in range(4)], axis=1
    )


def split_heads(value):
    return value.reshape(value.shape[0], value.shape[1] // DH, DH).transpose(1, 0, 2)


def join_heads(value):
    return value.transpose(1, 0, 2).reshape(value.shape[1], value.shape[0] * DH)


def per_device(
    hidden_in,
    query_w,
    key_w,
    value_w,
    output_w,
    inner_w,
    outer_w,
    query_b,
    value_b,
    output_b,
    inner_b,
    outer_b,
    first_gain,
    first_shift,
    second_gain,
    second_shift,
    key_cluster,
    document,
    cotangent,
):
    rows, width = hidden_in.shape
    n = lax.axis_size("blk")
    groups = lax.axis_size("head")
    me = lax.axis_index("blk")
    my_group = lax.axis_index("head")
    local = query_w.shape[1]
    scale = 1.0 / math.sqrt(DH)
    per_block = rows // CLUSTER
    room = 2 * rows // n
    slots = n * room

    target = key_cluster // per_block
    onehot = target[:, None] == jnp.arange(n, dtype=jnp.int32)[None, :]
    index = jnp.arange(rows, dtype=jnp.int32)
    before = (index[:, None] > index[None, :]).astype(BF)
    earlier = dot(before, onehot.astype(BF))
    rank = jnp.sum(jnp.where(onehot, earlier, 0.0), axis=1).astype(jnp.int32)
    place = target * room + rank
    pick = (jnp.arange(slots, dtype=jnp.int32)[:, None] == place[None, :]).astype(BF)
    share = width // groups
    own_share = lax.dynamic_slice_in_dim(hidden_in, my_group * share, share, 1)
    code = 1 + document * per_block + key_cluster % per_block
    payload = jnp.concatenate(
        [own_share, jnp.broadcast_to(code.astype(BF)[:, None], (rows, 256 - share))], axis=1
    )
    sent = dot(pick, payload).astype(BF)
    moved = lax.all_to_all(sent.reshape(n, room, 256), "blk", 0, 0).reshape(slots, 256)
    slot_x = gather_columns(moved[:, :share])
    slot_code = moved[:, share].astype(jnp.int32)

    qkvo = gather_rows(jnp.concatenate([query_w, key_w, value_w, output_w], axis=1))
    query_full = qkvo[:, :local]
    key_full = qkvo[:, local : 2 * local]
    value_full = qkvo[:, 2 * local : 3 * local]
    output_full = qkvo[:, 3 * local :]
    inner_full = lax.all_gather(inner_w, "blk", axis=0, tiled=True)
    outer_full = lax.all_gather(outer_w, "blk", axis=0, tiled=True)

    queries = split_heads((dot(hidden_in, query_full) + query_b).astype(BF))
    both = jnp.concatenate([slot_x, hidden_in])
    keys_all = dot(both, key_full).astype(BF)
    values_all = (dot(both, value_full) + value_b).astype(BF)
    keys, own_keys = split_heads(keys_all[:slots]), split_heads(keys_all[slots:])
    values, own_values = split_heads(values_all[:slots]), split_heads(values_all[slots:])

    row_cluster = index // CLUSTER
    slot_cluster = (slot_code - 1) % per_block
    slot_doc = (slot_code - 1) // per_block
    allowed = (
        (slot_code > 0)[None, :]
        & (row_cluster[:, None] == slot_cluster[None, :])
        & (document[:, None] == slot_doc[None, :])
    )
    alone = key_cluster != me * per_block + row_cluster
    scores = jnp.where(
        allowed[None],
        jnp.einsum("hqd,hkd->hqk", queries, keys, preferred_element_type=F32) * scale,
        NEG,
    )
    q_wide, k_wide, v_wide = (
        queries.astype(F32),
        own_keys.astype(F32),
        own_values.astype(F32),
    )
    own_score = jnp.where(alone[None], jnp.sum(q_wide * k_wide, axis=-1) * scale, NEG)
    top = jnp.maximum(jnp.max(scores, axis=-1), own_score)
    weights = jnp.where(allowed[None], jnp.exp(scores - top[..., None]), 0.0)
    own_weight = jnp.where(alone[None], jnp.exp(own_score - top), 0.0)
    total = jnp.sum(weights, axis=-1) + own_weight
    probs = weights / total[..., None]
    own_prob = own_weight / total
    probs_low = probs.astype(BF)
    own_low = own_prob.astype(BF)
    mixed = (
        jnp.einsum("hqk,hkd->hqd", probs_low, values, preferred_element_type=F32)
        + own_low.astype(F32)[..., None] * v_wide
    )
    attended = join_heads(mixed).astype(BF)

    branch = sum_head(dot_last(attended, output_full)) + output_b
    hidden_f = hidden_in.astype(F32)
    normed, normal_one, inv_one = norm_forward(hidden_f + branch, first_gain, first_shift)
    normed_low = normed.astype(BF)
    inner = dot(normed_low, inner_full) + inner_b
    active, gelu_back = jax.vjp(lambda value: jax.nn.gelu(value, approximate=False), inner)
    active_low = active.astype(BF)
    outer = sum_head(dot_last(active_low, outer_full)) + outer_b
    result, normal_two, inv_two = norm_forward(normed + outer, second_gain, second_shift)
    grad_two, grad_second_gain, grad_second_shift = norm_backward(
        cotangent.astype(F32), normal_two, inv_two, second_gain
    )
    grad_outer_low = grad_two.astype(BF)
    grad_outer_b = jnp.sum(grad_outer_low.astype(F32), axis=0)
    grad_outer_w = dot_first(grad_outer_low, active_low)
    grad_active = dot(grad_outer_low, outer_full).astype(BF).astype(F32)
    grad_inner_low = gelu_back(grad_active)[0].astype(BF)
    grad_inner_b = jnp.sum(grad_inner_low.astype(F32), axis=0)
    grad_inner_w = dot_first(normed_low, grad_inner_low)
    grad_normed = grad_two + sum_head(dot_last(grad_inner_low, inner_full))
    grad_one, grad_first_gain, grad_first_shift = norm_backward(
        grad_normed, normal_one, inv_one, first_gain
    )
    grad_branch_low = grad_one.astype(BF)
    grad_output_b = jnp.sum(grad_branch_low.astype(F32), axis=0)
    grad_output_w = dot_first(grad_branch_low, attended)
    grad_heads = split_heads(dot(grad_branch_low, output_full).astype(BF))
    grad_wide = grad_heads.astype(F32)
    delta = jnp.sum(grad_wide * mixed, axis=-1)

    grad_values = jnp.einsum(
        "hqk,hqd->hkd", probs_low, grad_heads, preferred_element_type=F32
    )
    grad_probs = jnp.einsum("hqd,hkd->hqk", grad_heads, values, preferred_element_type=F32)
    grad_scores = (probs * (grad_probs - delta[..., None])).astype(BF)
    own_grad_values = own_low.astype(F32)[..., None] * grad_wide
    own_grad_probs = jnp.sum(grad_wide * v_wide, axis=-1)
    own_grad_scores = (own_prob * (own_grad_probs - delta)).astype(BF).astype(F32)[..., None]
    grad_queries = (
        jnp.einsum("hqk,hkd->hqd", grad_scores, keys, preferred_element_type=F32)
        + own_grad_scores * k_wide
    ) * scale
    grad_keys = (
        jnp.einsum("hqk,hqd->hkd", grad_scores, queries, preferred_element_type=F32) * scale
    )
    own_grad_keys = own_grad_scores * q_wide * scale

    slot_grads = jnp.concatenate(
        [join_heads(grad_keys).astype(BF), join_heads(grad_values).astype(BF)], axis=1
    )
    returned = lax.all_to_all(slot_grads.reshape(n, room, 2 * local), "blk", 0, 0).reshape(
        slots, 2 * local
    )
    own_grads = jnp.concatenate([join_heads(own_grad_keys), join_heads(own_grad_values)], axis=1)
    token_grads = (own_grads + dot_first(pick, returned)).astype(BF)
    own_grads_low = own_grads.astype(BF)
    grad_query_low = join_heads(grad_queries).astype(BF)
    grad_rows = dot_last(
        jnp.concatenate([grad_query_low, token_grads], axis=1), qkvo[:, : 3 * local]
    )
    grad_input = grad_one + sum_head(grad_rows)

    grad_query_w = dot_first(hidden_in, grad_query_low)
    grad_kv_w = dot_first(both, jnp.concatenate([slot_grads, own_grads_low]))
    grad_query_b = jnp.sum(grad_query_low.astype(F32), axis=0)
    grad_value_b = jnp.sum(slot_grads[:, local:].astype(F32), axis=0) + jnp.sum(
        own_grads_low[:, local:].astype(F32), axis=0
    )
    summed_outer = scatter_sum(grad_outer_w)
    summed_inner = scatter_sum(grad_inner_w)
    summed = scatter_sum(jnp.concatenate([grad_query_w, grad_kv_w, grad_output_w], axis=1))
    small = (
        grad_query_b,
        grad_value_b,
        grad_output_b,
        grad_inner_b,
        grad_outer_b,
        grad_first_gain,
        grad_first_shift,
        grad_second_gain,
        grad_second_shift,
    )
    vector = sum_blk(jnp.concatenate(small).reshape(-1, 128))
    vector = vector.reshape(-1)
    bounds = [0]
    for item in small:
        bounds.append(bounds[-1] + item.shape[0])
    small = tuple(vector[a:b] for a, b in zip(bounds[:-1], bounds[1:]))
    return (
        result.astype(BF),
        grad_input,
        summed[:, :local],
        summed[:, local : 2 * local],
        summed[:, 2 * local : 3 * local],
        summed[:, 3 * local :],
        summed_inner,
        summed_outer,
    ) + small


def solution(mesh):
    matrix = P("blk", "head")
    in_specs = (
        (P("blk", None),)
        + (matrix,) * 6
        + (P("head"), P("head"), P(), P("head"))
        + (P(),) * 5
        + (P("blk"), P("blk"), P("blk", None))
    )
    out_specs = (
        (P("blk", None), P("blk", None))
        + (matrix,) * 6
        + (P("head"), P("head"), P(), P("head"))
        + (P(),) * 5
    )
    return jax.shard_map(
        per_device, mesh=mesh, in_specs=in_specs, out_specs=out_specs, check_vma=False
    )
```

```python
import functools
import math

import jax
import jax.numpy as jnp
from jax import lax
from jax.experimental import pallas as pl
from jax.experimental.pallas import tpu as pltpu
from jax.sharding import PartitionSpec as P

DH = 64
CLUSTER = 128
EPS = 1e-06
NEG = -1e30
SCALE = 1.0 / math.sqrt(DH)
META = 128
EXTRA = 16
VMEM = 16 << 20
BF = jnp.bfloat16
F32 = jnp.float32


def swap(value, axis, bits, name):
    with jax.named_scope(name):
        return lax.ppermute(value, axis, [(i, i ^ bits) for i in range(lax.axis_size(axis))])


def dot(left, right):
    return jnp.dot(left, right, preferred_element_type=F32)


def dot_last(left, right):
    return lax.dot_general(left, right, (((1,), (1,)), ((), ())), preferred_element_type=F32)


def dot_first(left, right):
    return lax.dot_general(left, right, (((0,), (0,)), ((), ())), preferred_element_type=F32)


def kernel_call(name, body, outs, args, scratch=(), flops=0, space=pltpu.VMEM):
    size = sum(math.prod(a.shape) * a.dtype.itemsize for a in list(args) + list(outs))
    whole = pl.BlockSpec(memory_space=pltpu.VMEM)
    return pl.pallas_call(
        body,
        out_shape=tuple(outs),
        in_specs=[pl.BlockSpec(memory_space=space)] * len(args),
        out_specs=tuple([whole] * len(outs)),
        scratch_shapes=list(scratch),
        name=name,
        compiler_params=pltpu.CompilerParams(vmem_limit_bytes=VMEM),
        cost_estimate=pl.CostEstimate(flops=flops, bytes_accessed=size, transcendentals=0),
    )(*args)


def like(shape, dtype=BF):
    return jax.ShapeDtypeStruct(shape, dtype)


def norm_forward(value, gain, shift):
    centered = value - jnp.mean(value, axis=-1, keepdims=True)
    variance = jnp.mean(centered * centered, axis=-1, keepdims=True)
    inv_std = lax.rsqrt(variance + EPS)
    normal_part = centered * inv_std
    return (normal_part * gain + shift, normal_part, inv_std)


def norm_backward(grad_out, normal_part, inv_std, gain):
    scaled = grad_out * gain
    mean_one = jnp.mean(scaled, axis=-1, keepdims=True)
    mean_two = jnp.mean(scaled * normal_part, axis=-1, keepdims=True)
    grad_in = inv_std * (scaled - mean_one - normal_part * mean_two)
    return (
        grad_in,
        jnp.sum(grad_out * normal_part, axis=0, keepdims=True),
        jnp.sum(grad_out, axis=0, keepdims=True),
    )


def extra_rows(*rows):
    width = rows[0].shape[1]
    return jnp.concatenate(list(rows) + [jnp.zeros((EXTRA - len(rows), width), F32)]).astype(BF)


def whole_matrix(pieces, scratch, column_at=0, facing_at=0):
    if len(pieces) == 1:
        return pieces[0][...]
    me = lax.axis_index("blk")
    own, column, facing, other = pieces[0], pieces[1:4], pieces[4], pieces[5]
    width = own.shape[1]
    scratch[me] = own[...]
    scratch[me ^ 1] = facing[:, facing_at : facing_at + width]
    for k in range(3):
        scratch[me ^ (2 * (k + 1))] = column[k][: own.shape[0], column_at : column_at + width]
        scratch[me ^ (2 * (k + 1) + 1)] = other[k, :, column_at : column_at + width]
    return scratch[...].reshape(-1, width)


def order(value, *after):
    return lax.optimization_barrier((value,) + after)[0]


def piece_scratch(pieces):
    if len(pieces) == 1:
        return pltpu.VMEM((8, 128), BF)
    return pltpu.VMEM((8,) + pieces[0].shape, BF)


def places(tag_row, n, per_block, rows):
    target = tag_row // per_block
    onehot = lax.broadcasted_iota(jnp.int32, (n, rows), 0) == target
    earlier = lax.broadcasted_iota(jnp.int32, (rows, rows), 0) < lax.broadcasted_iota(
        jnp.int32, (rows, rows), 1
    )
    count = dot(onehot.astype(F32).astype(BF), earlier.astype(F32).astype(BF))
    rank = jnp.sum(jnp.where(onehot, count, 0.0), axis=0, keepdims=True).astype(jnp.int32)
    return target, rank


def pack_kernel(n, room, per_block, groups, *refs):
    count = 9
    sources, rest = refs[:count], refs[count:]
    sends, (attend_ref, all_ref), rest = rest[:-12], rest[-12:-10], rest[-10:]
    held, sems = rest[:count], rest[count]
    copies = [
        pltpu.make_async_copy(source, to, sems.at[k])
        for k, (source, to) in enumerate(zip(sources, held))
    ]
    for copy in copies:
        copy.start()
    for copy in copies:
        copy.wait()
    x_ref, tag_ref, doc_ref, shards = held[0], held[1], held[2], held[3:]
    at = 0
    for k, shard in enumerate(shards):
        if k < 4:
            attend_ref[:, at : at + shard.shape[1]] = shard[...]
        all_ref[:, at : at + shard.shape[1]] = shard[...]
        at += shard.shape[1]
    rows, width = x_ref.shape
    share = room // groups
    target, rank = places(tag_ref[...], n, per_block, rows)
    offset = rank - lax.axis_index("head") * share
    inside = (offset >= 0) & (offset < share)
    code = (1 + doc_ref[...] * per_block + tag_ref[...] % per_block).astype(F32)
    if len(sends) == 1:
        (out_ref,) = sends
        place = jnp.where(inside, target * share + offset, -1)
        pick = lax.broadcasted_iota(jnp.int32, (n * share, rows), 0) == place
        out_ref[:, :width] = dot(pick.astype(F32).astype(BF), x_ref[...]).astype(BF)
        code = jnp.sum(jnp.where(pick, code, 0.0), axis=1, keepdims=True)
        out_ref[:, width:] = jnp.broadcast_to(code, (n * share, META)).astype(BF)
        return
    odd = lax.axis_index("blk") % 2
    for t, out_ref in enumerate(sends):
        there = inside & (target % 2 == odd ^ t)
        place = jnp.where(there, target // 2 * share + offset, -1)
        pick = lax.broadcasted_iota(jnp.int32, (4 * share, rows), 0) == place
        out_ref[: 4 * share, :] = dot(pick.astype(F32).astype(BF), x_ref[...]).astype(BF)
        level = lax.broadcasted_iota(jnp.int32, (EXTRA, rows), 0)
        codes = jnp.where(there & (target // 2 == level), code, 0.0).astype(BF)
        spot = lax.broadcasted_iota(jnp.int32, (META, rows), 0) == offset
        tile = dot_last(codes, spot.astype(F32).astype(BF)).astype(BF)
        out_ref[4 * share :, :META] = tile
        out_ref[4 * share :, META:] = jnp.zeros((EXTRA, width - META), BF)


def route_kernel(keep_ref, recv_ref, weight_ref, *outs):
    level = lax.axis_index("blk") // 2
    rows, share = weight_ref.shape[0], (keep_ref.shape[0] - EXTRA) // 4
    width = keep_ref.shape[1]
    lanes = lax.broadcasted_iota(jnp.int32, (EXTRA, META), 0)
    for k in range(4):
        z = level ^ k
        outs[k][:rows, :] = weight_ref[...]
        for t, ref in enumerate((keep_ref, recv_ref)):
            outs[k][rows + t * share : rows + (t + 1) * share, :] = ref[pl.ds(z * share, share), :]
        first = keep_ref[4 * share :, :META].astype(F32)
        second = recv_ref[4 * share :, :META].astype(F32)
        first = jnp.sum(jnp.where(lanes == z, first, 0.0), axis=0, keepdims=True)
        second = jnp.sum(jnp.where(lanes == z, second, 0.0), axis=0, keepdims=True)
        tile = jnp.where(lanes == 0, first, jnp.where(lanes == 1, second, 0.0))
        outs[k][rows + 2 * share :, :META] = tile.astype(BF)
        outs[k][rows + 2 * share :, META:] = jnp.zeros((EXTRA, width - META), BF)


def stack_kernel(a_ref, b_ref, c_ref, out_ref):
    for k, ref in enumerate((a_ref, b_ref, c_ref)):
        out_ref[k] = ref[...]


def slots_kernel(rows, m0, m1, m2, m3, out_ref, stack_ref):
    for k, ref in enumerate((m1, m2, m3)):
        stack_ref[k] = ref[:rows, :]
    share = (m0.shape[0] - rows - EXTRA) // 2
    width = m0.shape[1]
    level = lax.broadcasted_iota(jnp.int32, (EXTRA, META), 0)
    tile = jnp.zeros((EXTRA, META), F32)
    for k, ref in enumerate((m0, m1, m2, m3)):
        out_ref[2 * k * share : 2 * (k + 1) * share, :] = ref[rows : rows + 2 * share, :]
        codes = ref[rows + 2 * share :, :META].astype(F32)
        for t in range(2):
            tile = tile + jnp.where(level == 2 * k + t, codes[t : t + 1, :], 0.0)
    out_ref[8 * share :, :META] = tile.astype(BF)
    out_ref[8 * share :, META:] = jnp.zeros((EXTRA, width - META), BF)


def slot_codes(part, slots, width):
    if part.shape[1] > width:
        return part[:, width : width + 1].astype(F32)
    tile = part[slots:, :META]
    share = slots // 8
    row = lax.broadcasted_iota(jnp.int32, (slots, EXTRA), 0) // share
    spread = row == lax.broadcasted_iota(jnp.int32, (slots, EXTRA), 1)
    wide = dot(spread.astype(F32).astype(BF), tile)
    lane = lax.broadcasted_iota(jnp.int32, (slots, META), 1)
    here = lane == lax.broadcasted_iota(jnp.int32, (slots, META), 0) % share
    return jnp.sum(jnp.where(here, wide, 0.0), axis=1, keepdims=True)


def attend_kernel(per_block, count, *refs):
    x_ref, tag_ref, doc_ref, bias_ref = refs[:4]
    parts = refs[4:8]
    pieces = refs[8 : 8 + count]
    mine_ref, theirs_ref, a_ref, q_ref, kv_ref, mask_ref, stat_ref, scratch, y_ref = refs[
        8 + count :
    ]
    rows, width = x_ref.shape
    local = a_ref.shape[1]
    slots = kv_ref.shape[0] - rows
    step = slots // 4
    me = lax.axis_index("blk")
    core = lax.axis_index("head") % 2
    weight = whole_matrix(pieces, scratch)
    own = dot(x_ref[...], weight[:, : 3 * local]) + bias_ref[:1, : 3 * local]
    q_ref[...] = own[:, 2 * local :].astype(BF)
    kv_ref[slots:, :] = own[:, : 2 * local].astype(BF)
    row_cluster = lax.broadcasted_iota(jnp.int32, (1, rows), 1) // CLUSTER
    wanted = (1 + doc_ref[...] * per_block + row_cluster).astype(F32)
    for k in range(4):
        part = parts[k]
        kv_ref[k * step : (k + 1) * step, :] = (
            dot(part[:step, :width], weight[:, : 2 * local]) + bias_ref[:1, : 2 * local]
        ).astype(BF)
        code = slot_codes(part, step, width)
        mask_ref[k * step : (k + 1) * step, :] = jnp.where(code == wanted, 0.0, NEG).astype(BF)
    alone = tag_ref[...] != me * per_block + row_cluster
    diagonal = lax.broadcasted_iota(jnp.int32, (rows, rows), 0) == lax.broadcasted_iota(
        jnp.int32, (rows, rows), 1
    )
    mask_ref[slots:, :] = jnp.where(diagonal & alone, 0.0, NEG).astype(BF)
    mask = mask_ref[...].astype(F32)
    stats = []
    for j in range(local // DH):
        cut = slice(j * DH, (j + 1) * DH)
        scores = dot_last(kv_ref[:, cut], q_ref[:, cut]) * SCALE + mask
        top = jnp.max(scores, axis=0, keepdims=True)
        weights = jnp.exp(scores - top)
        inverse = 1.0 / jnp.sum(weights, axis=0, keepdims=True)
        probs = (weights * inverse).astype(BF)
        value = kv_ref[:, local + j * DH : local + (j + 1) * DH]
        a_ref[:, cut] = dot_first(probs, value).astype(BF)
        stats += [top, inverse]
    stat_ref[...] = jnp.concatenate(stats + [jnp.zeros((8 - len(stats), rows), F32)])
    y_ref[...] = dot_last(a_ref[...], weight[:, 3 * local :])
    half = rows // 2
    mine_ref[...] = y_ref[pl.ds(core * half, half), :]
    theirs_ref[...] = y_ref[pl.ds((1 - core) * half, half), :].astype(BF)


def attend_back_kernel(n, count, *refs):
    own_ref, other_ref, q_ref, kv_ref, mask_ref, stat_ref = refs[:6]
    pieces = refs[6 : 6 + count]
    eb_ref, dq_ref, dkv_ref = refs[6 + count : 9 + count]
    back, scratch = refs[9 + count : -1], refs[-1]
    rows, local = q_ref.shape
    slots = kv_ref.shape[0] - rows
    half = rows // 2
    core = lax.axis_index("head") % 2
    weight = whole_matrix(pieces, scratch)
    eb_ref[pl.ds(core * half, half), :] = own_ref[:half, :]
    eb_ref[pl.ds((1 - core) * half, half), :] = other_ref[:half, :]
    da = dot(eb_ref[...], weight[:, 3 * local :]).astype(BF)
    mask = mask_ref[...].astype(F32)
    for j in range(local // DH):
        cut = slice(j * DH, (j + 1) * DH)
        key, query = kv_ref[:, cut], q_ref[:, cut]
        value = kv_ref[:, local + j * DH : local + (j + 1) * DH]
        scores = dot_last(key, query) * SCALE + mask
        probs = jnp.exp(scores - stat_ref[2 * j : 2 * j + 1, :]) * stat_ref[
            2 * j + 1 : 2 * j + 2, :
        ]
        low = probs.astype(BF)
        dkv_ref[:, local + j * DH : local + (j + 1) * DH] = dot(low, da[:, cut]).astype(BF)
        grad = dot_last(value, da[:, cut])
        delta = jnp.sum(low.astype(F32) * grad, axis=0, keepdims=True)
        grad = (probs * (grad - delta)).astype(BF)
        dkv_ref[:, cut] = (dot(grad, query) * SCALE).astype(BF)
        dq_ref[:, cut] = (dot_first(grad, key) * SCALE).astype(BF)
    if back:
        level = lax.axis_index("blk") // 2
        share = slots // 4 // n
        for t in range(2):
            for z in range(4):
                for k in range(4):
                    at = k * slots // 4 + (2 * (z ^ level) + t) * share
                    to = (z * 4 + k) * share
                    back[t][to : to + share, :] = dkv_ref[pl.ds(at, share), :]


def back_middle_kernel(keep_ref, recv_ref, *outs):
    level = lax.axis_index("blk") // 2
    room = outs[0].shape[0] // 2
    for k in range(4):
        at = pl.ds((level ^ k) * room, room)
        outs[k][:room, :] = keep_ref[at, :]
        outs[k][room:, :] = recv_ref[at, :]


def token_kernel(n, room, per_block, parts, count, *refs):
    tag_ref, dkv_ref, dq_ref = refs[:3]
    back = refs[3 : 3 + parts]
    pieces = refs[3 + parts : 3 + parts + count]
    mine_ref, theirs_ref, scratch, z_ref = refs[3 + parts + count :]
    rows, local = dq_ref.shape
    slots = n * room
    half = rows // 2
    share = room // 4
    group = lax.axis_index("head")
    core = group % 2
    weight = whole_matrix(pieces, scratch)
    target, rank = places(tag_ref[...], n, per_block, rows)
    if parts > 1:
        target = target ^ lax.axis_index("blk")
    place = target * room + ((rank // share) ^ group) * share + rank % share
    total = dkv_ref[slots:, :].astype(F32)
    step = slots // parts
    for k in range(parts):
        pick = lax.broadcasted_iota(jnp.int32, (step, rows), 0) + k * step == place
        total = total + dot_first(pick.astype(F32).astype(BF), back[k][...])
    z_ref[...] = dot_last(total.astype(BF), weight[:, : 2 * local]) + dot_last(
        dq_ref[...], weight[:, 2 * local : 3 * local]
    )
    mine_ref[...] = z_ref[pl.ds(core * half, half), :]
    theirs_ref[...] = z_ref[pl.ds((1 - core) * half, half), :].astype(BF)


def norm_one_kernel(
    chip_ref, recv_ref, x_ref, vec_ref, h_ref, n_ref, r_ref, hb_ref
):
    half = chip_ref.shape[0]
    core = lax.axis_index("head") % 2
    branch = chip_ref[...].astype(F32) + recv_ref[...].astype(F32) + vec_ref[1:2, :]
    value = x_ref[pl.ds(core * half, half), :].astype(F32) + branch
    h, normal, inverse = norm_forward(value, vec_ref[2:3, :], vec_ref[3:4, :])
    h_ref[...] = h
    n_ref[...] = normal
    r_ref[...] = inverse
    hb_ref[...] = h.astype(BF)


def norm_two_kernel(
    chip_ref, recv_ref, h_ref, vec_ref, c_ref, out_ref, e_ref, eb_ref
):
    half = chip_ref.shape[0]
    core = lax.axis_index("head") % 2
    outer = chip_ref[...].astype(F32) + recv_ref[...].astype(F32) + vec_ref[4:5, :]
    gain_row = vec_ref[5:6, :]
    result, normal, inverse = norm_forward(h_ref[...] + outer, gain_row, vec_ref[6:7, :])
    out_ref[...] = result.astype(BF)
    cotangent = c_ref[pl.ds(core * half, half), :].astype(F32)
    grad, gain, shift = norm_backward(cotangent, normal, inverse, gain_row)
    e_ref[...] = grad
    eb_ref[:half, :] = grad.astype(BF)
    eb_ref[half:, :] = extra_rows(gain, shift)


def norm_back_kernel(chip_ref, recv_ref, e_ref, n_ref, r_ref, vec_ref, out_ref, eb_ref):
    half = chip_ref.shape[0]
    grad = e_ref[...] + (chip_ref[...].astype(F32) + recv_ref[...].astype(F32))
    grad, gain, shift = norm_backward(grad, n_ref[...], r_ref[...], vec_ref[2:3, :])
    out_ref[...] = grad
    eb_ref[:half, :] = grad.astype(BF)
    eb_ref[half:, :] = extra_rows(gain, shift)


def inner_kernel(count, at, *refs):
    own_ref, other_ref, bias_ref = refs[:3]
    pieces = refs[3 : 3 + count]
    g_ref, slope_ref, scratch = refs[3 + count :]
    half = own_ref.shape[0]
    weight = whole_matrix(pieces, scratch, *at)
    for k, part in enumerate((own_ref, other_ref)):
        u = dot(part[...], weight) + bias_ref[7:8, :]
        below = 0.5 * (1.0 + lax.erf(u * math.sqrt(0.5)))
        g_ref[k * half : (k + 1) * half, :] = (u * below).astype(BF)
        density = jnp.exp(-0.5 * u * u) * (1.0 / math.sqrt(2.0 * math.pi))
        slope_ref[k * half : (k + 1) * half, :] = below + u * density


def outer_kernel(count, at, *refs):
    g_ref = refs[0]
    pieces = refs[1 : 1 + count]
    mine_ref, theirs_ref, scratch = refs[1 + count :]
    half = mine_ref.shape[0]
    weight = whole_matrix(pieces, scratch, *at)
    mine_ref[...] = dot_last(g_ref[:half, :], weight)
    theirs_ref[...] = dot_last(g_ref[half:, :], weight).astype(BF)


def ff_back_kernel(count, outer_at, inner_at, *refs):
    own_ref, other_ref, slope_ref = refs[:3]
    outer, inner = refs[3 : 3 + count], refs[3 + count : 3 + 2 * count]
    mine_ref, theirs_ref, du_ref, scratch, scratch_two = refs[3 + 2 * count :]
    half = mine_ref.shape[0]
    outer = whole_matrix(outer, scratch, *outer_at)
    inner = whole_matrix(inner, scratch_two, *inner_at)
    for k, part in ((1, other_ref), (0, own_ref)):
        rows = slice(k * half, (k + 1) * half)
        dg = dot(part[:half, :], outer).astype(BF).astype(F32)
        du_ref[rows, :] = (dg * slope_ref[rows, :]).astype(BF)
        dh = dot_last(du_ref[rows, :], inner)
        if k:
            theirs_ref[...] = dh.astype(BF)
        else:
            mine_ref[...] = dh


def split_pieces(total, mine_ref, theirs_ref):
    me = lax.axis_index("blk")
    odd = me % 2
    rows = total.shape[0] // 8
    for z in range(4):
        at = slice(z * rows, (z + 1) * rows)
        mine_ref[at, :] = total[pl.ds((2 * z + odd) * rows, rows), :].astype(BF)
        theirs_ref[at, :] = total[pl.ds((2 * z + 1 - odd) * rows, rows), :].astype(BF)


def ff_weights_kernel(small, own_ref, other_ref, left_ref, *refs):
    half = left_ref.shape[0] // 2
    refs = list(refs)
    total = refs.pop()
    total[...] = dot_first(own_ref[:half, :], left_ref[:half, :]) + dot_first(
        other_ref[:half, :], left_ref[half:, :]
    )
    if small == "outer":
        small_ref = refs.pop()
        norms = own_ref[half:, :].astype(F32) + other_ref[half:, :].astype(F32)
        bias = jnp.sum(own_ref[:half, :].astype(F32), axis=0, keepdims=True) + jnp.sum(
            other_ref[:half, :].astype(F32), axis=0, keepdims=True
        )
        small_ref[...] = jnp.concatenate([norms[:2], bias, jnp.zeros((5, bias.shape[1]), F32)])
    else:
        small_ref = refs.pop()
        bias = jnp.sum(left_ref[...].astype(F32), axis=0, keepdims=True)
        small_ref[...] = jnp.concatenate([bias, jnp.zeros((7, bias.shape[1]), F32)])
    if len(refs) == 1:
        refs[0][...] = total[...]
    else:
        split_pieces(total, *refs)


def attend_weights_kernel(*refs):
    x_ref, p0, p1, p2, p3, dkv_ref, dq_ref, eb_ref, a_ref, own_ref, other_ref = refs[:11]
    outer_ref, inner_ref = refs[11:13]
    outs, total = list(refs[13:-1]), refs[-1]
    rows, width = x_ref.shape
    local = dq_ref.shape[1]
    slots = dkv_ref.shape[0] - rows
    step = slots // 4
    sums = dot_first(x_ref[...], dkv_ref[slots:, :])
    for k, part in enumerate((p0, p1, p2, p3)):
        sums = sums + dot_first(part[:step, :width], dkv_ref[k * step : (k + 1) * step, :])
    total[:, : 2 * local] = sums
    total[:, 2 * local : 3 * local] = dot_first(x_ref[...], dq_ref[...])
    total[:, 3 * local :] = dot_first(eb_ref[...], a_ref[...])
    half = rows // 2
    norms = own_ref[half:, :].astype(F32) + other_ref[half:, :].astype(F32)
    output_b = jnp.sum(eb_ref[...].astype(F32), axis=0, keepdims=True)
    query_b = jnp.sum(dq_ref[...].astype(F32), axis=0, keepdims=True)
    value_b = jnp.sum(dkv_ref[...].astype(F32), axis=0, keepdims=True)
    last = jnp.concatenate([value_b, query_b, jnp.zeros((1, width - 3 * local), F32)], axis=1)
    small = jnp.concatenate(
        [
            outer_ref[:3, :],
            inner_ref[:1, :],
            norms[:2],
            output_b,
            last,
            jnp.zeros((EXTRA - 8, width), F32),
        ]
    )
    if outs[0].shape == total.shape:
        outs[0][...] = total[...]
        outs[1][...] = small
    else:
        split_pieces(total, *outs)
        body = outs[0].shape[0] - EXTRA
        outs[0][body:, :] = small.astype(BF)
        outs[1][body:, :] = small.astype(BF)


def middle_kernel(extra, mine_ref, recv_ref, *outs):
    level = lax.axis_index("blk") // 2
    rows = outs[0].shape[0] - extra
    for k in range(4):
        at = pl.ds((level ^ k) * rows, rows)
        outs[k][:rows, :] = (mine_ref[at, :].astype(F32) + recv_ref[at, :].astype(F32)).astype(BF)
    if extra:
        small = mine_ref[4 * rows :, :].astype(F32) + recv_ref[4 * rows :, :].astype(F32)
        for k in range(4):
            outs[k][rows:, :] = small.astype(BF)


def last_kernel(t0, t1, t2, t3, *outs):
    total = (t0[...].astype(F32) + t1[...].astype(F32)) + (
        t2[...].astype(F32) + t3[...].astype(F32)
    )
    if len(outs) == 1:
        outs[0][...] = total
        return
    rows, local = outs[0].shape
    for k in range(4):
        outs[k][...] = total[:rows, k * local : (k + 1) * local]
    outs[4][...] = total[rows:, :]


def scatter_middle(mine, theirs, name, extra=0, after=None):
    recv = swap(theirs, "blk", 1, name + "_y")
    if after is not None:
        recv = order(recv, after)
    rows = (mine.shape[0] - extra) // 4 + extra
    return kernel_call(
        name + "_middle",
        functools.partial(middle_kernel, extra),
        [like((rows, mine.shape[1]))] * 4,
        [mine, recv],
    )


def scatter_last(parts, outs, name):
    moved = [parts[0]] + [swap(parts[k], "blk", 2 * k, f"{name}_z{2 * k}") for k in (1, 2, 3)]
    return kernel_call(name + "_last", last_kernel, outs, moved)


def chip_sum(mine, theirs, name):
    chip = (mine + swap(theirs, "head", 1, name + "_chip").astype(F32)).astype(BF)
    return chip, swap(chip, "head", 2, name + "_x")


def per_device(
    hidden_in,
    query_w,
    key_w,
    value_w,
    output_w,
    inner_w,
    outer_w,
    query_b,
    value_b,
    output_b,
    inner_b,
    outer_b,
    first_gain,
    first_shift,
    second_gain,
    second_shift,
    key_cluster,
    document,
    cotangent,
):
    rows, width = hidden_in.shape
    n = lax.axis_size("blk")
    groups = lax.axis_size("head")
    assert groups == 4
    local = query_w.shape[1]
    units = inner_w.shape[1]
    per_block = rows // CLUSTER
    room = 2 * rows // n
    slots = n * room
    half = rows // 2
    share = room // groups
    staged = n == 8
    core = lax.axis_index("head") % 2

    tag_row, doc_row = key_cluster.reshape(1, rows), document.reshape(1, rows)

    pack_args = [hidden_in, tag_row, doc_row, key_w, value_w, query_w, output_w, inner_w, outer_w]
    pack_args = [pltpu.with_memory_space_constraint(item, pltpu.HBM) for item in pack_args]
    if staged:
        sends = [like((4 * share + EXTRA, width))] * 2
    else:
        sends = [like((n * share, width + META))]
    *sent, attend_w, all_w = kernel_call(
        "pack",
        functools.partial(pack_kernel, n, room, per_block, groups),
        sends + [like((width // n, 4 * local)), like((width // n, 4 * local + 2 * units))],
        pack_args,
        [pltpu.VMEM(item.shape, item.dtype) for item in pack_args]
        + [pltpu.SemaphoreType.DMA((len(pack_args),))],
        flops=2 * n * share * rows * width,
        space=pltpu.HBM,
    )
    if staged:
        column = lambda value, name: [
            swap(value[k], "blk", 2 * k, f"{name}_z{2 * k}") for k in (1, 2, 3)
        ]
        slots_y = swap(sent[1], "blk", 1, "slots_y")
        messages = kernel_call(
            "route",
            route_kernel,
            [like((width // n + 2 * share + EXTRA, width))] * 4,
            [sent[0], slots_y, attend_w],
        )
        arrived = [messages[0]] + column(messages, "attend_w")
        facing = swap(order(all_w, messages[0]), "blk", 1, "facing_w")
        later_w = order(all_w, facing)[:, 4 * local :]
        ff_column = column([later_w] * 4, "ff_w")
        moved, rest = kernel_call(
            "slots",
            functools.partial(slots_kernel, width // n),
            [like((n * share + EXTRA, width)), like((3, width // n, 4 * local))],
            arrived,
        )
        rest = swap(rest, "blk", 1, "attend_w_rest")
        attend_p = [attend_w] + arrived[1:] + [facing, rest]
        (rest,) = kernel_call(
            "stack", stack_kernel, [like((3, width // n, 2 * units))], ff_column
        )
        rest = swap(rest, "blk", 1, "ff_w_rest")
        inner_p = [inner_w] + ff_column + [facing, rest]
        outer_p = [outer_w] + ff_column + [facing, rest]
    else:
        moved = lax.all_to_all(sent[0].reshape(n, share, width + META), "blk", 0, 0)
        moved = moved.reshape(sent[0].shape)
        gather = lambda value: [lax.all_gather(value, "blk", axis=0, tiled=True)]
        attend_p, inner_p, outer_p = gather(attend_w), gather(inner_w), gather(outer_w)
    far = swap(moved, "head", 2, "slots_x")
    parts = [moved, swap(moved, "head", 1, "slots_chip"), far, swap(far, "head", 1, "slots_far")]
    inner_at = (0, 4 * local)
    outer_at = (units, 4 * local + units)

    count = len(attend_p)
    blank = jnp.zeros((local,), F32)
    vectors = [
        jnp.concatenate([blank, value_b, query_b, blank]),
        output_b,
        first_gain,
        first_shift,
        outer_b,
        second_gain,
        second_shift,
        inner_b,
    ]
    vectors = jnp.stack(order(vectors, attend_w))
    mine, theirs, a, q, kv, mask, stat = kernel_call(
        "attend",
        functools.partial(attend_kernel, per_block, count),
        [
            like((half, width), F32),
            like((half, width)),
            like((rows, local)),
            like((rows, local)),
            like((slots + rows, 2 * local)),
            like((slots + rows, rows)),
            like((8, rows), F32),
        ],
        [hidden_in, tag_row, doc_row, vectors] + parts + attend_p,
        [piece_scratch(attend_p), pltpu.VMEM((rows, width), F32)],
        flops=2 * rows * width * local * 9,
    )
    chip, recv = chip_sum(mine, theirs, "branch")
    if staged:
        recv = order(recv, *ff_column)
    h, normal_one, inv_one, hb = kernel_call(
        "norm_one",
        norm_one_kernel,
        [
            like((half, width), F32),
            like((half, width), F32),
            like((half, 1), F32),
            like((half, width)),
        ],
        [chip, recv, hidden_in, vectors],
    )
    hb_other = swap(hb, "head", 1, "hb")

    g, slope = kernel_call(
        "inner",
        functools.partial(inner_kernel, count, inner_at),
        [like((rows, units)), like((rows, units), F32)],
        [hb, hb_other, vectors] + inner_p,
        [piece_scratch(inner_p)],
        flops=2 * rows * width * units,
    )
    mine, theirs = kernel_call(
        "outer",
        functools.partial(outer_kernel, count, outer_at),
        [like((half, width), F32), like((half, width))],
        [g] + outer_p,
        [piece_scratch(outer_p)],
        flops=2 * rows * width * units,
    )
    chip, recv = chip_sum(mine, theirs, "ff")
    result, e_two, eb_two = kernel_call(
        "norm_two",
        norm_two_kernel,
        [like((half, width)), like((half, width), F32), like((half + EXTRA, width))],
        [chip, recv, h, vectors, cotangent],
    )
    eb_two_other = swap(eb_two, "head", 1, "eb_two")
    mine, theirs, du = kernel_call(
        "ff_back",
        functools.partial(ff_back_kernel, count, outer_at, inner_at),
        [like((half, width), F32), like((half, width)), like((rows, units))],
        [eb_two, eb_two_other, slope] + outer_p + inner_p,
        [piece_scratch(outer_p), piece_scratch(inner_p)],
        flops=4 * rows * width * units,
    )
    chip, recv = chip_sum(mine, theirs, "ff_back")

    if staged:
        grad_outs = [like((width // 2, units)), like((width // 2, units))]
    else:
        grad_outs = [like((width, units), F32)]
    outer_g = kernel_call(
        "outer_grad",
        functools.partial(ff_weights_kernel, "outer"),
        grad_outs + [like((8, width), F32)],
        [eb_two, eb_two_other, g],
        [pltpu.VMEM((width, units), F32)],
        flops=2 * rows * width * units,
    )
    inner_g = kernel_call(
        "inner_grad",
        functools.partial(ff_weights_kernel, "inner"),
        grad_outs + [like((8, units), F32)],
        [hb, hb_other, du],
        [pltpu.VMEM((width, units), F32)],
        flops=2 * rows * width * units,
    )
    recv = order(recv, outer_g[0], inner_g[0])
    if staged:
        outer_m = scatter_middle(*outer_g[:2], "outer_g")
        (grad_outer_w,) = scatter_last(outer_m, [like((width // n, units), F32)], "outer_g")
    else:
        grad_outer_w = lax.psum_scatter(outer_g[0], "blk", scatter_dimension=0, tiled=True)
        grad_inner_w = lax.psum_scatter(inner_g[0], "blk", scatter_dimension=0, tiled=True)

    e_one, eb_one = kernel_call(
        "norm_back",
        norm_back_kernel,
        [like((half, width), F32), like((half + EXTRA, width))],
        [chip, recv, e_two, normal_one, inv_one, vectors],
    )
    eb_one_other = swap(eb_one, "head", 1, "eb_one")
    if staged:
        eb_one_other = order(eb_one_other, outer_m[0])
    back_outs = [like((slots // 2, 2 * local))] * 2 if staged else []
    eb_full, dq, dkv, *back = kernel_call(
        "attend_back",
        functools.partial(attend_back_kernel, n, count),
        [
            like((rows, width)),
            like((rows, local)),
            like((slots + rows, 2 * local)),
        ]
        + back_outs,
        [eb_one, eb_one_other, q, kv, mask, stat] + attend_p,
        [piece_scratch(attend_p)],
        flops=2 * rows * width * local * 8,
    )
    if staged:
        grad_outs = [like((width // 2 + EXTRA, width))] * 2
    else:
        grad_outs = [like((width, width), F32), like((EXTRA, width), F32)]
    attend_g = kernel_call(
        "attend_grad",
        attend_weights_kernel,
        grad_outs,
        [hidden_in] + parts + [dkv, dq, eb_full, a, eb_one, eb_one_other, outer_g[-1], inner_g[-1]],
        [pltpu.VMEM((width, width), F32)],
        flops=2 * rows * width * local * 8,
    )
    if staged:
        inner_m = scatter_middle(*inner_g[:2], "inner_g", after=dq)
        recv = swap(back[1], "blk", 1, "back_y")
        recv = order(recv, inner_m[0], grad_outer_w)
        pairs = kernel_call(
            "back_middle", back_middle_kernel, [like((slots // 4, 2 * local))] * 4, [back[0], recv]
        )
        moved = [pairs[0]] + [swap(pairs[k], "blk", 2 * k, f"back_z{2 * k}") for k in (1, 2, 3)]
        attend_m = scatter_middle(*attend_g, "attend_g", extra=EXTRA)
        (grad_inner_w,) = scatter_last(inner_m, [like((width // n, units), F32)], "inner_g")
        moved[0] = order(moved[0], attend_m[0])
    else:
        moved = dkv[:slots].reshape(4, n, share, 2 * local).transpose(1, 0, 2, 3)
        moved = lax.all_to_all(moved, "blk", 0, 0).reshape(slots, 2 * local)
        moved = [moved]
    mine, theirs = kernel_call(
        "token",
        functools.partial(token_kernel, n, room, per_block, len(moved), count),
        [like((half, width), F32), like((half, width))],
        [tag_row, dkv, dq] + moved + attend_p,
        [piece_scratch(attend_p), pltpu.VMEM((rows, width), F32)],
        flops=2 * rows * width * local * 4,
    )
    chip, recv = chip_sum(mine, theirs, "last")
    if staged:
        *grads, small = scatter_last(
            attend_m,
            [like((width // n, local), F32)] * 4 + [like((EXTRA, width), F32)],
            "attend_g",
        )
    else:
        summed = lax.psum_scatter(attend_g[0], "blk", scatter_dimension=0, tiled=True)
        grads = [summed[:, k * local : (k + 1) * local] for k in range(4)]
        small = lax.psum(attend_g[1], "blk")
    grad_key_w, grad_value_w, grad_query_w, grad_output_w = grads

    if staged:
        recv = order(recv, grad_inner_w)
    last = e_one + (chip.astype(F32) + recv.astype(F32))
    last_other = swap(last, "head", 1, "last")
    result_other = swap(result, "head", 1, "result")

    def joined(own, other):
        return jnp.where(
            core == 0, jnp.concatenate([own, other]), jnp.concatenate([other, own])
        )

    return (
        joined(result, result_other),
        joined(last, last_other),
        grad_query_w,
        grad_key_w,
        grad_value_w,
        grad_output_w,
        grad_inner_w,
        grad_outer_w,
        small[7, 2 * local : 3 * local],
        small[7, local : 2 * local],
        small[6],
        small[3],
        small[2],
        small[4],
        small[5],
        small[0],
        small[1],
    )


def solution(mesh):
    matrix = P("blk", "head")
    in_specs = (
        (P("blk", None),)
        + (matrix,) * 6
        + (P("head"), P("head"), P(), P("head"))
        + (P(),) * 5
        + (P("blk"), P("blk"), P("blk", None))
    )
    out_specs = (
        (P("blk", None), P("blk", None))
        + (matrix,) * 6
        + (P("head"), P("head"), P(), P("head"))
        + (P(),) * 5
    )
    return jax.shard_map(
        per_device, mesh=mesh, in_specs=in_specs, out_specs=out_specs, check_vma=False
    )
```

```python
import functools
import math

import jax
import jax.numpy as jnp
from jax import lax
from jax.experimental import pallas as pl
from jax.experimental.pallas import tpu as pltpu
from jax.sharding import PartitionSpec as P

DH = 64
CLUSTER = 128
EPS = 1e-06
NEG = -1e30
SCALE = 1.0 / math.sqrt(DH)
META = 128
EXTRA = 16
VMEM = 16 << 20
BF = jnp.bfloat16
F32 = jnp.float32


def swap(value, axis, bits, name):
    with jax.named_scope(name):
        return lax.ppermute(value, axis, [(i, i ^ bits) for i in range(lax.axis_size(axis))])


def dot(left, right):
    return jnp.dot(left, right, preferred_element_type=F32)


def dot_last(left, right):
    return lax.dot_general(left, right, (((1,), (1,)), ((), ())), preferred_element_type=F32)


def dot_first(left, right):
    return lax.dot_general(left, right, (((0,), (0,)), ((), ())), preferred_element_type=F32)


def kernel_call(name, body, outs, args, scratch=(), flops=0, space=pltpu.VMEM):
    size = sum(math.prod(a.shape) * a.dtype.itemsize for a in list(args) + list(outs))
    whole = pl.BlockSpec(memory_space=pltpu.VMEM)
    return pl.pallas_call(
        body,
        out_shape=tuple(outs),
        in_specs=[pl.BlockSpec(memory_space=space)] * len(args),
        out_specs=tuple([whole] * len(outs)),
        scratch_shapes=list(scratch),
        name=name,
        compiler_params=pltpu.CompilerParams(vmem_limit_bytes=VMEM),
        cost_estimate=pl.CostEstimate(flops=flops, bytes_accessed=size, transcendentals=0),
    )(*args)


def like(shape, dtype=BF):
    return jax.ShapeDtypeStruct(shape, dtype)


def norm_forward(value, gain, shift):
    centered = value - jnp.mean(value, axis=-1, keepdims=True)
    variance = jnp.mean(centered * centered, axis=-1, keepdims=True)
    inv_std = lax.rsqrt(variance + EPS)
    normal_part = centered * inv_std
    return (normal_part * gain + shift, normal_part, inv_std)


def norm_backward(grad_out, normal_part, inv_std, gain):
    scaled = grad_out * gain
    mean_one = jnp.mean(scaled, axis=-1, keepdims=True)
    mean_two = jnp.mean(scaled * normal_part, axis=-1, keepdims=True)
    grad_in = inv_std * (scaled - mean_one - normal_part * mean_two)
    return (
        grad_in,
        jnp.sum(grad_out * normal_part, axis=0, keepdims=True),
        jnp.sum(grad_out, axis=0, keepdims=True),
    )


def extra_rows(*rows):
    width = rows[0].shape[1]
    return jnp.concatenate(list(rows) + [jnp.zeros((EXTRA - len(rows), width), F32)]).astype(BF)


def whole_matrix(pieces, plan, scratch):
    if len(pieces) == 1:
        return pieces[0][...]
    me = lax.axis_index("blk")
    rows, width = scratch.shape[1:]
    for piece, (sources, at) in zip(pieces, plan):
        for k, source in enumerate(sources):
            if len(piece.shape) == 3:
                scratch[me ^ source] = piece[k, :, at : at + width]
            else:
                scratch[me ^ source] = piece[k * rows : (k + 1) * rows, at : at + width]
    return scratch[...].reshape(-1, width)


def order(value, *after):
    return lax.optimization_barrier((value,) + after)[0]


def piece_scratch(pieces, width):
    if len(pieces) == 1:
        return pltpu.VMEM((8, 128), BF)
    return pltpu.VMEM((8, pieces[0].shape[0], width), BF)


def places(tag_row, n, per_block, rows):
    target = tag_row // per_block
    onehot = lax.broadcasted_iota(jnp.int32, (n, rows), 0) == target
    earlier = lax.broadcasted_iota(jnp.int32, (rows, rows), 0) < lax.broadcasted_iota(
        jnp.int32, (rows, rows), 1
    )
    count = dot(onehot.astype(F32).astype(BF), earlier.astype(F32).astype(BF))
    rank = jnp.sum(jnp.where(onehot, count, 0.0), axis=0, keepdims=True).astype(jnp.int32)
    return target, rank


def fetch(sources, held, sems):
    copies = [
        pltpu.make_async_copy(source, to, sems.at[k])
        for k, (source, to) in enumerate(zip(sources, held))
    ]
    for copy in copies:
        copy.start()
    for copy in copies:
        copy.wait()


def pack_kernel(n, room, per_block, groups, *refs):
    count = 18
    sources, rest = refs[:count], refs[count:]
    held, sems = rest[-count - 1 : -1], rest[-1]
    *sends, attend_ref, all_ref, vec_ref = rest[: -count - 1]
    fetch(sources, held, sems)
    at = 0
    for k, shard in enumerate(held[:6]):
        if k < 4:
            attend_ref[:, at : at + shard.shape[1]] = shard[...]
        all_ref[:, at : at + shard.shape[1]] = shard[...]
        at += shard.shape[1]
    x_ref, tag_ref, doc_ref, value_b, query_b, *vectors = held[6:]
    blank = jnp.zeros((1, value_b.shape[0]), F32)
    biases = [blank, value_b[...].reshape(1, -1), query_b[...].reshape(1, -1), blank]
    vec_ref[...] = jnp.concatenate(
        [jnp.concatenate(biases, axis=1)] + [item[...].reshape(1, -1) for item in vectors]
    )
    rows, width = x_ref.shape
    share = room // groups
    target, rank = places(tag_ref[...], n, per_block, rows)
    offset = rank - lax.axis_index("head") * share
    inside = (offset >= 0) & (offset < share)
    code = (1 + doc_ref[...] * per_block + tag_ref[...] % per_block).astype(F32)
    if len(sends) == 1:
        (out_ref,) = sends
        place = jnp.where(inside, target * share + offset, -1)
        pick = lax.broadcasted_iota(jnp.int32, (n * share, rows), 0) == place
        out_ref[:, :width] = dot(pick.astype(F32).astype(BF), x_ref[...]).astype(BF)
        code = jnp.sum(jnp.where(pick, code, 0.0), axis=1, keepdims=True)
        out_ref[:, width:] = jnp.broadcast_to(code, (n * share, META)).astype(BF)
        return
    odd = lax.axis_index("blk") % 2
    for t, out_ref in enumerate(sends):
        there = inside & (target % 2 == odd ^ t)
        place = jnp.where(there, target // 2 * share + offset, -1)
        pick = lax.broadcasted_iota(jnp.int32, (4 * share, rows), 0) == place
        out_ref[: 4 * share, :] = dot(pick.astype(F32).astype(BF), x_ref[...]).astype(BF)
        level = lax.broadcasted_iota(jnp.int32, (EXTRA, rows), 0)
        codes = jnp.where(there & (target // 2 == level), code, 0.0).astype(BF)
        spot = lax.broadcasted_iota(jnp.int32, (META, rows), 0) == offset
        tile = dot_last(codes, spot.astype(F32).astype(BF)).astype(BF)
        out_ref[4 * share :, :META] = tile
        out_ref[4 * share :, META:] = jnp.zeros((EXTRA, width - META), BF)


def route_kernel(keep_ref, recv_ref, *outs):
    level = lax.axis_index("blk") // 2
    rows, share = 0, (keep_ref.shape[0] - EXTRA) // 4
    width = keep_ref.shape[1]
    lanes = lax.broadcasted_iota(jnp.int32, (EXTRA, META), 0)
    for k in range(4):
        z = level ^ k
        for t, ref in enumerate((keep_ref, recv_ref)):
            outs[k][rows + t * share : rows + (t + 1) * share, :] = ref[pl.ds(z * share, share), :]
        first = keep_ref[4 * share :, :META].astype(F32)
        second = recv_ref[4 * share :, :META].astype(F32)
        first = jnp.sum(jnp.where(lanes == z, first, 0.0), axis=0, keepdims=True)
        second = jnp.sum(jnp.where(lanes == z, second, 0.0), axis=0, keepdims=True)
        tile = jnp.where(lanes == 0, first, jnp.where(lanes == 1, second, 0.0))
        outs[k][rows + 2 * share :, :META] = tile.astype(BF)
        outs[k][rows + 2 * share :, META:] = jnp.zeros((EXTRA, width - META), BF)


def stack_kernel(*refs):
    out_ref, at = refs[-1], 0
    for ref in refs[:-1]:
        if len(ref.shape) == 3:
            out_ref[at : at + ref.shape[0]] = ref[...]
            at += ref.shape[0]
        else:
            out_ref[at] = ref[...]
            at += 1


def stack(name, *parts):
    count = sum(1 if part.ndim == 2 else part.shape[0] for part in parts)
    (out,) = kernel_call(name, stack_kernel, [like((count,) + parts[0].shape[-2:])], parts)
    return out


def gather_far(value, facing, name, hold=None):
    far = swap(value, "blk", 4, name + "_far")
    near = swap(stack(name + "_pair", value, far), "blk", 2, name + "_near")
    rest = stack(name + "_rest", far, near)
    return [value, facing, far, near], rest


def slots_kernel(*refs):
    out_ref = refs[4]
    share, width = (refs[0].shape[0] - EXTRA) // 2, refs[0].shape[1]
    lane = lax.broadcasted_iota(jnp.int32, (2 * share, META), 1)
    row = lax.broadcasted_iota(jnp.int32, (2 * share, META), 0)
    for k, ref in enumerate(refs[:4]):
        at = slice(2 * k * share, 2 * (k + 1) * share)
        out_ref[at, :width] = ref[: 2 * share, :]
        codes = ref[2 * share :, :META].astype(F32)
        spread = jnp.where(row < share, codes[:1, :], codes[1:2, :])
        code = jnp.sum(jnp.where(lane == row % share, spread, 0.0), axis=1, keepdims=True)
        out_ref[at, width:] = jnp.broadcast_to(code, (2 * share, META)).astype(BF)


def attend_kernel(per_block, count, plan, *refs):
    x_ref, tag_ref, doc_ref, bias_ref = refs[:4]
    parts = refs[4:8]
    pieces = refs[8 : 8 + count]
    mine_ref, theirs_ref, a_ref, q_ref, kv_ref, mask_ref, stat_ref, scratch, y_ref = refs[
        8 + count :
    ]
    rows, width = x_ref.shape
    local = a_ref.shape[1]
    slots = kv_ref.shape[0] - rows
    step = slots // 4
    me = lax.axis_index("blk")
    core = lax.axis_index("head") % 2
    weight = whole_matrix(pieces, plan, scratch)
    own = dot(x_ref[...], weight[:, : 3 * local]) + bias_ref[:1, : 3 * local]
    q_ref[...] = own[:, 2 * local :].astype(BF)
    kv_ref[slots:, :] = own[:, : 2 * local].astype(BF)
    row_cluster = lax.broadcasted_iota(jnp.int32, (1, rows), 1) // CLUSTER
    wanted = (1 + doc_ref[...] * per_block + row_cluster).astype(F32)
    for k in range(4):
        part = parts[k]
        kv_ref[k * step : (k + 1) * step, :] = (
            dot(part[:, :width], weight[:, : 2 * local]) + bias_ref[:1, : 2 * local]
        ).astype(BF)
        code = part[:, width : width + 1].astype(F32)
        mask_ref[k * step : (k + 1) * step, :] = jnp.where(code == wanted, 0.0, NEG).astype(BF)
    alone = tag_ref[...] != me * per_block + row_cluster
    diagonal = lax.broadcasted_iota(jnp.int32, (rows, rows), 0) == lax.broadcasted_iota(
        jnp.int32, (rows, rows), 1
    )
    mask_ref[slots:, :] = jnp.where(diagonal & alone, 0.0, NEG).astype(BF)
    mask = mask_ref[...].astype(F32)
    stats = []
    for j in range(local // DH):
        cut = slice(j * DH, (j + 1) * DH)
        scores = dot_last(kv_ref[:, cut], q_ref[:, cut]) * SCALE + mask
        top = jnp.max(scores, axis=0, keepdims=True)
        weights = jnp.exp(scores - top)
        inverse = 1.0 / jnp.sum(weights, axis=0, keepdims=True)
        probs = (weights * inverse).astype(BF)
        value = kv_ref[:, local + j * DH : local + (j + 1) * DH]
        a_ref[:, cut] = dot_first(probs, value).astype(BF)
        stats += [top, inverse]
    stat_ref[...] = jnp.concatenate(stats + [jnp.zeros((8 - len(stats), rows), F32)])
    y_ref[...] = dot_last(a_ref[...], weight[:, 3 * local :])
    half = rows // 2
    mine_ref[...] = y_ref[pl.ds(core * half, half), :]
    theirs_ref[...] = y_ref[pl.ds((1 - core) * half, half), :].astype(BF)


def attend_back_kernel(n, count, plan, *refs):
    own_ref, other_ref, q_ref, kv_ref, mask_ref, stat_ref = refs[:6]
    pieces = refs[6 : 6 + count]
    eb_ref, dq_ref, dkv_ref = refs[6 + count : 9 + count]
    back, scratch = refs[9 + count : -1], refs[-1]
    rows, local = q_ref.shape
    slots = kv_ref.shape[0] - rows
    half = rows // 2
    core = lax.axis_index("head") % 2
    weight = whole_matrix(pieces, plan, scratch)
    eb_ref[pl.ds(core * half, half), :] = own_ref[:half, :]
    eb_ref[pl.ds((1 - core) * half, half), :] = other_ref[:half, :]
    da = dot(eb_ref[...], weight[:, 3 * local :]).astype(BF)
    mask = mask_ref[...].astype(F32)
    for j in range(local // DH):
        cut = slice(j * DH, (j + 1) * DH)
        key, query = kv_ref[:, cut], q_ref[:, cut]
        value = kv_ref[:, local + j * DH : local + (j + 1) * DH]
        scores = dot_last(key, query) * SCALE + mask
        probs = jnp.exp(scores - stat_ref[2 * j : 2 * j + 1, :]) * stat_ref[
            2 * j + 1 : 2 * j + 2, :
        ]
        low = probs.astype(BF)
        dkv_ref[:, local + j * DH : local + (j + 1) * DH] = dot(low, da[:, cut]).astype(BF)
        grad = dot_last(value, da[:, cut])
        delta = jnp.sum(low.astype(F32) * grad, axis=0, keepdims=True)
        grad = (probs * (grad - delta)).astype(BF)
        dkv_ref[:, cut] = (dot(grad, query) * SCALE).astype(BF)
        dq_ref[:, cut] = (dot_first(grad, key) * SCALE).astype(BF)
    if back:
        level = lax.axis_index("blk") // 2
        share = slots // 4 // n
        for t in range(2):
            for z in range(4):
                for k in range(4):
                    at = k * slots // 4 + (2 * (z ^ level) + t) * share
                    to = (z * 4 + k) * share
                    back[t][to : to + share, :] = dkv_ref[pl.ds(at, share), :]


def back_middle_kernel(keep_ref, recv_ref, *outs):
    level = lax.axis_index("blk") // 2
    room = outs[0].shape[0] // 2
    for k in range(4):
        at = pl.ds((level ^ k) * room, room)
        outs[k][:room, :] = keep_ref[at, :]
        outs[k][room:, :] = recv_ref[at, :]


def token_kernel(n, room, per_block, parts, count, plan, *refs):
    tag_ref, dkv_ref, dq_ref = refs[:3]
    back = refs[3 : 3 + parts]
    pieces = refs[3 + parts : 3 + parts + count]
    mine_ref, theirs_ref, scratch, z_ref = refs[3 + parts + count :]
    rows, local = dq_ref.shape
    slots = n * room
    half = rows // 2
    share = room // 4
    group = lax.axis_index("head")
    core = group % 2
    weight = whole_matrix(pieces, plan, scratch)
    target, rank = places(tag_ref[...], n, per_block, rows)
    if parts > 1:
        target = target ^ lax.axis_index("blk")
    place = target * room + ((rank // share) ^ group) * share + rank % share
    total = dkv_ref[slots:, :].astype(F32)
    step = slots // parts
    for k in range(parts):
        pick = lax.broadcasted_iota(jnp.int32, (step, rows), 0) + k * step == place
        total = total + dot_first(pick.astype(F32).astype(BF), back[k][...])
    z_ref[...] = dot_last(total.astype(BF), weight[:, : 2 * local]) + dot_last(
        dq_ref[...], weight[:, 2 * local : 3 * local]
    )
    mine_ref[...] = z_ref[pl.ds(core * half, half), :]
    theirs_ref[...] = z_ref[pl.ds((1 - core) * half, half), :].astype(BF)


def norm_one_kernel(
    chip_ref, recv_ref, x_ref, vec_ref, h_ref, n_ref, r_ref, hb_ref
):
    half = chip_ref.shape[0]
    core = lax.axis_index("head") % 2
    branch = chip_ref[...].astype(F32) + recv_ref[...].astype(F32) + vec_ref[1:2, :]
    value = x_ref[pl.ds(core * half, half), :].astype(F32) + branch
    h, normal, inverse = norm_forward(value, vec_ref[2:3, :], vec_ref[3:4, :])
    h_ref[...] = h
    n_ref[...] = normal
    r_ref[...] = inverse
    hb_ref[...] = h.astype(BF)


def norm_two_kernel(
    chip_ref, recv_ref, h_ref, vec_ref, c_ref, out_ref, e_ref, eb_ref
):
    half = chip_ref.shape[0]
    core = lax.axis_index("head") % 2
    outer = chip_ref[...].astype(F32) + recv_ref[...].astype(F32) + vec_ref[4:5, :]
    gain_row = vec_ref[5:6, :]
    result, normal, inverse = norm_forward(h_ref[...] + outer, gain_row, vec_ref[6:7, :])
    out_ref[...] = result.astype(BF)
    cotangent = c_ref[pl.ds(core * half, half), :].astype(F32)
    grad, gain, shift = norm_backward(cotangent, normal, inverse, gain_row)
    e_ref[...] = grad
    eb_ref[:half, :] = grad.astype(BF)
    eb_ref[half:, :] = extra_rows(gain, shift)


def norm_back_kernel(chip_ref, recv_ref, e_ref, n_ref, r_ref, vec_ref, out_ref, eb_ref):
    half = chip_ref.shape[0]
    grad = e_ref[...] + (chip_ref[...].astype(F32) + recv_ref[...].astype(F32))
    grad, gain, shift = norm_backward(grad, n_ref[...], r_ref[...], vec_ref[2:3, :])
    out_ref[...] = grad
    eb_ref[:half, :] = grad.astype(BF)
    eb_ref[half:, :] = extra_rows(gain, shift)


def inner_kernel(count, plan, *refs):
    own_ref, other_ref, bias_ref = refs[:3]
    pieces = refs[3 : 3 + count]
    g_ref, slope_ref, scratch = refs[3 + count :]
    half = own_ref.shape[0]
    weight = whole_matrix(pieces, plan, scratch)
    for k, part in enumerate((own_ref, other_ref)):
        u = dot(part[...], weight) + bias_ref[7:8, :]
        below = 0.5 * (1.0 + lax.erf(u * math.sqrt(0.5)))
        g_ref[k * half : (k + 1) * half, :] = (u * below).astype(BF)
        density = jnp.exp(-0.5 * u * u) * (1.0 / math.sqrt(2.0 * math.pi))
        slope_ref[k * half : (k + 1) * half, :] = below + u * density


def outer_kernel(count, plan, *refs):
    g_ref = refs[0]
    pieces = refs[1 : 1 + count]
    mine_ref, theirs_ref, scratch = refs[1 + count :]
    half = mine_ref.shape[0]
    weight = whole_matrix(pieces, plan, scratch)
    mine_ref[...] = dot_last(g_ref[:half, :], weight)
    theirs_ref[...] = dot_last(g_ref[half:, :], weight).astype(BF)


def ff_back_kernel(count, outer_plan, inner_plan, *refs):
    own_ref, other_ref, slope_ref = refs[:3]
    outer, inner = refs[3 : 3 + count], refs[3 + count : 3 + 2 * count]
    mine_ref, theirs_ref, du_ref, scratch, scratch_two = refs[3 + 2 * count :]
    half = mine_ref.shape[0]
    outer = whole_matrix(outer, outer_plan, scratch)
    inner = whole_matrix(inner, inner_plan, scratch_two)
    for k, part in ((1, other_ref), (0, own_ref)):
        rows = slice(k * half, (k + 1) * half)
        dg = dot(part[:half, :], outer).astype(BF).astype(F32)
        du_ref[rows, :] = (dg * slope_ref[rows, :]).astype(BF)
        dh = dot_last(du_ref[rows, :], inner)
        if k:
            theirs_ref[...] = dh.astype(BF)
        else:
            mine_ref[...] = dh


def split_pieces(total, mine_ref, theirs_ref):
    me = lax.axis_index("blk")
    odd = me % 2
    rows = total.shape[0] // 8
    for z in range(4):
        at = slice(z * rows, (z + 1) * rows)
        mine_ref[at, :] = total[pl.ds((2 * z + odd) * rows, rows), :].astype(BF)
        theirs_ref[at, :] = total[pl.ds((2 * z + 1 - odd) * rows, rows), :].astype(BF)


def ff_weights_kernel(small, own_ref, other_ref, left_ref, *refs):
    half = left_ref.shape[0] // 2
    refs = list(refs)
    total = refs.pop()
    total[...] = dot_first(own_ref[:half, :], left_ref[:half, :]) + dot_first(
        other_ref[:half, :], left_ref[half:, :]
    )
    if small == "outer":
        small_ref = refs.pop()
        norms = own_ref[half:, :].astype(F32) + other_ref[half:, :].astype(F32)
        bias = jnp.sum(own_ref[:half, :].astype(F32), axis=0, keepdims=True) + jnp.sum(
            other_ref[:half, :].astype(F32), axis=0, keepdims=True
        )
        small_ref[...] = jnp.concatenate([norms[:2], bias, jnp.zeros((5, bias.shape[1]), F32)])
    else:
        small_ref = refs.pop()
        bias = jnp.sum(left_ref[...].astype(F32), axis=0, keepdims=True)
        small_ref[...] = jnp.concatenate([bias, jnp.zeros((7, bias.shape[1]), F32)])
    if len(refs) == 1:
        refs[0][...] = total[...]
    else:
        split_pieces(total, *refs)


def attend_weights_kernel(*refs):
    x_ref, p0, p1, p2, p3, dkv_ref, dq_ref, eb_ref, a_ref, own_ref, other_ref = refs[:11]
    outer_ref, inner_ref = refs[11:13]
    outs, total = list(refs[13:-1]), refs[-1]
    rows, width = x_ref.shape
    local = dq_ref.shape[1]
    slots = dkv_ref.shape[0] - rows
    step = slots // 4
    sums = dot_first(x_ref[...], dkv_ref[slots:, :])
    for k, part in enumerate((p0, p1, p2, p3)):
        sums = sums + dot_first(part[:, :width], dkv_ref[k * step : (k + 1) * step, :])
    total[:, : 2 * local] = sums
    total[:, 2 * local : 3 * local] = dot_first(x_ref[...], dq_ref[...])
    total[:, 3 * local :] = dot_first(eb_ref[...], a_ref[...])
    half = rows // 2
    norms = own_ref[half:, :].astype(F32) + other_ref[half:, :].astype(F32)
    output_b = jnp.sum(eb_ref[...].astype(F32), axis=0, keepdims=True)
    query_b = jnp.sum(dq_ref[...].astype(F32), axis=0, keepdims=True)
    value_b = jnp.sum(dkv_ref[...].astype(F32), axis=0, keepdims=True)
    last = jnp.concatenate([value_b, query_b, jnp.zeros((1, width - 3 * local), F32)], axis=1)
    small = jnp.concatenate(
        [
            outer_ref[:3, :],
            inner_ref[:1, :],
            norms[:2],
            output_b,
            last,
            jnp.zeros((EXTRA - 8, width), F32),
        ]
    )
    if outs[0].shape == total.shape:
        outs[0][...] = total[...]
        outs[1][...] = small
    else:
        split_pieces(total, *outs)
        body = outs[0].shape[0] - EXTRA
        outs[0][body:, :] = small.astype(BF)
        outs[1][body:, :] = small.astype(BF)


def middle_kernel(extra, near, mine_ref, recv_ref, *outs):
    level = lax.axis_index("blk") // 2
    if near:
        rows = (mine_ref.shape[0] - extra) // 4
        order_of = ((level ^ 1, level ^ 3), (level, level ^ 2))
    else:
        rows = (mine_ref.shape[0] - extra) // 2
        order_of = ((1,), (0,))
    last = mine_ref.shape[0] - extra
    for out, pieces in zip(outs, order_of):
        for k, piece in enumerate(pieces):
            at = pl.ds(piece * rows, rows)
            out[k * rows : (k + 1) * rows, :] = (
                mine_ref[at, :].astype(F32) + recv_ref[at, :].astype(F32)
            ).astype(BF)
        if extra:
            small = mine_ref[last:, :].astype(F32) + recv_ref[last:, :].astype(F32)
            out[len(pieces) * rows :, :] = small.astype(BF)


def last_kernel(left_ref, right_ref, *outs):
    total = left_ref[...].astype(F32) + right_ref[...].astype(F32)
    if len(outs) == 1:
        outs[0][...] = total
        return
    rows, local = outs[0].shape
    for k in range(4):
        outs[k][...] = total[:rows, k * local : (k + 1) * local]
    spread_small(total[rows:, :], local, outs[4:])


def spread_small(small, local, outs):
    for k, out in enumerate(outs[:7]):
        out[...] = small[k, :]
    outs[7][...] = small[7, 2 * local : 3 * local]
    outs[8][...] = small[7, local : 2 * local]


def small_kernel(small_ref, *outs):
    spread_small(small_ref[...], outs[7].shape[0], outs)


def scatter_step(name, mine, recv, near, extra=0):
    rows = (mine.shape[0] - extra) // 2 + extra
    return kernel_call(
        name,
        functools.partial(middle_kernel, extra, near),
        [like((rows, mine.shape[1]))] * 2,
        [mine, recv],
    )


def chip_sum(mine, theirs, name):
    chip = (mine + swap(theirs, "head", 1, name + "_chip").astype(F32)).astype(BF)
    return chip, swap(chip, "head", 2, name + "_x")


def per_device(
    hidden_in,
    query_w,
    key_w,
    value_w,
    output_w,
    inner_w,
    outer_w,
    query_b,
    value_b,
    output_b,
    inner_b,
    outer_b,
    first_gain,
    first_shift,
    second_gain,
    second_shift,
    key_cluster,
    document,
    cotangent,
):
    rows, width = hidden_in.shape
    n = lax.axis_size("blk")
    groups = lax.axis_size("head")
    assert groups == 4
    local = query_w.shape[1]
    units = inner_w.shape[1]
    per_block = rows // CLUSTER
    room = 2 * rows // n
    slots = n * room
    half = rows // 2
    share = room // groups
    staged = n == 8
    core = lax.axis_index("head") % 2

    tag_row, doc_row = key_cluster.reshape(1, rows), document.reshape(1, rows)

    if staged:
        sends = [like((4 * share + EXTRA, width))] * 2
    else:
        sends = [like((n * share, width + META))]
    pack_args = [key_w, value_w, query_w, output_w, inner_w, outer_w]
    pack_args += [hidden_in, tag_row, doc_row, value_b, query_b, output_b]
    pack_args += [first_gain, first_shift, outer_b, second_gain, second_shift, inner_b]
    *sent, attend_w, all_w, vectors = kernel_call(
        "pack",
        functools.partial(pack_kernel, n, room, per_block, groups),
        sends
        + [
            like((width // n, 4 * local)),
            like((width // n, 4 * local + 2 * units)),
            like((8, width), F32),
        ],
        [pltpu.with_memory_space_constraint(item, pltpu.HBM) for item in pack_args],
        [pltpu.VMEM(item.shape, item.dtype) for item in pack_args]
        + [pltpu.SemaphoreType.DMA((len(pack_args),))],
        flops=2 * n * share * rows * width,
        space=pltpu.HBM,
    )
    if staged:
        column = lambda value, name: [
            swap(value[k], "blk", 2 * k, f"{name}_z{2 * k}") for k in (1, 2, 3)
        ]
        slots_y = swap(sent[1], "blk", 1, "slots_y")
        attend_column = column([attend_w] * 4, "attend_w")
        messages = kernel_call(
            "route", route_kernel, [like((2 * share + EXTRA, width))] * 4, [sent[0], slots_y]
        )
        arrived = [messages[0]] + column(messages, "slots")
        facing = swap(order(all_w, slots_y), "blk", 1, "facing_w")
        arrived[0] = order(arrived[0], facing)
        (moved,) = kernel_call("slots", slots_kernel, [like((n * share, width + META))], arrived)
        rest = swap(stack("attend_w_rest", *attend_column), "blk", 1, "attend_w_rest")
        attend_p = [attend_w, facing] + attend_column + [rest]
        inner_p, inner_rest = gather_far(order(inner_w, *attend_column), facing, "inner_w")
        outer_p, outer_rest = gather_far(order(outer_w, inner_p[2]), facing, "outer_w")
        inner_p.append(swap(inner_rest, "blk", 1, "inner_w_rest"))
        outer_p.append(swap(outer_rest, "blk", 1, "outer_w_rest"))
    else:
        moved = lax.all_to_all(sent[0].reshape(n, share, width + META), "blk", 0, 0)
        moved = moved.reshape(sent[0].shape)
        gather = lambda value: [lax.all_gather(value, "blk", axis=0, tiled=True)]
        attend_p, inner_p, outer_p = gather(attend_w), gather(inner_w), gather(outer_w)
    far = swap(moved, "head", 2, "slots_x")
    parts = [moved, swap(moved, "head", 1, "slots_chip"), far, swap(far, "head", 1, "slots_far")]
    attend_plan = [((0,), 0), ((1,), 0), ((2,), 0), ((4,), 0), ((6,), 0), ((3, 5, 7), 0)]
    inner_plan = [((0,), 0), ((1,), 4 * local), ((4,), 0), ((2, 6), 0), ((5, 3, 7), 0)]
    outer_plan = [((0,), 0), ((1,), 4 * local + units), ((4,), 0), ((2, 6), 0), ((5, 3, 7), 0)]

    count = len(attend_p)
    mine, theirs, a, q, kv, mask, stat = kernel_call(
        "attend",
        functools.partial(attend_kernel, per_block, count, attend_plan),
        [
            like((half, width), F32),
            like((half, width)),
            like((rows, local)),
            like((rows, local)),
            like((slots + rows, 2 * local)),
            like((slots + rows, rows)),
            like((8, rows), F32),
        ],
        [hidden_in, tag_row, doc_row, vectors] + parts + attend_p,
        [piece_scratch(attend_p, 4 * local), pltpu.VMEM((rows, width), F32)],
        flops=2 * rows * width * local * 9,
    )
    if staged:
        mine = order(mine, inner_p[3], outer_p[2])
    chip, recv = chip_sum(mine, theirs, "branch")
    if staged:
        recv = order(recv, outer_p[3])
    h, normal_one, inv_one, hb = kernel_call(
        "norm_one",
        norm_one_kernel,
        [
            like((half, width), F32),
            like((half, width), F32),
            like((half, 1), F32),
            like((half, width)),
        ],
        [chip, recv, hidden_in, vectors],
    )
    hb_other = swap(hb, "head", 1, "hb")

    g, slope = kernel_call(
        "inner",
        functools.partial(inner_kernel, len(inner_p), inner_plan),
        [like((rows, units)), like((rows, units), F32)],
        [hb, hb_other, vectors] + inner_p,
        [piece_scratch(inner_p, units)],
        flops=2 * rows * width * units,
    )
    mine, theirs = kernel_call(
        "outer",
        functools.partial(outer_kernel, len(outer_p), outer_plan),
        [like((half, width), F32), like((half, width))],
        [g] + outer_p,
        [piece_scratch(outer_p, units)],
        flops=2 * rows * width * units,
    )
    chip, recv = chip_sum(mine, theirs, "ff")
    result, e_two, eb_two = kernel_call(
        "norm_two",
        norm_two_kernel,
        [like((half, width)), like((half, width), F32), like((half + EXTRA, width))],
        [chip, recv, h, vectors, cotangent],
    )
    eb_two_other = swap(eb_two, "head", 1, "eb_two")
    mine, theirs, du = kernel_call(
        "ff_back",
        functools.partial(ff_back_kernel, len(outer_p), outer_plan, inner_plan),
        [like((half, width), F32), like((half, width)), like((rows, units))],
        [eb_two, eb_two_other, slope] + outer_p + inner_p,
        [piece_scratch(outer_p, units), piece_scratch(inner_p, units)],
        flops=4 * rows * width * units,
    )
    chip, recv = chip_sum(mine, theirs, "ff_back")

    if staged:
        grad_outs = [like((width // 2, units)), like((width // 2, units))]
    else:
        grad_outs = [like((width, units), F32)]
    outer_g = kernel_call(
        "outer_grad",
        functools.partial(ff_weights_kernel, "outer"),
        grad_outs + [like((8, width), F32)],
        [eb_two, eb_two_other, g],
        [pltpu.VMEM((width, units), F32)],
        flops=2 * rows * width * units,
    )
    inner_g = kernel_call(
        "inner_grad",
        functools.partial(ff_weights_kernel, "inner"),
        grad_outs + [like((8, units), F32)],
        [hb, hb_other, du],
        [pltpu.VMEM((width, units), F32)],
        flops=2 * rows * width * units,
    )
    recv = order(recv, outer_g[0], inner_g[0])
    grad_units = [like((width // n, units), F32)]
    if staged:
        outer_y = swap(outer_g[1], "blk", 1, "outer_g_y")
        outer_m = scatter_step("outer_g_one", outer_g[0], outer_y, True)
    else:
        grad_outer_w = lax.psum_scatter(outer_g[0], "blk", scatter_dimension=0, tiled=True)
        grad_inner_w = lax.psum_scatter(inner_g[0], "blk", scatter_dimension=0, tiled=True)

    e_one, eb_one = kernel_call(
        "norm_back",
        norm_back_kernel,
        [like((half, width), F32), like((half + EXTRA, width))],
        [chip, recv, e_two, normal_one, inv_one, vectors],
    )
    eb_one_other = swap(eb_one, "head", 1, "eb_one")
    if staged:
        eb_one_other = order(eb_one_other, outer_m[0])
    back_outs = [like((slots // 2, 2 * local))] * 2 if staged else []
    eb_full, dq, dkv, *back = kernel_call(
        "attend_back",
        functools.partial(attend_back_kernel, n, count, attend_plan),
        [
            like((rows, width)),
            like((rows, local)),
            like((slots + rows, 2 * local)),
        ]
        + back_outs,
        [eb_one, eb_one_other, q, kv, mask, stat] + attend_p,
        [piece_scratch(attend_p, 4 * local)],
        flops=2 * rows * width * local * 8,
    )
    if staged:
        grad_outs = [like((width // 2 + EXTRA, width))] * 2
    else:
        grad_outs = [like((width, width), F32), like((EXTRA, width), F32)]
    attend_g = kernel_call(
        "attend_grad",
        attend_weights_kernel,
        grad_outs,
        [hidden_in] + parts + [dkv, dq, eb_full, a, eb_one, eb_one_other, outer_g[-1], inner_g[-1]],
        [pltpu.VMEM((width, width), F32)],
        flops=2 * rows * width * local * 8,
    )
    if staged:
        outer_near = swap(outer_m[0], "blk", 2, "outer_g_near")
        outer_m = scatter_step("outer_g_two", outer_m[1], outer_near, False)
        inner_y = swap(inner_g[1], "blk", 1, "inner_g_y")
        inner_y = order(inner_y, attend_g[1], outer_m[0])
        inner_m = scatter_step("inner_g_one", inner_g[0], inner_y, True)
        recv = swap(back[1], "blk", 1, "back_y")
        attend_y = swap(order(attend_g[1], recv), "blk", 1, "attend_g_y")
        recv = order(recv, inner_m[0])
        pairs = kernel_call(
            "back_middle", back_middle_kernel, [like((slots // 4, 2 * local))] * 4, [back[0], recv]
        )
        moved = [pairs[0]] + [swap(pairs[k], "blk", 2 * k, f"back_z{2 * k}") for k in (1, 2, 3)]
        inner_near = swap(inner_m[0], "blk", 2, "inner_g_near")
        outer_far = swap(outer_m[0], "blk", 4, "outer_g_far")
        inner_m = scatter_step("inner_g_two", inner_m[1], inner_near, False)
        (grad_outer_w,) = kernel_call(
            "outer_g_last", last_kernel, grad_units, [outer_m[1], outer_far]
        )
        inner_far = swap(inner_m[0], "blk", 4, "inner_g_far")
        (grad_inner_w,) = kernel_call(
            "inner_g_last", last_kernel, grad_units, [inner_m[1], inner_far]
        )
        moved[0] = order(moved[0], grad_inner_w, grad_outer_w)
    else:
        moved = dkv[:slots].reshape(4, n, share, 2 * local).transpose(1, 0, 2, 3)
        moved = lax.all_to_all(moved, "blk", 0, 0).reshape(slots, 2 * local)
        moved = [moved]
    mine, theirs = kernel_call(
        "token",
        functools.partial(
            token_kernel, n, room, per_block, len(moved), count, attend_plan
        ),
        [like((half, width), F32), like((half, width))],
        [tag_row, dkv, dq] + moved + attend_p,
        [piece_scratch(attend_p, 4 * local), pltpu.VMEM((rows, width), F32)],
        flops=2 * rows * width * local * 4,
    )
    if staged:
        attend_m = scatter_step("attend_g_one", attend_g[0], attend_y, True, EXTRA)
        mine = order(mine, attend_m[0])
    chip, recv = chip_sum(mine, theirs, "last")
    last = e_one + (chip.astype(F32) + recv.astype(F32))
    last_other = swap(last, "head", 1, "last")
    result_other = swap(result, "head", 1, "result")

    def joined(own, other):
        return jnp.where(
            core == 0, jnp.concatenate([own, other]), jnp.concatenate([other, own])
        )

    layer_out = joined(result, result_other)
    grad_input = joined(last, last_other)
    small_outs = [like((width,), F32)] * 7 + [like((local,), F32)] * 2
    if staged:
        attend_near = swap(attend_m[0], "blk", 2, "attend_g_near")
        attend_m = scatter_step("attend_g_two", attend_m[1], attend_near, False, EXTRA)
        attend_far = swap(attend_m[0], "blk", 4, "attend_g_far")
        attend_far = order(attend_far, grad_input, layer_out)
        grads = kernel_call(
            "attend_g_last",
            last_kernel,
            [like((width // n, local), F32)] * 4 + small_outs,
            [attend_m[1], attend_far],
        )
        grads, small = grads[:4], grads[4:]
    else:
        summed = lax.psum_scatter(attend_g[0], "blk", scatter_dimension=0, tiled=True)
        grads = [summed[:, k * local : (k + 1) * local] for k in range(4)]
        small = kernel_call("small", small_kernel, small_outs, [lax.psum(attend_g[1], "blk")])
    grad_key_w, grad_value_w, grad_query_w, grad_output_w = grads

    return (
        layer_out,
        grad_input,
        grad_query_w,
        grad_key_w,
        grad_value_w,
        grad_output_w,
        grad_inner_w,
        grad_outer_w,
        small[7],
        small[8],
        small[6],
        small[3],
        small[2],
        small[4],
        small[5],
        small[0],
        small[1],
    )


def solution(mesh):
    matrix = P("blk", "head")
    in_specs = (
        (P("blk", None),)
        + (matrix,) * 6
        + (P("head"), P("head"), P(), P("head"))
        + (P(),) * 5
        + (P("blk"), P("blk"), P("blk", None))
    )
    out_specs = (
        (P("blk", None), P("blk", None))
        + (matrix,) * 6
        + (P("head"), P("head"), P(), P("head"))
        + (P(),) * 5
    )
    return jax.shard_map(
        per_device, mesh=mesh, in_specs=in_specs, out_specs=out_specs, check_vma=False
    )
```

```python
import functools
import math

import jax
import jax.numpy as jnp
from jax import lax
from jax.experimental import pallas as pl
from jax.experimental.pallas import tpu as pltpu
from jax.sharding import PartitionSpec as P

DH = 64
CLUSTER = 128
EPS = 1e-06
NEG = -1e30
SCALE = 1.0 / math.sqrt(DH)
META = 128
EXTRA = 16
VMEM = 16 << 20
BF = jnp.bfloat16
F32 = jnp.float32


def swap(value, axis, bits, name):
    with jax.named_scope(name):
        return lax.ppermute(value, axis, [(i, i ^ bits) for i in range(lax.axis_size(axis))])


def dot(left, right):
    return jnp.dot(left, right, preferred_element_type=F32)


def dot_last(left, right):
    return lax.dot_general(left, right, (((1,), (1,)), ((), ())), preferred_element_type=F32)


def dot_first(left, right):
    return lax.dot_general(left, right, (((0,), (0,)), ((), ())), preferred_element_type=F32)


def kernel_call(name, body, outs, args, scratch=(), flops=0, space=pltpu.VMEM):
    size = sum(math.prod(a.shape) * a.dtype.itemsize for a in list(args) + list(outs))
    whole = pl.BlockSpec(memory_space=pltpu.VMEM)
    return pl.pallas_call(
        body,
        out_shape=tuple(outs),
        in_specs=[pl.BlockSpec(memory_space=space)] * len(args),
        out_specs=tuple([whole] * len(outs)),
        scratch_shapes=list(scratch),
        name=name,
        compiler_params=pltpu.CompilerParams(vmem_limit_bytes=VMEM),
        cost_estimate=pl.CostEstimate(flops=flops, bytes_accessed=size, transcendentals=0),
    )(*args)


def like(shape, dtype=BF):
    return jax.ShapeDtypeStruct(shape, dtype)


def norm_forward(value, gain, shift):
    centered = value - jnp.mean(value, axis=-1, keepdims=True)
    variance = jnp.mean(centered * centered, axis=-1, keepdims=True)
    inv_std = lax.rsqrt(variance + EPS)
    normal_part = centered * inv_std
    return (normal_part * gain + shift, normal_part, inv_std)


def norm_backward(grad_out, normal_part, inv_std, gain):
    scaled = grad_out * gain
    mean_one = jnp.mean(scaled, axis=-1, keepdims=True)
    mean_two = jnp.mean(scaled * normal_part, axis=-1, keepdims=True)
    grad_in = inv_std * (scaled - mean_one - normal_part * mean_two)
    return (
        grad_in,
        jnp.sum(grad_out * normal_part, axis=0, keepdims=True),
        jnp.sum(grad_out, axis=0, keepdims=True),
    )


def extra_rows(*rows):
    width = rows[0].shape[1]
    return jnp.concatenate(list(rows) + [jnp.zeros((EXTRA - len(rows), width), F32)]).astype(BF)


def whole_matrix(pieces, plan, scratch):
    if len(pieces) == 1:
        return pieces[0][...]
    me = lax.axis_index("blk")
    rows, width = scratch.shape[1:]
    for piece, (sources, at) in zip(pieces, plan):
        for k, source in enumerate(sources):
            if len(piece.shape) == 3:
                scratch[me ^ source] = piece[k, :, at : at + width]
            else:
                scratch[me ^ source] = piece[k * rows : (k + 1) * rows, at : at + width]
    return scratch[...].reshape(-1, width)


def order(value, *after):
    return lax.optimization_barrier((value,) + after)[0]


def piece_scratch(pieces, width):
    if len(pieces) == 1:
        return pltpu.VMEM((8, 128), BF)
    return pltpu.VMEM((8, pieces[0].shape[-2], width), BF)


def places(tag_row, n, per_block, rows):
    target = tag_row // per_block
    onehot = lax.broadcasted_iota(jnp.int32, (n, rows), 0) == target
    earlier = lax.broadcasted_iota(jnp.int32, (rows, rows), 0) < lax.broadcasted_iota(
        jnp.int32, (rows, rows), 1
    )
    count = dot(onehot.astype(F32).astype(BF), earlier.astype(F32).astype(BF))
    rank = jnp.sum(jnp.where(onehot, count, 0.0), axis=0, keepdims=True).astype(jnp.int32)
    return target, rank


def fetch(sources, held, sems):
    copies = [
        pltpu.make_async_copy(source, to, sems.at[k])
        for k, (source, to) in enumerate(zip(sources, held))
    ]
    for copy in copies:
        copy.start()
    for copy in copies:
        copy.wait()


def pack_kernel(n, room, per_block, groups, *refs):
    count = 18
    sources, rest = refs[:count], refs[count:]
    held, sems = rest[-count - 1 : -1], rest[-1]
    *sends, attend_ref, ff_ref, vec_ref = rest[: -count - 1]
    fetch(sources, held, sems)
    for out, shards in ((attend_ref, held[:4]), (ff_ref, held[4:6])):
        at = 0
        for shard in shards:
            out[:, at : at + shard.shape[1]] = shard[...]
            at += shard.shape[1]
    x_ref, tag_ref, doc_ref, value_b, query_b, *vectors = held[6:]
    blank = jnp.zeros((1, value_b.shape[0]), F32)
    biases = [blank, value_b[...].reshape(1, -1), query_b[...].reshape(1, -1), blank]
    vec_ref[...] = jnp.concatenate(
        [jnp.concatenate(biases, axis=1)] + [item[...].reshape(1, -1) for item in vectors]
    )
    rows, width = x_ref.shape
    share = room // groups
    target, rank = places(tag_ref[...], n, per_block, rows)
    offset = rank - lax.axis_index("head") * share
    inside = (offset >= 0) & (offset < share)
    code = (1 + doc_ref[...] * per_block + tag_ref[...] % per_block).astype(F32)
    if len(sends) == 1:
        (out_ref,) = sends
        place = jnp.where(inside, target * share + offset, -1)
        pick = lax.broadcasted_iota(jnp.int32, (n * share, rows), 0) == place
        out_ref[:, :width] = dot(pick.astype(F32).astype(BF), x_ref[...]).astype(BF)
        code = jnp.sum(jnp.where(pick, code, 0.0), axis=1, keepdims=True)
        out_ref[:, width:] = jnp.broadcast_to(code, (n * share, META)).astype(BF)
        return
    odd = lax.axis_index("blk") % 2
    for t, out_ref in enumerate(sends):
        there = inside & (target % 2 == odd ^ t)
        place = jnp.where(there, target // 2 * share + offset, -1)
        pick = lax.broadcasted_iota(jnp.int32, (4 * share, rows), 0) == place
        out_ref[: 4 * share, :] = dot(pick.astype(F32).astype(BF), x_ref[...]).astype(BF)
        level = lax.broadcasted_iota(jnp.int32, (EXTRA, rows), 0)
        codes = jnp.where(there & (target // 2 == level), code, 0.0).astype(BF)
        spot = lax.broadcasted_iota(jnp.int32, (META, rows), 0) == offset
        tile = dot_last(codes, spot.astype(F32).astype(BF)).astype(BF)
        out_ref[4 * share :, :META] = tile
        out_ref[4 * share :, META:] = jnp.zeros((EXTRA, width - META), BF)


def route_kernel(keep_ref, recv_ref, *outs):
    level = lax.axis_index("blk") // 2
    rows, share = 0, (keep_ref.shape[0] - EXTRA) // 4
    width = keep_ref.shape[1]
    lanes = lax.broadcasted_iota(jnp.int32, (EXTRA, META), 0)
    for k in range(4):
        z = level ^ k
        for t, ref in enumerate((keep_ref, recv_ref)):
            outs[k][rows + t * share : rows + (t + 1) * share, :] = ref[pl.ds(z * share, share), :]
        first = keep_ref[4 * share :, :META].astype(F32)
        second = recv_ref[4 * share :, :META].astype(F32)
        first = jnp.sum(jnp.where(lanes == z, first, 0.0), axis=0, keepdims=True)
        second = jnp.sum(jnp.where(lanes == z, second, 0.0), axis=0, keepdims=True)
        tile = jnp.where(lanes == 0, first, jnp.where(lanes == 1, second, 0.0))
        outs[k][rows + 2 * share :, :META] = tile.astype(BF)
        outs[k][rows + 2 * share :, META:] = jnp.zeros((EXTRA, width - META), BF)


def stack_kernel(*refs):
    out_ref, at = refs[-1], 0
    for ref in refs[:-1]:
        if len(ref.shape) == 3:
            out_ref[at : at + ref.shape[0]] = ref[...]
            at += ref.shape[0]
        else:
            out_ref[at] = ref[...]
            at += 1


def stack(name, *parts):
    count = sum(1 if part.ndim == 2 else part.shape[0] for part in parts)
    (out,) = kernel_call(name, stack_kernel, [like((count,) + parts[0].shape[-2:])], parts)
    return out


def slots_kernel(*refs):
    out_ref = refs[4]
    share, width = (refs[0].shape[0] - EXTRA) // 2, refs[0].shape[1]
    lane = lax.broadcasted_iota(jnp.int32, (2 * share, META), 1)
    row = lax.broadcasted_iota(jnp.int32, (2 * share, META), 0)
    for k, ref in enumerate(refs[:4]):
        at = slice(2 * k * share, 2 * (k + 1) * share)
        out_ref[at, :width] = ref[: 2 * share, :]
        codes = ref[2 * share :, :META].astype(F32)
        spread = jnp.where(row < share, codes[:1, :], codes[1:2, :])
        code = jnp.sum(jnp.where(lane == row % share, spread, 0.0), axis=1, keepdims=True)
        out_ref[at, width:] = jnp.broadcast_to(code, (2 * share, META)).astype(BF)


def attend_kernel(per_block, count, plan, *refs):
    x_ref, tag_ref, doc_ref, bias_ref = refs[:4]
    parts = refs[4:8]
    pieces = refs[8 : 8 + count]
    mine_ref, theirs_ref, a_ref, q_ref, kv_ref, mask_ref, stat_ref, scratch, y_ref = refs[
        8 + count :
    ]
    rows, width = x_ref.shape
    local = a_ref.shape[1]
    slots = kv_ref.shape[0] - rows
    step = slots // 4
    me = lax.axis_index("blk")
    core = lax.axis_index("head") % 2
    weight = whole_matrix(pieces, plan, scratch)
    own = dot(x_ref[...], weight[:, : 3 * local]) + bias_ref[:1, : 3 * local]
    q_ref[...] = own[:, 2 * local :].astype(BF)
    kv_ref[slots:, :] = own[:, : 2 * local].astype(BF)
    row_cluster = lax.broadcasted_iota(jnp.int32, (1, rows), 1) // CLUSTER
    wanted = (1 + doc_ref[...] * per_block + row_cluster).astype(F32)
    for k in range(4):
        part = parts[k]
        kv_ref[k * step : (k + 1) * step, :] = (
            dot(part[:, :width], weight[:, : 2 * local]) + bias_ref[:1, : 2 * local]
        ).astype(BF)
        code = part[:, width : width + 1].astype(F32)
        mask_ref[k * step : (k + 1) * step, :] = jnp.where(code == wanted, 0.0, NEG).astype(BF)
    alone = tag_ref[...] != me * per_block + row_cluster
    diagonal = lax.broadcasted_iota(jnp.int32, (rows, rows), 0) == lax.broadcasted_iota(
        jnp.int32, (rows, rows), 1
    )
    mask_ref[slots:, :] = jnp.where(diagonal & alone, 0.0, NEG).astype(BF)
    mask = mask_ref[...].astype(F32)
    stats = []
    for j in range(local // DH):
        cut = slice(j * DH, (j + 1) * DH)
        scores = dot_last(kv_ref[:, cut], q_ref[:, cut]) * SCALE + mask
        top = jnp.max(scores, axis=0, keepdims=True)
        weights = jnp.exp(scores - top)
        inverse = 1.0 / jnp.sum(weights, axis=0, keepdims=True)
        probs = (weights * inverse).astype(BF)
        value = kv_ref[:, local + j * DH : local + (j + 1) * DH]
        a_ref[:, cut] = dot_first(probs, value).astype(BF)
        stats += [top, inverse]
    stat_ref[...] = jnp.concatenate(stats + [jnp.zeros((8 - len(stats), rows), F32)])
    y_ref[...] = dot_last(a_ref[...], weight[:, 3 * local :])
    half = rows // 2
    mine_ref[...] = y_ref[pl.ds(core * half, half), :]
    theirs_ref[...] = y_ref[pl.ds((1 - core) * half, half), :].astype(BF)


def attend_back_kernel(n, count, plan, *refs):
    own_ref, other_ref, q_ref, kv_ref, mask_ref, stat_ref = refs[:6]
    pieces = refs[6 : 6 + count]
    eb_ref, dq_ref, dkv_ref = refs[6 + count : 9 + count]
    back, scratch = refs[9 + count : -1], refs[-1]
    rows, local = q_ref.shape
    slots = kv_ref.shape[0] - rows
    half = rows // 2
    core = lax.axis_index("head") % 2
    weight = whole_matrix(pieces, plan, scratch)
    eb_ref[pl.ds(core * half, half), :] = own_ref[:half, :]
    eb_ref[pl.ds((1 - core) * half, half), :] = other_ref[:half, :]
    da = dot(eb_ref[...], weight[:, 3 * local :]).astype(BF)
    mask = mask_ref[...].astype(F32)
    for j in range(local // DH):
        cut = slice(j * DH, (j + 1) * DH)
        key, query = kv_ref[:, cut], q_ref[:, cut]
        value = kv_ref[:, local + j * DH : local + (j + 1) * DH]
        scores = dot_last(key, query) * SCALE + mask
        probs = jnp.exp(scores - stat_ref[2 * j : 2 * j + 1, :]) * stat_ref[
            2 * j + 1 : 2 * j + 2, :
        ]
        low = probs.astype(BF)
        dkv_ref[:, local + j * DH : local + (j + 1) * DH] = dot(low, da[:, cut]).astype(BF)
        grad = dot_last(value, da[:, cut])
        delta = jnp.sum(low.astype(F32) * grad, axis=0, keepdims=True)
        grad = (probs * (grad - delta)).astype(BF)
        dkv_ref[:, cut] = (dot(grad, query) * SCALE).astype(BF)
        dq_ref[:, cut] = (dot_first(grad, key) * SCALE).astype(BF)
    if back:
        share = slots // 4 // n
        for t in range(2):
            for z in range(4):
                for k in range(4):
                    at = k * slots // 4 + (2 * z + t) * share
                    to = (z * 4 + k) * share
                    back[t][to : to + share, :] = dkv_ref[at : at + share, :]


def back_kernel(room, left_ref, right_ref, keep_ref, send_ref):
    for k in range(left_ref.shape[0] // room):
        out, to = (send_ref if k % 2 else keep_ref), k // 2 * 2 * room
        out[to : to + room, :] = left_ref[k * room : (k + 1) * room, :]
        out[to + room : to + 2 * room, :] = right_ref[k * room : (k + 1) * room, :]


def token_kernel(n, room, per_block, parts, count, plan, *refs):
    tag_ref, dkv_ref, dq_ref = refs[:3]
    back = refs[3 : 3 + parts]
    pieces = refs[3 + parts : 3 + parts + count]
    mine_ref, theirs_ref, scratch, z_ref = refs[3 + parts + count :]
    rows, local = dq_ref.shape
    slots = n * room
    half = rows // 2
    share = room // 4
    group = lax.axis_index("head")
    core = group % 2
    weight = whole_matrix(pieces, plan, scratch)
    target, rank = places(tag_ref[...], n, per_block, rows)
    if parts > 1:
        target = target ^ lax.axis_index("blk")
    place = target * room + ((rank // share) ^ group) * share + rank % share
    total = dkv_ref[slots:, :].astype(F32)
    step = slots // parts
    for k in range(parts):
        pick = lax.broadcasted_iota(jnp.int32, (step, rows), 0) + k * step == place
        total = total + dot_first(pick.astype(F32).astype(BF), back[k][...])
    z_ref[...] = dot_last(total.astype(BF), weight[:, : 2 * local]) + dot_last(
        dq_ref[...], weight[:, 2 * local : 3 * local]
    )
    mine_ref[...] = z_ref[pl.ds(core * half, half), :]
    theirs_ref[...] = z_ref[pl.ds((1 - core) * half, half), :].astype(BF)


def norm_one_kernel(
    chip_ref, recv_ref, x_ref, vec_ref, h_ref, n_ref, r_ref, hb_ref
):
    half = chip_ref.shape[0]
    core = lax.axis_index("head") % 2
    branch = chip_ref[...].astype(F32) + recv_ref[...].astype(F32) + vec_ref[1:2, :]
    value = x_ref[pl.ds(core * half, half), :].astype(F32) + branch
    h, normal, inverse = norm_forward(value, vec_ref[2:3, :], vec_ref[3:4, :])
    h_ref[...] = h
    n_ref[...] = normal
    r_ref[...] = inverse
    hb_ref[...] = h.astype(BF)


def norm_two_kernel(
    chip_ref, recv_ref, h_ref, vec_ref, c_ref, out_ref, e_ref, eb_ref
):
    half = chip_ref.shape[0]
    core = lax.axis_index("head") % 2
    outer = chip_ref[...].astype(F32) + recv_ref[...].astype(F32) + vec_ref[4:5, :]
    gain_row = vec_ref[5:6, :]
    result, normal, inverse = norm_forward(h_ref[...] + outer, gain_row, vec_ref[6:7, :])
    out_ref[...] = result.astype(BF)
    cotangent = c_ref[pl.ds(core * half, half), :].astype(F32)
    grad, gain, shift = norm_backward(cotangent, normal, inverse, gain_row)
    e_ref[...] = grad
    eb_ref[:half, :] = grad.astype(BF)
    eb_ref[half:, :] = extra_rows(gain, shift)


def norm_back_kernel(chip_ref, recv_ref, e_ref, n_ref, r_ref, vec_ref, out_ref, eb_ref):
    half = chip_ref.shape[0]
    grad = e_ref[...] + (chip_ref[...].astype(F32) + recv_ref[...].astype(F32))
    grad, gain, shift = norm_backward(grad, n_ref[...], r_ref[...], vec_ref[2:3, :])
    out_ref[...] = grad
    eb_ref[:half, :] = grad.astype(BF)
    eb_ref[half:, :] = extra_rows(gain, shift)


def inner_kernel(count, plan, *refs):
    own_ref, other_ref, bias_ref = refs[:3]
    pieces = refs[3 : 3 + count]
    g_ref, slope_ref, scratch = refs[3 + count :]
    half = own_ref.shape[0]
    weight = whole_matrix(pieces, plan, scratch)
    for k, part in enumerate((own_ref, other_ref)):
        u = dot(part[...], weight) + bias_ref[7:8, :]
        below = 0.5 * (1.0 + lax.erf(u * math.sqrt(0.5)))
        g_ref[k * half : (k + 1) * half, :] = (u * below).astype(BF)
        density = jnp.exp(-0.5 * u * u) * (1.0 / math.sqrt(2.0 * math.pi))
        slope_ref[k * half : (k + 1) * half, :] = below + u * density


def outer_kernel(count, plan, *refs):
    g_ref = refs[0]
    pieces = refs[1 : 1 + count]
    mine_ref, theirs_ref, scratch = refs[1 + count :]
    half = mine_ref.shape[0]
    weight = whole_matrix(pieces, plan, scratch)
    mine_ref[...] = dot_last(g_ref[:half, :], weight)
    theirs_ref[...] = dot_last(g_ref[half:, :], weight).astype(BF)


def ff_back_kernel(outer_plan, inner_plan, outer_count, inner_count, *refs):
    own_ref, other_ref, slope_ref = refs[:3]
    outer, inner = refs[3 : 3 + outer_count], refs[3 + outer_count :][:inner_count]
    mine_ref, theirs_ref, du_ref, scratch, scratch_two = refs[3 + outer_count + inner_count :]
    half = mine_ref.shape[0]
    outer = whole_matrix(outer, outer_plan, scratch)
    inner = whole_matrix(inner, inner_plan, scratch_two)
    for k, part in ((1, other_ref), (0, own_ref)):
        rows = slice(k * half, (k + 1) * half)
        dg = dot(part[:half, :], outer).astype(BF).astype(F32)
        du_ref[rows, :] = (dg * slope_ref[rows, :]).astype(BF)
        dh = dot_last(du_ref[rows, :], inner)
        if k:
            theirs_ref[...] = dh.astype(BF)
        else:
            mine_ref[...] = dh


def halves(blocks, bit):
    return [b for b in blocks if not b & bit], [b for b in blocks if b & bit]


def split_pieces(total, bit, mine_ref, theirs_ref):
    me = lax.axis_index("blk")
    rows = total.shape[0] // 8
    for out, blocks in zip((mine_ref, theirs_ref), halves(range(8), bit)):
        for k, block in enumerate(blocks):
            out[k * rows : (k + 1) * rows, :] = total[pl.ds((me ^ block) * rows, rows), :].astype(BF)


def ff_weights_kernel(small, own_ref, other_ref, left_ref, *refs):
    half = left_ref.shape[0] // 2
    refs = list(refs)
    total = refs.pop()
    total[...] = dot_first(own_ref[:half, :], left_ref[:half, :]) + dot_first(
        other_ref[:half, :], left_ref[half:, :]
    )
    if small == "outer":
        small_ref = refs.pop()
        norms = own_ref[half:, :].astype(F32) + other_ref[half:, :].astype(F32)
        bias = jnp.sum(own_ref[:half, :].astype(F32), axis=0, keepdims=True) + jnp.sum(
            other_ref[:half, :].astype(F32), axis=0, keepdims=True
        )
        small_ref[...] = jnp.concatenate([norms[:2], bias, jnp.zeros((5, bias.shape[1]), F32)])
    else:
        small_ref = refs.pop()
        bias = jnp.sum(left_ref[...].astype(F32), axis=0, keepdims=True)
        small_ref[...] = jnp.concatenate([bias, jnp.zeros((7, bias.shape[1]), F32)])
    if len(refs) == 1:
        refs[0][...] = total[...]
    else:
        split_pieces(total, 1 if small == "outer" else 2, *refs)


def attend_weights_kernel(*refs):
    x_ref, p0, p1, p2, p3, dkv_ref, dq_ref, eb_ref, a_ref, own_ref, other_ref = refs[:11]
    outer_ref, inner_ref = refs[11:13]
    outs, total = list(refs[13:-1]), refs[-1]
    rows, width = x_ref.shape
    local = dq_ref.shape[1]
    slots = dkv_ref.shape[0] - rows
    step = slots // 4
    sums = dot_first(x_ref[...], dkv_ref[slots:, :])
    for k, part in enumerate((p0, p1, p2, p3)):
        sums = sums + dot_first(part[:, :width], dkv_ref[k * step : (k + 1) * step, :])
    total[:, : 2 * local] = sums
    total[:, 2 * local : 3 * local] = dot_first(x_ref[...], dq_ref[...])
    total[:, 3 * local :] = dot_first(eb_ref[...], a_ref[...])
    half = rows // 2
    norms = own_ref[half:, :].astype(F32) + other_ref[half:, :].astype(F32)
    output_b = jnp.sum(eb_ref[...].astype(F32), axis=0, keepdims=True)
    query_b = jnp.sum(dq_ref[...].astype(F32), axis=0, keepdims=True)
    value_b = jnp.sum(dkv_ref[...].astype(F32), axis=0, keepdims=True)
    last = jnp.concatenate([value_b, query_b, jnp.zeros((1, width - 3 * local), F32)], axis=1)
    small = jnp.concatenate(
        [
            outer_ref[:3, :],
            inner_ref[:1, :],
            norms[:2],
            output_b,
            last,
            jnp.zeros((EXTRA - 8, width), F32),
        ]
    )
    if outs[0].shape == total.shape:
        outs[0][...] = total[...]
        outs[1][...] = small
    else:
        split_pieces(total, 1, *outs)
        body = outs[0].shape[0] - EXTRA
        outs[0][body:, :] = small.astype(BF)
        outs[1][body:, :] = small.astype(BF)


def middle_kernel(extra, blocks, bit, mine_ref, recv_ref, *outs):
    rows = (mine_ref.shape[0] - extra) // len(blocks)
    last = mine_ref.shape[0] - extra
    for out, pieces in zip(outs, halves(blocks, bit)):
        for k, piece in enumerate(pieces):
            at = slice(blocks.index(piece) * rows, (blocks.index(piece) + 1) * rows)
            out[k * rows : (k + 1) * rows, :] = (
                mine_ref[at, :].astype(F32) + recv_ref[at, :].astype(F32)
            ).astype(BF)
        if extra:
            small = mine_ref[last:, :].astype(F32) + recv_ref[last:, :].astype(F32)
            out[len(pieces) * rows :, :] = small.astype(BF)


def last_kernel(left_ref, right_ref, *outs):
    total = left_ref[...].astype(F32) + right_ref[...].astype(F32)
    if len(outs) == 1:
        outs[0][...] = total
        return
    rows, local = outs[0].shape
    for k in range(4):
        outs[k][...] = total[:rows, k * local : (k + 1) * local]
    spread_small(total[rows:, :], local, outs[4:])


def spread_small(small, local, outs):
    for k, out in enumerate(outs[:7]):
        out[...] = small[k, :]
    outs[7][...] = small[7, 2 * local : 3 * local]
    outs[8][...] = small[7, local : 2 * local]


def small_kernel(small_ref, *outs):
    spread_small(small_ref[...], outs[7].shape[0], outs)


def scatter_step(name, mine, recv, blocks, bit, extra=0):
    rows = (mine.shape[0] - extra) // 2 + extra
    return kernel_call(
        name,
        functools.partial(middle_kernel, extra, blocks, bit),
        [like((rows, mine.shape[1]))] * 2,
        [mine, recv],
    )


def chip_sum(mine, theirs, name):
    chip = (mine + swap(theirs, "head", 1, name + "_chip").astype(F32)).astype(BF)
    return chip, swap(chip, "head", 2, name + "_x")


def per_device(
    hidden_in,
    query_w,
    key_w,
    value_w,
    output_w,
    inner_w,
    outer_w,
    query_b,
    value_b,
    output_b,
    inner_b,
    outer_b,
    first_gain,
    first_shift,
    second_gain,
    second_shift,
    key_cluster,
    document,
    cotangent,
):
    rows, width = hidden_in.shape
    n = lax.axis_size("blk")
    groups = lax.axis_size("head")
    assert groups == 4
    local = query_w.shape[1]
    units = inner_w.shape[1]
    per_block = rows // CLUSTER
    room = 2 * rows // n
    slots = n * room
    half = rows // 2
    share = room // groups
    staged = n == 8
    core = lax.axis_index("head") % 2

    tag_row, doc_row = key_cluster.reshape(1, rows), document.reshape(1, rows)

    if staged:
        sends = [like((4 * share + EXTRA, width))] * 2
    else:
        sends = [like((n * share, width + META))]
    pack_args = [key_w, value_w, query_w, output_w, inner_w, outer_w]
    pack_args += [hidden_in, tag_row, doc_row, value_b, query_b, output_b]
    pack_args += [first_gain, first_shift, outer_b, second_gain, second_shift, inner_b]
    *sent, attend_w, ff_w, vectors = kernel_call(
        "pack",
        functools.partial(pack_kernel, n, room, per_block, groups),
        sends
        + [
            like((width // n, 4 * local)),
            like((width // n, 2 * units)),
            like((8, width), F32),
        ],
        [pltpu.with_memory_space_constraint(item, pltpu.HBM) for item in pack_args],
        [pltpu.VMEM(item.shape, item.dtype) for item in pack_args]
        + [pltpu.SemaphoreType.DMA((len(pack_args),))],
        flops=2 * n * share * rows * width,
        space=pltpu.HBM,
    )
    if staged:
        attend_column = [
            swap(attend_w, "blk", bits, f"attend_w_z{bits}") for bits in (2, 4, 6)
        ]
        slots_y = swap(sent[1], "blk", 1, "slots_y")
        messages = kernel_call(
            "route", route_kernel, [like((2 * share + EXTRA, width))] * 4, [sent[0], slots_y]
        )
        arrived = [messages[0]] + [
            swap(messages[k], "blk", 2 * k, f"slots_z{2 * k}") for k in (1, 2, 3)
        ]
        (moved,) = kernel_call("slots", slots_kernel, [like((n * share, width + META))], arrived)
        column = order(attend_column, messages[0])
        column = stack("attend_w_column", attend_w, *column)
        rest = swap(column, "blk", 1, "attend_w_rest")
        attend_p = [attend_w] + attend_column + [rest]
        inner_far = swap(order(inner_w, *attend_column), "blk", 4, "inner_w_far")
        inner_near = swap(stack("inner_w_pair", inner_w, inner_far), "blk", 2, "inner_w_near")
        outer_far = swap(order(outer_w, inner_far), "blk", 4, "outer_w_far")
    else:
        moved = lax.all_to_all(sent[0].reshape(n, share, width + META), "blk", 0, 0)
        moved = moved.reshape(sent[0].shape)
        gather = lambda value: [lax.all_gather(value, "blk", axis=0, tiled=True)]
        attend_p, inner_p, outer_p = gather(attend_w), gather(inner_w), gather(outer_w)
    far = swap(moved, "head", 2, "slots_x")
    parts = [moved, swap(moved, "head", 1, "slots_chip"), far, swap(far, "head", 1, "slots_far")]
    attend_plan = [((0,), 0), ((2,), 0), ((4,), 0), ((6,), 0), ((1, 3, 5, 7), 0)]
    inner_plan = [((0,), 0), ((1,), 0), ((4,), 0), ((2, 6), 0), ((5, 3, 7), 0)]
    outer_plan = [((0,), 0), ((1,), units), ((4,), 0), ((2, 6), 0), ((5, 3, 7), 0)]

    count = len(attend_p)
    mine, theirs, a, q, kv, mask, stat = kernel_call(
        "attend",
        functools.partial(attend_kernel, per_block, count, attend_plan),
        [
            like((half, width), F32),
            like((half, width)),
            like((rows, local)),
            like((rows, local)),
            like((slots + rows, 2 * local)),
            like((slots + rows, rows)),
            like((8, rows), F32),
        ],
        [hidden_in, tag_row, doc_row, vectors] + parts + attend_p,
        [piece_scratch(attend_p, 4 * local), pltpu.VMEM((rows, width), F32)],
        flops=2 * rows * width * local * 9,
    )
    if staged:
        facing = swap(order(ff_w, far), "blk", 1, "facing_w")
        outer_far = order(outer_far, theirs)
        outer_near = swap(stack("outer_w_pair", outer_w, outer_far), "blk", 2, "outer_w_near")
        inner_rest = stack("inner_w_column", inner_far, inner_near)
        inner_rest = swap(inner_rest, "blk", 1, "inner_w_rest")
        outer_rest = stack("outer_w_column", outer_far, outer_near)
        outer_rest = swap(outer_rest, "blk", 1, "outer_w_rest")
        inner_p = [inner_w, facing, inner_far, inner_near, inner_rest]
        outer_p = [outer_w, facing, outer_far, outer_near, outer_rest]
        mine = order(mine, facing, outer_far)
    chip, recv = chip_sum(mine, theirs, "branch")
    if staged:
        recv = order(recv, outer_near)
    h, normal_one, inv_one, hb = kernel_call(
        "norm_one",
        norm_one_kernel,
        [
            like((half, width), F32),
            like((half, width), F32),
            like((half, 1), F32),
            like((half, width)),
        ],
        [chip, recv, hidden_in, vectors],
    )
    hb_other = swap(hb, "head", 1, "hb")

    g, slope = kernel_call(
        "inner",
        functools.partial(inner_kernel, len(inner_p), inner_plan),
        [like((rows, units)), like((rows, units), F32)],
        [hb, hb_other, vectors] + inner_p,
        [piece_scratch(inner_p, units)],
        flops=2 * rows * width * units,
    )
    mine, theirs = kernel_call(
        "outer",
        functools.partial(outer_kernel, len(outer_p), outer_plan),
        [like((half, width), F32), like((half, width))],
        [g] + outer_p,
        [piece_scratch(outer_p, units)],
        flops=2 * rows * width * units,
    )
    chip, recv = chip_sum(mine, theirs, "ff")
    result, e_two, eb_two = kernel_call(
        "norm_two",
        norm_two_kernel,
        [like((half, width)), like((half, width), F32), like((half + EXTRA, width))],
        [chip, recv, h, vectors, cotangent],
    )
    eb_two_other = swap(eb_two, "head", 1, "eb_two")
    mine, theirs, du = kernel_call(
        "ff_back",
        functools.partial(
            ff_back_kernel, outer_plan, inner_plan, len(outer_p), len(inner_p)
        ),
        [like((half, width), F32), like((half, width)), like((rows, units))],
        [eb_two, eb_two_other, slope] + outer_p + inner_p,
        [piece_scratch(outer_p, units), piece_scratch(inner_p, units)],
        flops=4 * rows * width * units,
    )
    if staged:
        grad_outs = [like((width // 2, units)), like((width // 2, units))]
    else:
        grad_outs = [like((width, units), F32)]
    outer_g = kernel_call(
        "outer_grad",
        functools.partial(ff_weights_kernel, "outer"),
        grad_outs + [like((8, width), F32)],
        [eb_two, eb_two_other, g],
        [pltpu.VMEM((width, units), F32)],
        flops=2 * rows * width * units,
    )
    mine = order(mine, outer_g[0])
    chip, recv = chip_sum(mine, theirs, "ff_back")
    inner_g = kernel_call(
        "inner_grad",
        functools.partial(ff_weights_kernel, "inner"),
        grad_outs + [like((8, units), F32)],
        [hb, hb_other, du],
        [pltpu.VMEM((width, units), F32)],
        flops=2 * rows * width * units,
    )
    recv = order(recv, outer_g[0], inner_g[0])
    grad_units = [like((width // n, units), F32)]
    if staged:
        outer_y = swap(outer_g[1], "blk", 1, "outer_g_y")
        inner_near = swap(inner_g[1], "blk", 2, "inner_g_near")
    else:
        grad_outer_w = lax.psum_scatter(outer_g[0], "blk", scatter_dimension=0, tiled=True)
        grad_inner_w = lax.psum_scatter(inner_g[0], "blk", scatter_dimension=0, tiled=True)

    e_one, eb_one = kernel_call(
        "norm_back",
        norm_back_kernel,
        [like((half, width), F32), like((half + EXTRA, width))],
        [chip, recv, e_two, normal_one, inv_one, vectors],
    )
    eb_one_other = swap(eb_one, "head", 1, "eb_one")
    back_outs = [like((slots // 2, 2 * local))] * 2 if staged else []
    eb_full, dq, dkv, *back = kernel_call(
        "attend_back",
        functools.partial(attend_back_kernel, n, count, attend_plan),
        [
            like((rows, width)),
            like((rows, local)),
            like((slots + rows, 2 * local)),
        ]
        + back_outs,
        [eb_one, eb_one_other, q, kv, mask, stat] + attend_p,
        [piece_scratch(attend_p, 4 * local)],
        flops=2 * rows * width * local * 8,
    )
    if staged:
        back_y = swap(back[1], "blk", 1, "back_y")
        outer_k, outer_s = scatter_step("outer_g_one", outer_g[0], outer_y, [0, 2, 4, 6], 2)
        inner_near = order(inner_near, outer_k)
        inner_k, inner_s = scatter_step("inner_g_one", inner_g[0], inner_near, [0, 1, 4, 5], 1)
        dq = order(dq, inner_k, outer_k)
        grad_outs = [like((width // 2 + EXTRA, width))] * 2
    else:
        grad_outs = [like((width, width), F32), like((EXTRA, width), F32)]
    attend_g = kernel_call(
        "attend_grad",
        attend_weights_kernel,
        grad_outs,
        [hidden_in] + parts + [dkv, dq, eb_full, a, eb_one, eb_one_other, outer_g[-1], inner_g[-1]],
        [pltpu.VMEM((width, width), F32)],
        flops=2 * rows * width * local * 8,
    )
    if staged:
        back_y = order(back_y, attend_g[1])
        attend_y = swap(order(attend_g[1], back_y), "blk", 1, "attend_g_y")
        half_slots = [like((slots // 2, 2 * local))] * 2
        back_k, back_s = kernel_call(
            "back_one", functools.partial(back_kernel, room), half_slots, [back[0], back_y]
        )
        back_near = swap(back_s, "blk", 2, "back_near")
        outer_near = swap(order(outer_s, back_near), "blk", 2, "outer_g_near")
        inner_y = swap(inner_s, "blk", 1, "inner_g_y")
        back_k, back_s = kernel_call(
            "back_two", functools.partial(back_kernel, 2 * room), half_slots, [back_k, back_near]
        )
        moved = [back_k, swap(back_s, "blk", 4, "back_far")]
        outer_k, outer_s = scatter_step("outer_g_two", outer_k, outer_near, [0, 4], 4)
        attend_k, attend_s = scatter_step(
            "attend_g_one", attend_g[0], attend_y, [0, 2, 4, 6], 2, EXTRA
        )
        inner_k, inner_s = scatter_step("inner_g_two", inner_k, inner_y, [0, 4], 4)
        inner_last = swap(inner_s, "blk", 4, "inner_g_far")
        moved[0] = order(moved[0], outer_k, attend_k, inner_k)
        outer_far = swap(order(outer_s, moved[1]), "blk", 4, "outer_g_far")
        (grad_outer_w,) = kernel_call(
            "outer_g_last", last_kernel, grad_units, [outer_k, outer_far]
        )
        (grad_inner_w,) = kernel_call(
            "inner_g_last", last_kernel, grad_units, [inner_k, inner_last]
        )
    else:
        moved = dkv[:slots].reshape(4, n, share, 2 * local).transpose(1, 0, 2, 3)
        moved = lax.all_to_all(moved, "blk", 0, 0).reshape(slots, 2 * local)
        moved = [moved]
    mine, theirs = kernel_call(
        "token",
        functools.partial(
            token_kernel, n, room, per_block, len(moved), count, attend_plan
        ),
        [like((half, width), F32), like((half, width))],
        [tag_row, dkv, dq] + moved + attend_p,
        [piece_scratch(attend_p, 4 * local), pltpu.VMEM((rows, width), F32)],
        flops=2 * rows * width * local * 4,
    )
    chip, recv = chip_sum(mine, theirs, "last")
    if staged:
        attend_near = swap(attend_s, "blk", 2, "attend_g_near")
        attend_k, attend_s = scatter_step(
            "attend_g_two", attend_k, attend_near, [0, 4], 4, EXTRA
        )
        recv = order(recv, attend_k, grad_outer_w)
    last = e_one + (chip.astype(F32) + recv.astype(F32))
    last_other = swap(last, "head", 1, "last")
    result_other = swap(result, "head", 1, "result")

    def joined(own, other):
        return jnp.where(
            core == 0, jnp.concatenate([own, other]), jnp.concatenate([other, own])
        )

    layer_out = joined(result, result_other)
    if staged:
        last_other = order(last_other, grad_inner_w, grad_outer_w)
    grad_input = joined(last, last_other)
    small_outs = [like((width,), F32)] * 7 + [like((local,), F32)] * 2
    if staged:
        attend_far = swap(attend_s, "blk", 4, "attend_g_far")
        attend_far = order(attend_far, grad_input, layer_out)
        grads = kernel_call(
            "attend_g_last",
            last_kernel,
            [like((width // n, local), F32)] * 4 + small_outs,
            [attend_k, attend_far],
        )
        grads, small = grads[:4], grads[4:]
    else:
        summed = lax.psum_scatter(attend_g[0], "blk", scatter_dimension=0, tiled=True)
        grads = [summed[:, k * local : (k + 1) * local] for k in range(4)]
        small = kernel_call("small", small_kernel, small_outs, [lax.psum(attend_g[1], "blk")])
    grad_key_w, grad_value_w, grad_query_w, grad_output_w = grads

    return (
        layer_out,
        grad_input,
        grad_query_w,
        grad_key_w,
        grad_value_w,
        grad_output_w,
        grad_inner_w,
        grad_outer_w,
        small[7],
        small[8],
        small[6],
        small[3],
        small[2],
        small[4],
        small[5],
        small[0],
        small[1],
    )


def solution(mesh):
    matrix = P("blk", "head")
    in_specs = (
        (P("blk", None),)
        + (matrix,) * 6
        + (P("head"), P("head"), P(), P("head"))
        + (P(),) * 5
        + (P("blk"), P("blk"), P("blk", None))
    )
    out_specs = (
        (P("blk", None), P("blk", None))
        + (matrix,) * 6
        + (P("head"), P("head"), P(), P("head"))
        + (P(),) * 5
    )
    return jax.shard_map(
        per_device, mesh=mesh, in_specs=in_specs, out_specs=out_specs, check_vma=False
    )
```

```python
import functools
import math

import jax
import jax.numpy as jnp
from jax import lax
from jax.experimental import pallas as pl
from jax.experimental.pallas import tpu as pltpu
from jax.sharding import PartitionSpec as P

DH = 64
CLUSTER = 128
EPS = 1e-06
NEG = -1e30
SCALE = 1.0 / math.sqrt(DH)
META = 128
EXTRA = 16
VMEM = 16 << 20
BF = jnp.bfloat16
F32 = jnp.float32


def swap(value, axis, bits, name):
    with jax.named_scope(name):
        return lax.ppermute(value, axis, [(i, i ^ bits) for i in range(lax.axis_size(axis))])


def dot(left, right):
    return jnp.dot(left, right, preferred_element_type=F32)


def dot_last(left, right):
    return lax.dot_general(left, right, (((1,), (1,)), ((), ())), preferred_element_type=F32)


def dot_first(left, right):
    return lax.dot_general(left, right, (((0,), (0,)), ((), ())), preferred_element_type=F32)


def kernel_call(name, body, outs, args, scratch=(), flops=0, space=pltpu.VMEM):
    size = sum(math.prod(a.shape) * a.dtype.itemsize for a in list(args) + list(outs))
    whole = pl.BlockSpec(memory_space=pltpu.VMEM)
    return pl.pallas_call(
        body,
        out_shape=tuple(outs),
        in_specs=[pl.BlockSpec(memory_space=space)] * len(args),
        out_specs=tuple([whole] * len(outs)),
        scratch_shapes=list(scratch),
        name=name,
        compiler_params=pltpu.CompilerParams(vmem_limit_bytes=VMEM),
        cost_estimate=pl.CostEstimate(flops=flops, bytes_accessed=size, transcendentals=0),
    )(*args)


def like(shape, dtype=BF):
    return jax.ShapeDtypeStruct(shape, dtype)


def norm_forward(value, gain, shift):
    centered = value - jnp.mean(value, axis=-1, keepdims=True)
    variance = jnp.mean(centered * centered, axis=-1, keepdims=True)
    inv_std = lax.rsqrt(variance + EPS)
    normal_part = centered * inv_std
    return (normal_part * gain + shift, normal_part, inv_std)


def norm_backward(grad_out, normal_part, inv_std, gain):
    scaled = grad_out * gain
    mean_one = jnp.mean(scaled, axis=-1, keepdims=True)
    mean_two = jnp.mean(scaled * normal_part, axis=-1, keepdims=True)
    grad_in = inv_std * (scaled - mean_one - normal_part * mean_two)
    return (
        grad_in,
        jnp.sum(grad_out * normal_part, axis=0, keepdims=True),
        jnp.sum(grad_out, axis=0, keepdims=True),
    )


def extra_rows(*rows):
    width = rows[0].shape[1]
    return jnp.concatenate(list(rows) + [jnp.zeros((EXTRA - len(rows), width), F32)]).astype(BF)


def whole_matrix(pieces, plan, scratch):
    if len(pieces) == 1:
        return pieces[0][...]
    me = lax.axis_index("blk")
    rows, width = scratch.shape[1:]
    for piece, (sources, at) in zip(pieces, plan):
        for k, source in enumerate(sources):
            if len(piece.shape) == 3:
                scratch[me ^ source] = piece[k, :, at : at + width]
            else:
                scratch[me ^ source] = piece[k * rows : (k + 1) * rows, at : at + width]
    return scratch[...].reshape(-1, width)


def order(value, *after):
    return lax.optimization_barrier((value,) + after)[0]


def piece_scratch(pieces, width):
    if len(pieces) == 1:
        return pltpu.VMEM((8, 128), BF)
    return pltpu.VMEM((8, pieces[0].shape[-2], width), BF)


def places(tag_row, n, per_block, rows):
    target = tag_row // per_block
    onehot = lax.broadcasted_iota(jnp.int32, (n, rows), 0) == target
    earlier = lax.broadcasted_iota(jnp.int32, (rows, rows), 0) < lax.broadcasted_iota(
        jnp.int32, (rows, rows), 1
    )
    count = dot(onehot.astype(F32).astype(BF), earlier.astype(F32).astype(BF))
    rank = jnp.sum(jnp.where(onehot, count, 0.0), axis=0, keepdims=True).astype(jnp.int32)
    return target, rank


def fetch(sources, held, sems):
    copies = [
        pltpu.make_async_copy(source, to, sems.at[k])
        for k, (source, to) in enumerate(zip(sources, held))
    ]
    for copy in copies:
        copy.start()
    for copy in copies:
        copy.wait()


def pack_kernel(n, room, per_block, groups, *refs):
    count = 18
    sources, rest = refs[:count], refs[count:]
    held, sems = rest[-count - 1 : -1], rest[-1]
    *sends, attend_ref, ff_ref, vec_ref = rest[: -count - 1]
    fetch(sources, held, sems)
    for out, shards in ((attend_ref, held[:4]), (ff_ref, held[4:6])):
        at = 0
        for shard in shards:
            out[:, at : at + shard.shape[1]] = shard[...]
            at += shard.shape[1]
    x_ref, tag_ref, doc_ref, value_b, query_b, *vectors = held[6:]
    blank = jnp.zeros((1, value_b.shape[0]), F32)
    biases = [blank, value_b[...].reshape(1, -1), query_b[...].reshape(1, -1), blank]
    vec_ref[...] = jnp.concatenate(
        [jnp.concatenate(biases, axis=1)] + [item[...].reshape(1, -1) for item in vectors]
    )
    rows, width = x_ref.shape
    share = room // groups
    target, rank = places(tag_ref[...], n, per_block, rows)
    offset = rank - lax.axis_index("head") * share
    inside = (offset >= 0) & (offset < share)
    code = (1 + doc_ref[...] * per_block + tag_ref[...] % per_block).astype(F32)
    if len(sends) == 1:
        (out_ref,) = sends
        place = jnp.where(inside, target * share + offset, -1)
        pick = lax.broadcasted_iota(jnp.int32, (n * share, rows), 0) == place
        out_ref[:, :width] = dot(pick.astype(F32).astype(BF), x_ref[...]).astype(BF)
        code = jnp.sum(jnp.where(pick, code, 0.0), axis=1, keepdims=True)
        out_ref[:, width:] = jnp.broadcast_to(code, (n * share, META)).astype(BF)
        return
    odd = lax.axis_index("blk") % 2
    for t, out_ref in enumerate(sends):
        there = inside & (target % 2 == odd ^ t)
        place = jnp.where(there, target // 2 * share + offset, -1)
        pick = lax.broadcasted_iota(jnp.int32, (4 * share, rows), 0) == place
        out_ref[: 4 * share, :] = dot(pick.astype(F32).astype(BF), x_ref[...]).astype(BF)
        level = lax.broadcasted_iota(jnp.int32, (EXTRA, rows), 0)
        codes = jnp.where(there & (target // 2 == level), code, 0.0).astype(BF)
        spot = lax.broadcasted_iota(jnp.int32, (META, rows), 0) == offset
        tile = dot_last(codes, spot.astype(F32).astype(BF)).astype(BF)
        out_ref[4 * share :, :META] = tile
        out_ref[4 * share :, META:] = jnp.zeros((EXTRA, width - META), BF)


def route_kernel(keep_ref, recv_ref, *outs):
    level = lax.axis_index("blk") // 2
    rows, share = 0, (keep_ref.shape[0] - EXTRA) // 4
    width = keep_ref.shape[1]
    lanes = lax.broadcasted_iota(jnp.int32, (EXTRA, META), 0)
    for k in range(4):
        z = level ^ k
        for t, ref in enumerate((keep_ref, recv_ref)):
            outs[k][rows + t * share : rows + (t + 1) * share, :] = ref[pl.ds(z * share, share), :]
        first = keep_ref[4 * share :, :META].astype(F32)
        second = recv_ref[4 * share :, :META].astype(F32)
        first = jnp.sum(jnp.where(lanes == z, first, 0.0), axis=0, keepdims=True)
        second = jnp.sum(jnp.where(lanes == z, second, 0.0), axis=0, keepdims=True)
        tile = jnp.where(lanes == 0, first, jnp.where(lanes == 1, second, 0.0))
        outs[k][rows + 2 * share :, :META] = tile.astype(BF)
        outs[k][rows + 2 * share :, META:] = jnp.zeros((EXTRA, width - META), BF)


def stack_kernel(*refs):
    out_ref, at = refs[-1], 0
    for ref in refs[:-1]:
        if len(ref.shape) == 3:
            out_ref[at : at + ref.shape[0]] = ref[...]
            at += ref.shape[0]
        else:
            out_ref[at] = ref[...]
            at += 1


def stack(name, *parts):
    count = sum(1 if part.ndim == 2 else part.shape[0] for part in parts)
    (out,) = kernel_call(name, stack_kernel, [like((count,) + parts[0].shape[-2:])], parts)
    return out


def slots_kernel(*refs):
    out_ref = refs[4]
    share, width = (refs[0].shape[0] - EXTRA) // 2, refs[0].shape[1]
    lane = lax.broadcasted_iota(jnp.int32, (2 * share, META), 1)
    row = lax.broadcasted_iota(jnp.int32, (2 * share, META), 0)
    for k, ref in enumerate(refs[:4]):
        at = slice(2 * k * share, 2 * (k + 1) * share)
        out_ref[at, :width] = ref[: 2 * share, :]
        codes = ref[2 * share :, :META].astype(F32)
        spread = jnp.where(row < share, codes[:1, :], codes[1:2, :])
        code = jnp.sum(jnp.where(lane == row % share, spread, 0.0), axis=1, keepdims=True)
        out_ref[at, width:] = jnp.broadcast_to(code, (2 * share, META)).astype(BF)


def attend_kernel(per_block, count, plan, *refs):
    x_ref, tag_ref, doc_ref, bias_ref = refs[:4]
    parts = refs[4:8]
    pieces = refs[8 : 8 + count]
    mine_ref, theirs_ref, a_ref, q_ref, kv_ref, mask_ref, stat_ref, scratch, y_ref = refs[
        8 + count :
    ]
    rows, width = x_ref.shape
    local = a_ref.shape[1]
    slots = kv_ref.shape[0] - rows
    step = slots // 4
    me = lax.axis_index("blk")
    core = lax.axis_index("head") % 2
    weight = whole_matrix(pieces, plan, scratch)
    own = dot(x_ref[...], weight[:, : 3 * local]) + bias_ref[:1, : 3 * local]
    q_ref[...] = own[:, 2 * local :].astype(BF)
    kv_ref[slots:, :] = own[:, : 2 * local].astype(BF)
    row_cluster = lax.broadcasted_iota(jnp.int32, (1, rows), 1) // CLUSTER
    wanted = (1 + doc_ref[...] * per_block + row_cluster).astype(F32)
    for k in range(4):
        part = parts[k]
        kv_ref[k * step : (k + 1) * step, :] = (
            dot(part[:, :width], weight[:, : 2 * local]) + bias_ref[:1, : 2 * local]
        ).astype(BF)
        code = part[:, width : width + 1].astype(F32)
        mask_ref[k * step : (k + 1) * step, :] = jnp.where(code == wanted, 0.0, NEG).astype(BF)
    alone = tag_ref[...] != me * per_block + row_cluster
    diagonal = lax.broadcasted_iota(jnp.int32, (rows, rows), 0) == lax.broadcasted_iota(
        jnp.int32, (rows, rows), 1
    )
    mask_ref[slots:, :] = jnp.where(diagonal & alone, 0.0, NEG).astype(BF)
    mask = mask_ref[...].astype(F32)
    stats = []
    for j in range(local // DH):
        cut = slice(j * DH, (j + 1) * DH)
        scores = dot_last(kv_ref[:, cut], q_ref[:, cut]) * SCALE + mask
        top = jnp.max(scores, axis=0, keepdims=True)
        weights = jnp.exp(scores - top)
        inverse = 1.0 / jnp.sum(weights, axis=0, keepdims=True)
        probs = (weights * inverse).astype(BF)
        value = kv_ref[:, local + j * DH : local + (j + 1) * DH]
        a_ref[:, cut] = dot_first(probs, value).astype(BF)
        stats += [top, inverse]
    stat_ref[...] = jnp.concatenate(stats + [jnp.zeros((8 - len(stats), rows), F32)])
    y_ref[...] = dot_last(a_ref[...], weight[:, 3 * local :])
    half = rows // 2
    mine_ref[...] = y_ref[pl.ds(core * half, half), :]
    theirs_ref[...] = y_ref[pl.ds((1 - core) * half, half), :].astype(BF)


def attend_back_kernel(n, count, plan, *refs):
    own_ref, other_ref, q_ref, kv_ref, mask_ref, stat_ref = refs[:6]
    pieces = refs[6 : 6 + count]
    eb_ref, dq_ref, dkv_ref = refs[6 + count : 9 + count]
    back, scratch = refs[9 + count : -1], refs[-1]
    rows, local = q_ref.shape
    slots = kv_ref.shape[0] - rows
    half = rows // 2
    core = lax.axis_index("head") % 2
    weight = whole_matrix(pieces, plan, scratch)
    eb_ref[pl.ds(core * half, half), :] = own_ref[:half, :]
    eb_ref[pl.ds((1 - core) * half, half), :] = other_ref[:half, :]
    da = dot(eb_ref[...], weight[:, 3 * local :]).astype(BF)
    mask = mask_ref[...].astype(F32)
    for j in range(local // DH):
        cut = slice(j * DH, (j + 1) * DH)
        key, query = kv_ref[:, cut], q_ref[:, cut]
        value = kv_ref[:, local + j * DH : local + (j + 1) * DH]
        scores = dot_last(key, query) * SCALE + mask
        probs = jnp.exp(scores - stat_ref[2 * j : 2 * j + 1, :]) * stat_ref[
            2 * j + 1 : 2 * j + 2, :
        ]
        low = probs.astype(BF)
        dkv_ref[:, local + j * DH : local + (j + 1) * DH] = dot(low, da[:, cut]).astype(BF)
        grad = dot_last(value, da[:, cut])
        delta = jnp.sum(low.astype(F32) * grad, axis=0, keepdims=True)
        grad = (probs * (grad - delta)).astype(BF)
        dkv_ref[:, cut] = (dot(grad, query) * SCALE).astype(BF)
        dq_ref[:, cut] = (dot_first(grad, key) * SCALE).astype(BF)
    if back:
        share = slots // 4 // n
        for t in range(2):
            for z in range(4):
                for k in range(4):
                    at = k * slots // 4 + (2 * z + t) * share
                    to = (z * 4 + k) * share
                    back[t][to : to + share, :] = dkv_ref[at : at + share, :]


def back_kernel(room, left_ref, right_ref, keep_ref, send_ref):
    for k in range(left_ref.shape[0] // room):
        out, to = (send_ref if k % 2 else keep_ref), k // 2 * 2 * room
        out[to : to + room, :] = left_ref[k * room : (k + 1) * room, :]
        out[to + room : to + 2 * room, :] = right_ref[k * room : (k + 1) * room, :]


def token_kernel(n, room, per_block, parts, count, plan, *refs):
    tag_ref, dkv_ref, dq_ref = refs[:3]
    back = refs[3 : 3 + parts]
    pieces = refs[3 + parts : 3 + parts + count]
    mine_ref, theirs_ref, scratch, z_ref = refs[3 + parts + count :]
    rows, local = dq_ref.shape
    slots = n * room
    half = rows // 2
    share = room // 4
    group = lax.axis_index("head")
    core = group % 2
    weight = whole_matrix(pieces, plan, scratch)
    target, rank = places(tag_ref[...], n, per_block, rows)
    if parts > 1:
        target = target ^ lax.axis_index("blk")
    place = target * room + ((rank // share) ^ group) * share + rank % share
    total = dkv_ref[slots:, :].astype(F32)
    step = slots // parts
    for k in range(parts):
        pick = lax.broadcasted_iota(jnp.int32, (step, rows), 0) + k * step == place
        total = total + dot_first(pick.astype(F32).astype(BF), back[k][...])
    z_ref[...] = dot_last(total.astype(BF), weight[:, : 2 * local]) + dot_last(
        dq_ref[...], weight[:, 2 * local : 3 * local]
    )
    mine_ref[...] = z_ref[pl.ds(core * half, half), :]
    theirs_ref[...] = z_ref[pl.ds((1 - core) * half, half), :].astype(BF)


def norm_one_kernel(
    chip_ref, recv_ref, x_ref, vec_ref, h_ref, n_ref, r_ref, hb_ref
):
    half = chip_ref.shape[0]
    core = lax.axis_index("head") % 2
    branch = chip_ref[...].astype(F32) + recv_ref[...].astype(F32) + vec_ref[1:2, :]
    value = x_ref[pl.ds(core * half, half), :].astype(F32) + branch
    h, normal, inverse = norm_forward(value, vec_ref[2:3, :], vec_ref[3:4, :])
    h_ref[...] = h
    n_ref[...] = normal
    r_ref[...] = inverse
    hb_ref[...] = h.astype(BF)


def norm_two_kernel(
    chip_ref, recv_ref, h_ref, vec_ref, c_ref, out_ref, e_ref, eb_ref
):
    half = chip_ref.shape[0]
    core = lax.axis_index("head") % 2
    outer = chip_ref[...].astype(F32) + recv_ref[...].astype(F32) + vec_ref[4:5, :]
    gain_row = vec_ref[5:6, :]
    result, normal, inverse = norm_forward(h_ref[...] + outer, gain_row, vec_ref[6:7, :])
    out_ref[...] = result.astype(BF)
    cotangent = c_ref[pl.ds(core * half, half), :].astype(F32)
    grad, gain, shift = norm_backward(cotangent, normal, inverse, gain_row)
    e_ref[...] = grad
    eb_ref[:half, :] = grad.astype(BF)
    eb_ref[half:, :] = extra_rows(gain, shift)


def norm_back_kernel(chip_ref, recv_ref, e_ref, n_ref, r_ref, vec_ref, out_ref, eb_ref):
    half = chip_ref.shape[0]
    grad = e_ref[...] + (chip_ref[...].astype(F32) + recv_ref[...].astype(F32))
    grad, gain, shift = norm_backward(grad, n_ref[...], r_ref[...], vec_ref[2:3, :])
    out_ref[...] = grad
    eb_ref[:half, :] = grad.astype(BF)
    eb_ref[half:, :] = extra_rows(gain, shift)


def inner_kernel(count, plan, *refs):
    own_ref, other_ref, bias_ref = refs[:3]
    pieces = refs[3 : 3 + count]
    g_ref, slope_ref, scratch = refs[3 + count :]
    half = own_ref.shape[0]
    weight = whole_matrix(pieces, plan, scratch)
    for k, part in enumerate((own_ref, other_ref)):
        u = dot(part[...], weight) + bias_ref[7:8, :]
        below = 0.5 * (1.0 + lax.erf(u * math.sqrt(0.5)))
        g_ref[k * half : (k + 1) * half, :] = (u * below).astype(BF)
        density = jnp.exp(-0.5 * u * u) * (1.0 / math.sqrt(2.0 * math.pi))
        slope_ref[k * half : (k + 1) * half, :] = below + u * density


def outer_kernel(count, plan, *refs):
    g_ref = refs[0]
    pieces = refs[1 : 1 + count]
    mine_ref, theirs_ref, scratch = refs[1 + count :]
    half = mine_ref.shape[0]
    weight = whole_matrix(pieces, plan, scratch)
    mine_ref[...] = dot_last(g_ref[:half, :], weight)
    theirs_ref[...] = dot_last(g_ref[half:, :], weight).astype(BF)


def ff_back_kernel(outer_plan, inner_plan, outer_count, inner_count, *refs):
    own_ref, other_ref, slope_ref = refs[:3]
    outer, inner = refs[3 : 3 + outer_count], refs[3 + outer_count :][:inner_count]
    mine_ref, theirs_ref, du_ref, scratch, scratch_two = refs[3 + outer_count + inner_count :]
    half = mine_ref.shape[0]
    outer = whole_matrix(outer, outer_plan, scratch)
    inner = whole_matrix(inner, inner_plan, scratch_two)
    for k, part in ((1, other_ref), (0, own_ref)):
        rows = slice(k * half, (k + 1) * half)
        dg = dot(part[:half, :], outer).astype(BF).astype(F32)
        du_ref[rows, :] = (dg * slope_ref[rows, :]).astype(BF)
        dh = dot_last(du_ref[rows, :], inner)
        if k:
            theirs_ref[...] = dh.astype(BF)
        else:
            mine_ref[...] = dh


def halves(blocks, bit):
    return [b for b in blocks if not b & bit], [b for b in blocks if b & bit]


def split_pieces(total, bit, mine_ref, theirs_ref):
    me = lax.axis_index("blk")
    rows = total.shape[0] // 8
    for out, blocks in zip((mine_ref, theirs_ref), halves(range(8), bit)):
        for k, block in enumerate(blocks):
            out[k * rows : (k + 1) * rows, :] = total[pl.ds((me ^ block) * rows, rows), :].astype(BF)


def ff_weights_kernel(small, own_ref, other_ref, left_ref, *refs):
    half = left_ref.shape[0] // 2
    refs = list(refs)
    total = refs.pop()
    total[...] = dot_first(own_ref[:half, :], left_ref[:half, :]) + dot_first(
        other_ref[:half, :], left_ref[half:, :]
    )
    if small == "outer":
        small_ref = refs.pop()
        norms = own_ref[half:, :].astype(F32) + other_ref[half:, :].astype(F32)
        bias = jnp.sum(own_ref[:half, :].astype(F32), axis=0, keepdims=True) + jnp.sum(
            other_ref[:half, :].astype(F32), axis=0, keepdims=True
        )
        small_ref[...] = jnp.concatenate([norms[:2], bias, jnp.zeros((5, bias.shape[1]), F32)])
    else:
        small_ref = refs.pop()
        bias = jnp.sum(left_ref[...].astype(F32), axis=0, keepdims=True)
        small_ref[...] = jnp.concatenate([bias, jnp.zeros((7, bias.shape[1]), F32)])
    if len(refs) == 1:
        refs[0][...] = total[...]
    else:
        split_pieces(total, 1 if small == "outer" else 2, *refs)


def attend_weights_kernel(*refs):
    x_ref, p0, p1, p2, p3, dkv_ref, dq_ref, eb_ref, a_ref, own_ref, other_ref = refs[:11]
    outer_ref, inner_ref = refs[11:13]
    outs, total = list(refs[13:-1]), refs[-1]
    rows, width = x_ref.shape
    local = dq_ref.shape[1]
    slots = dkv_ref.shape[0] - rows
    step = slots // 4
    sums = dot_first(x_ref[...], dkv_ref[slots:, :])
    for k, part in enumerate((p0, p1, p2, p3)):
        sums = sums + dot_first(part[:, :width], dkv_ref[k * step : (k + 1) * step, :])
    total[:, : 2 * local] = sums
    total[:, 2 * local : 3 * local] = dot_first(x_ref[...], dq_ref[...])
    total[:, 3 * local :] = dot_first(eb_ref[...], a_ref[...])
    half = rows // 2
    norms = own_ref[half:, :].astype(F32) + other_ref[half:, :].astype(F32)
    output_b = jnp.sum(eb_ref[...].astype(F32), axis=0, keepdims=True)
    query_b = jnp.sum(dq_ref[...].astype(F32), axis=0, keepdims=True)
    value_b = jnp.sum(dkv_ref[...].astype(F32), axis=0, keepdims=True)
    last = jnp.concatenate([value_b, query_b, jnp.zeros((1, width - 3 * local), F32)], axis=1)
    small = jnp.concatenate(
        [
            outer_ref[:3, :],
            inner_ref[:1, :],
            norms[:2],
            output_b,
            last,
            jnp.zeros((EXTRA - 8, width), F32),
        ]
    )
    if outs[0].shape == total.shape:
        outs[0][...] = total[...]
        outs[1][...] = small
    else:
        split_pieces(total, 1, *outs)
        body = outs[0].shape[0] - EXTRA
        outs[0][body:, :] = small.astype(BF)
        outs[1][body:, :] = small.astype(BF)


def middle_kernel(extra, blocks, bit, mine_ref, recv_ref, *outs):
    rows = (mine_ref.shape[0] - extra) // len(blocks)
    last = mine_ref.shape[0] - extra
    for out, pieces in zip(outs, halves(blocks, bit)):
        for k, piece in enumerate(pieces):
            at = slice(blocks.index(piece) * rows, (blocks.index(piece) + 1) * rows)
            out[k * rows : (k + 1) * rows, :] = (
                mine_ref[at, :].astype(F32) + recv_ref[at, :].astype(F32)
            ).astype(BF)
        if extra:
            small = mine_ref[last:, :].astype(F32) + recv_ref[last:, :].astype(F32)
            out[len(pieces) * rows :, :] = small.astype(BF)


def last_kernel(left_ref, right_ref, *outs):
    total = left_ref[...].astype(F32) + right_ref[...].astype(F32)
    if len(outs) == 1:
        outs[0][...] = total
        return
    rows, local = outs[0].shape
    for k in range(4):
        outs[k][...] = total[:rows, k * local : (k + 1) * local]
    spread_small(total[rows:, :], local, outs[4:])


def spread_small(small, local, outs):
    for k, out in enumerate(outs[:7]):
        out[...] = small[k, :]
    outs[7][...] = small[7, 2 * local : 3 * local]
    outs[8][...] = small[7, local : 2 * local]


def small_kernel(small_ref, *outs):
    spread_small(small_ref[...], outs[7].shape[0], outs)


def scatter_step(name, mine, recv, blocks, bit, extra=0):
    rows = (mine.shape[0] - extra) // 2 + extra
    return kernel_call(
        name,
        functools.partial(middle_kernel, extra, blocks, bit),
        [like((rows, mine.shape[1]))] * 2,
        [mine, recv],
    )


def chip_sum(mine, theirs, name):
    chip = (mine + swap(theirs, "head", 1, name + "_chip").astype(F32)).astype(BF)
    return chip, swap(chip, "head", 2, name + "_x")


def per_device(
    hidden_in,
    query_w,
    key_w,
    value_w,
    output_w,
    inner_w,
    outer_w,
    query_b,
    value_b,
    output_b,
    inner_b,
    outer_b,
    first_gain,
    first_shift,
    second_gain,
    second_shift,
    key_cluster,
    document,
    cotangent,
):
    rows, width = hidden_in.shape
    n = lax.axis_size("blk")
    groups = lax.axis_size("head")
    assert groups == 4
    local = query_w.shape[1]
    units = inner_w.shape[1]
    per_block = rows // CLUSTER
    room = 2 * rows // n
    slots = n * room
    half = rows // 2
    share = room // groups
    staged = n == 8
    core = lax.axis_index("head") % 2

    tag_row, doc_row = key_cluster.reshape(1, rows), document.reshape(1, rows)

    if staged:
        sends = [like((4 * share + EXTRA, width))] * 2
    else:
        sends = [like((n * share, width + META))]
    pack_args = [key_w, value_w, query_w, output_w, inner_w, outer_w]
    pack_args += [hidden_in, tag_row, doc_row, value_b, query_b, output_b]
    pack_args += [first_gain, first_shift, outer_b, second_gain, second_shift, inner_b]
    *sent, attend_w, ff_w, vectors = kernel_call(
        "pack",
        functools.partial(pack_kernel, n, room, per_block, groups),
        sends
        + [
            like((width // n, 4 * local)),
            like((width // n, 2 * units)),
            like((8, width), F32),
        ],
        [pltpu.with_memory_space_constraint(item, pltpu.HBM) for item in pack_args],
        [pltpu.VMEM(item.shape, item.dtype) for item in pack_args]
        + [pltpu.SemaphoreType.DMA((len(pack_args),))],
        flops=2 * n * share * rows * width,
        space=pltpu.HBM,
    )
    if staged:
        attend_column = [
            swap(attend_w, "blk", bits, f"attend_w_z{bits}") for bits in (2, 4, 6)
        ]
        slots_y = swap(sent[1], "blk", 1, "slots_y")
        messages = kernel_call(
            "route", route_kernel, [like((2 * share + EXTRA, width))] * 4, [sent[0], slots_y]
        )
        arrived = [messages[0]] + [
            swap(messages[k], "blk", 2 * k, f"slots_z{2 * k}") for k in (1, 2, 3)
        ]
        (moved,) = kernel_call("slots", slots_kernel, [like((n * share, width + META))], arrived)
        column = order(attend_column, messages[0])
        column = stack("attend_w_column", attend_w, *column)
        rest = swap(column, "blk", 1, "attend_w_rest")
        attend_p = [attend_w] + attend_column + [rest]
        inner_far = swap(order(inner_w, *attend_column), "blk", 4, "inner_w_far")
        inner_near = swap(stack("inner_w_pair", inner_w, inner_far), "blk", 2, "inner_w_near")
        outer_far = swap(order(outer_w, inner_far), "blk", 4, "outer_w_far")
    else:
        moved = lax.all_to_all(sent[0].reshape(n, share, width + META), "blk", 0, 0)
        moved = moved.reshape(sent[0].shape)
        gather = lambda value: [lax.all_gather(value, "blk", axis=0, tiled=True)]
        attend_p, inner_p, outer_p = gather(attend_w), gather(inner_w), gather(outer_w)
    far = swap(moved, "head", 2, "slots_x")
    parts = [moved, swap(moved, "head", 1, "slots_chip"), far, swap(far, "head", 1, "slots_far")]
    attend_plan = [((0,), 0), ((2,), 0), ((4,), 0), ((6,), 0), ((1, 3, 5, 7), 0)]
    inner_plan = [((0,), 0), ((1,), 0), ((4,), 0), ((2, 6), 0), ((5, 3, 7), 0)]
    outer_plan = [((0,), 0), ((1,), units), ((4,), 0), ((2, 6), 0), ((5, 3, 7), 0)]

    count = len(attend_p)
    mine, theirs, a, q, kv, mask, stat = kernel_call(
        "attend",
        functools.partial(attend_kernel, per_block, count, attend_plan),
        [
            like((half, width), F32),
            like((half, width)),
            like((rows, local)),
            like((rows, local)),
            like((slots + rows, 2 * local)),
            like((slots + rows, rows)),
            like((8, rows), F32),
        ],
        [hidden_in, tag_row, doc_row, vectors] + parts + attend_p,
        [piece_scratch(attend_p, 4 * local), pltpu.VMEM((rows, width), F32)],
        flops=2 * rows * width * local * 9,
    )
    if staged:
        facing = swap(order(ff_w, far), "blk", 1, "facing_w")
        outer_far = order(outer_far, theirs)
        outer_near = swap(stack("outer_w_pair", outer_w, outer_far), "blk", 2, "outer_w_near")
        inner_rest = stack("inner_w_column", inner_far, inner_near)
        inner_rest = swap(inner_rest, "blk", 1, "inner_w_rest")
        outer_rest = stack("outer_w_column", outer_far, outer_near)
        outer_rest = swap(outer_rest, "blk", 1, "outer_w_rest")
        inner_p = [inner_w, facing, inner_far, inner_near, inner_rest]
        outer_p = [outer_w, facing, outer_far, outer_near, outer_rest]
        mine = order(mine, facing, outer_far)
    chip, recv = chip_sum(mine, theirs, "branch")
    if staged:
        recv = order(recv, outer_near)
    h, normal_one, inv_one, hb = kernel_call(
        "norm_one",
        norm_one_kernel,
        [
            like((half, width), F32),
            like((half, width), F32),
            like((half, 1), F32),
            like((half, width)),
        ],
        [chip, recv, hidden_in, vectors],
    )
    hb_other = swap(hb, "head", 1, "hb")

    g, slope = kernel_call(
        "inner",
        functools.partial(inner_kernel, len(inner_p), inner_plan),
        [like((rows, units)), like((rows, units), F32)],
        [hb, hb_other, vectors] + inner_p,
        [piece_scratch(inner_p, units)],
        flops=2 * rows * width * units,
    )
    mine, theirs = kernel_call(
        "outer",
        functools.partial(outer_kernel, len(outer_p), outer_plan),
        [like((half, width), F32), like((half, width))],
        [g] + outer_p,
        [piece_scratch(outer_p, units)],
        flops=2 * rows * width * units,
    )
    chip, recv = chip_sum(mine, theirs, "ff")
    result, e_two, eb_two = kernel_call(
        "norm_two",
        norm_two_kernel,
        [like((half, width)), like((half, width), F32), like((half + EXTRA, width))],
        [chip, recv, h, vectors, cotangent],
    )
    eb_two_other = swap(eb_two, "head", 1, "eb_two")
    mine, theirs, du = kernel_call(
        "ff_back",
        functools.partial(
            ff_back_kernel, outer_plan, inner_plan, len(outer_p), len(inner_p)
        ),
        [like((half, width), F32), like((half, width)), like((rows, units))],
        [eb_two, eb_two_other, slope] + outer_p + inner_p,
        [piece_scratch(outer_p, units), piece_scratch(inner_p, units)],
        flops=4 * rows * width * units,
    )
    if staged:
        grad_outs = [like((width // 2, units)), like((width // 2, units))]
    else:
        grad_outs = [like((width, units), F32)]
    outer_g = kernel_call(
        "outer_grad",
        functools.partial(ff_weights_kernel, "outer"),
        grad_outs + [like((8, width), F32)],
        [eb_two, eb_two_other, g],
        [pltpu.VMEM((width, units), F32)],
        flops=2 * rows * width * units,
    )
    mine = order(mine, outer_g[0])
    chip, recv = chip_sum(mine, theirs, "ff_back")
    inner_g = kernel_call(
        "inner_grad",
        functools.partial(ff_weights_kernel, "inner"),
        grad_outs + [like((8, units), F32)],
        [hb, hb_other, du],
        [pltpu.VMEM((width, units), F32)],
        flops=2 * rows * width * units,
    )
    recv = order(recv, outer_g[0], inner_g[0])
    grad_units = [like((width // n, units), F32)]
    if staged:
        outer_y = swap(outer_g[1], "blk", 1, "outer_g_y")
        inner_near = swap(inner_g[1], "blk", 2, "inner_g_near")
    else:
        grad_outer_w = lax.psum_scatter(outer_g[0], "blk", scatter_dimension=0, tiled=True)
        grad_inner_w = lax.psum_scatter(inner_g[0], "blk", scatter_dimension=0, tiled=True)

    e_one, eb_one = kernel_call(
        "norm_back",
        norm_back_kernel,
        [like((half, width), F32), like((half + EXTRA, width))],
        [chip, recv, e_two, normal_one, inv_one, vectors],
    )
    eb_one_other = swap(eb_one, "head", 1, "eb_one")
    back_outs = [like((slots // 2, 2 * local))] * 2 if staged else []
    eb_full, dq, dkv, *back = kernel_call(
        "attend_back",
        functools.partial(attend_back_kernel, n, count, attend_plan),
        [
            like((rows, width)),
            like((rows, local)),
            like((slots + rows, 2 * local)),
        ]
        + back_outs,
        [eb_one, eb_one_other, q, kv, mask, stat] + attend_p,
        [piece_scratch(attend_p, 4 * local)],
        flops=2 * rows * width * local * 8,
    )
    if staged:
        back_y = swap(back[1], "blk", 1, "back_y")
        outer_k, outer_s = scatter_step("outer_g_one", outer_g[0], outer_y, [0, 2, 4, 6], 2)
        inner_near = order(inner_near, outer_k)
        inner_k, inner_s = scatter_step("inner_g_one", inner_g[0], inner_near, [0, 1, 4, 5], 1)
        dq = order(dq, inner_k, outer_k)
        grad_outs = [like((width // 2 + EXTRA, width))] * 2
    else:
        grad_outs = [like((width, width), F32), like((EXTRA, width), F32)]
    attend_g = kernel_call(
        "attend_grad",
        attend_weights_kernel,
        grad_outs,
        [hidden_in] + parts + [dkv, dq, eb_full, a, eb_one, eb_one_other, outer_g[-1], inner_g[-1]],
        [pltpu.VMEM((width, width), F32)],
        flops=2 * rows * width * local * 8,
    )
    if staged:
        back_y = order(back_y, attend_g[1])
        attend_y = swap(order(attend_g[1], back_y), "blk", 1, "attend_g_y")
        half_slots = [like((slots // 2, 2 * local))] * 2
        back_k, back_s = kernel_call(
            "back_one", functools.partial(back_kernel, room), half_slots, [back[0], back_y]
        )
        back_near = swap(back_s, "blk", 2, "back_near")
        outer_near = swap(order(outer_s, back_near), "blk", 2, "outer_g_near")
        inner_y = swap(inner_s, "blk", 1, "inner_g_y")
        back_k, back_s = kernel_call(
            "back_two", functools.partial(back_kernel, 2 * room), half_slots, [back_k, back_near]
        )
        moved = [back_k, swap(back_s, "blk", 4, "back_far")]
        outer_k, outer_s = scatter_step("outer_g_two", outer_k, outer_near, [0, 4], 4)
        attend_k, attend_s = scatter_step(
            "attend_g_one", attend_g[0], attend_y, [0, 2, 4, 6], 2, EXTRA
        )
        inner_k, inner_s = scatter_step("inner_g_two", inner_k, inner_y, [0, 4], 4)
        inner_last = swap(inner_s, "blk", 4, "inner_g_far")
        moved[0] = order(moved[0], outer_k, attend_k)
        outer_far = swap(order(outer_s, moved[1]), "blk", 4, "outer_g_far")
        (grad_outer_w,) = kernel_call(
            "outer_g_last", last_kernel, grad_units, [outer_k, outer_far]
        )
        (grad_inner_w,) = kernel_call(
            "inner_g_last", last_kernel, grad_units, [inner_k, inner_last]
        )
    else:
        moved = dkv[:slots].reshape(4, n, share, 2 * local).transpose(1, 0, 2, 3)
        moved = lax.all_to_all(moved, "blk", 0, 0).reshape(slots, 2 * local)
        moved = [moved]
    mine, theirs = kernel_call(
        "token",
        functools.partial(
            token_kernel, n, room, per_block, len(moved), count, attend_plan
        ),
        [like((half, width), F32), like((half, width))],
        [tag_row, dkv, dq] + moved + attend_p,
        [piece_scratch(attend_p, 4 * local), pltpu.VMEM((rows, width), F32)],
        flops=2 * rows * width * local * 4,
    )
    if staged:
        mine = order(mine, inner_k)
    chip, recv = chip_sum(mine, theirs, "last")
    if staged:
        attend_near = swap(attend_s, "blk", 2, "attend_g_near")
        attend_k, attend_s = scatter_step(
            "attend_g_two", attend_k, attend_near, [0, 4], 4, EXTRA
        )
        recv = order(recv, attend_k, grad_outer_w, grad_inner_w)
    last = e_one + (chip.astype(F32) + recv.astype(F32))
    last_other = swap(last, "head", 1, "last")
    result_other = swap(result, "head", 1, "result")

    def joined(own, other):
        return jnp.where(
            core == 0, jnp.concatenate([own, other]), jnp.concatenate([other, own])
        )

    layer_out = joined(result, result_other)
    grad_input = joined(last, last_other)
    small_outs = [like((width,), F32)] * 7 + [like((local,), F32)] * 2
    if staged:
        attend_far = swap(attend_s, "blk", 4, "attend_g_far")
        attend_far = order(attend_far, grad_input, layer_out)
        grads = kernel_call(
            "attend_g_last",
            last_kernel,
            [like((width // n, local), F32)] * 4 + small_outs,
            [attend_k, attend_far],
        )
        grads, small = grads[:4], grads[4:]
    else:
        summed = lax.psum_scatter(attend_g[0], "blk", scatter_dimension=0, tiled=True)
        grads = [summed[:, k * local : (k + 1) * local] for k in range(4)]
        small = kernel_call("small", small_kernel, small_outs, [lax.psum(attend_g[1], "blk")])
    grad_key_w, grad_value_w, grad_query_w, grad_output_w = grads

    return (
        layer_out,
        grad_input,
        grad_query_w,
        grad_key_w,
        grad_value_w,
        grad_output_w,
        grad_inner_w,
        grad_outer_w,
        small[7],
        small[8],
        small[6],
        small[3],
        small[2],
        small[4],
        small[5],
        small[0],
        small[1],
    )


def solution(mesh):
    matrix = P("blk", "head")
    in_specs = (
        (P("blk", None),)
        + (matrix,) * 6
        + (P("head"), P("head"), P(), P("head"))
        + (P(),) * 5
        + (P("blk"), P("blk"), P("blk", None))
    )
    out_specs = (
        (P("blk", None), P("blk", None))
        + (matrix,) * 6
        + (P("head"), P("head"), P(), P("head"))
        + (P(),) * 5
    )
    return jax.shard_map(
        per_device, mesh=mesh, in_specs=in_specs, out_specs=out_specs, check_vma=False
    )
```

```python
import functools
import math

import jax
import jax.numpy as jnp
from jax import lax
from jax.experimental import pallas as pl
from jax.experimental.pallas import tpu as pltpu
from jax.sharding import PartitionSpec as P

DH = 64
CLUSTER = 128
EPS = 1e-06
NEG = -1e30
SCALE = 1.0 / math.sqrt(DH)
META = 128
EXTRA = 16
VMEM = 16 << 20
BF = jnp.bfloat16
F32 = jnp.float32


def swap(value, axis, bits, name):
    with jax.named_scope(name):
        return lax.ppermute(value, axis, [(i, i ^ bits) for i in range(lax.axis_size(axis))])


def dot(left, right):
    return jnp.dot(left, right, preferred_element_type=F32)


def dot_last(left, right):
    return lax.dot_general(left, right, (((1,), (1,)), ((), ())), preferred_element_type=F32)


def dot_first(left, right):
    return lax.dot_general(left, right, (((0,), (0,)), ((), ())), preferred_element_type=F32)


def kernel_call(name, body, outs, args, scratch=(), flops=0, space=pltpu.VMEM):
    size = sum(math.prod(a.shape) * a.dtype.itemsize for a in list(args) + list(outs))
    whole = pl.BlockSpec(memory_space=pltpu.VMEM)
    return pl.pallas_call(
        body,
        out_shape=tuple(outs),
        in_specs=[pl.BlockSpec(memory_space=space)] * len(args),
        out_specs=tuple([whole] * len(outs)),
        scratch_shapes=list(scratch),
        name=name,
        compiler_params=pltpu.CompilerParams(vmem_limit_bytes=VMEM),
        cost_estimate=pl.CostEstimate(flops=flops, bytes_accessed=size, transcendentals=0),
    )(*args)


def like(shape, dtype=BF):
    return jax.ShapeDtypeStruct(shape, dtype)


def norm_forward(value, gain, shift):
    centered = value - jnp.mean(value, axis=-1, keepdims=True)
    variance = jnp.mean(centered * centered, axis=-1, keepdims=True)
    inv_std = lax.rsqrt(variance + EPS)
    normal_part = centered * inv_std
    return (normal_part * gain + shift, normal_part, inv_std)


def norm_backward(grad_out, normal_part, inv_std, gain):
    scaled = grad_out * gain
    mean_one = jnp.mean(scaled, axis=-1, keepdims=True)
    mean_two = jnp.mean(scaled * normal_part, axis=-1, keepdims=True)
    grad_in = inv_std * (scaled - mean_one - normal_part * mean_two)
    return (
        grad_in,
        jnp.sum(grad_out * normal_part, axis=0, keepdims=True),
        jnp.sum(grad_out, axis=0, keepdims=True),
    )


def extra_rows(*rows):
    width = rows[0].shape[1]
    return jnp.concatenate(list(rows) + [jnp.zeros((EXTRA - len(rows), width), F32)]).astype(BF)


def whole_matrix(pieces, plan, scratch):
    if len(pieces) == 1:
        return pieces[0][...]
    me = lax.axis_index("blk")
    rows, width = scratch.shape[1:]
    for piece, (sources, at) in zip(pieces, plan):
        for k, source in enumerate(sources):
            if len(piece.shape) == 3:
                scratch[me ^ source] = piece[k, :, at : at + width]
            else:
                scratch[me ^ source] = piece[k * rows : (k + 1) * rows, at : at + width]
    return scratch[...].reshape(-1, width)


def order(value, *after):
    return lax.optimization_barrier((value,) + after)[0]


def piece_scratch(pieces, width):
    if len(pieces) == 1:
        return pltpu.VMEM((8, 128), BF)
    return pltpu.VMEM((8, pieces[0].shape[-2], width), BF)


def places(tag_row, n, per_block, rows):
    target = tag_row // per_block
    onehot = lax.broadcasted_iota(jnp.int32, (n, rows), 0) == target
    earlier = lax.broadcasted_iota(jnp.int32, (rows, rows), 0) < lax.broadcasted_iota(
        jnp.int32, (rows, rows), 1
    )
    count = dot(onehot.astype(F32).astype(BF), earlier.astype(F32).astype(BF))
    rank = jnp.sum(jnp.where(onehot, count, 0.0), axis=0, keepdims=True).astype(jnp.int32)
    return target, rank


def fetch(sources, held, sems):
    copies = [
        pltpu.make_async_copy(source, to, sems.at[k])
        for k, (source, to) in enumerate(zip(sources, held))
    ]
    for copy in copies:
        copy.start()
    for copy in copies:
        copy.wait()


def pack_kernel(n, room, per_block, groups, *refs):
    count = 18
    sources, rest = refs[:count], refs[count:]
    held, sems = rest[-count - 1 : -1], rest[-1]
    *sends, attend_ref, ff_ref, vec_ref = rest[: -count - 1]
    fetch(sources, held, sems)
    for out, shards in ((attend_ref, held[:4]), (ff_ref, held[4:6])):
        at = 0
        for shard in shards:
            out[:, at : at + shard.shape[1]] = shard[...]
            at += shard.shape[1]
    x_ref, tag_ref, doc_ref, value_b, query_b, *vectors = held[6:]
    blank = jnp.zeros((1, value_b.shape[0]), F32)
    biases = [blank, value_b[...].reshape(1, -1), query_b[...].reshape(1, -1), blank]
    vec_ref[...] = jnp.concatenate(
        [jnp.concatenate(biases, axis=1)] + [item[...].reshape(1, -1) for item in vectors]
    )
    rows, width = x_ref.shape
    share = room // groups
    target, rank = places(tag_ref[...], n, per_block, rows)
    offset = rank - lax.axis_index("head") * share
    inside = (offset >= 0) & (offset < share)
    code = (1 + doc_ref[...] * per_block + tag_ref[...] % per_block).astype(F32)
    if len(sends) == 1:
        (out_ref,) = sends
        place = jnp.where(inside, target * share + offset, -1)
        pick = lax.broadcasted_iota(jnp.int32, (n * share, rows), 0) == place
        out_ref[:, :width] = dot(pick.astype(F32).astype(BF), x_ref[...]).astype(BF)
        code = jnp.sum(jnp.where(pick, code, 0.0), axis=1, keepdims=True)
        out_ref[:, width:] = jnp.broadcast_to(code, (n * share, META)).astype(BF)
        return
    odd = lax.axis_index("blk") % 2
    for t, out_ref in enumerate(sends):
        there = inside & (target % 2 == odd ^ t)
        place = jnp.where(there, target // 2 * share + offset, -1)
        pick = lax.broadcasted_iota(jnp.int32, (4 * share, rows), 0) == place
        out_ref[: 4 * share, :] = dot(pick.astype(F32).astype(BF), x_ref[...]).astype(BF)
        level = lax.broadcasted_iota(jnp.int32, (EXTRA, rows), 0)
        codes = jnp.where(there & (target // 2 == level), code, 0.0).astype(BF)
        spot = lax.broadcasted_iota(jnp.int32, (META, rows), 0) == offset
        tile = dot_last(codes, spot.astype(F32).astype(BF)).astype(BF)
        out_ref[4 * share :, :META] = tile
        out_ref[4 * share :, META:] = jnp.zeros((EXTRA, width - META), BF)


def route_kernel(keep_ref, recv_ref, *outs):
    level = lax.axis_index("blk") // 2
    rows, share = 0, (keep_ref.shape[0] - EXTRA) // 4
    width = keep_ref.shape[1]
    lanes = lax.broadcasted_iota(jnp.int32, (EXTRA, META), 0)
    for k in range(4):
        z = level ^ k
        for t, ref in enumerate((keep_ref, recv_ref)):
            outs[k][rows + t * share : rows + (t + 1) * share, :] = ref[pl.ds(z * share, share), :]
        first = keep_ref[4 * share :, :META].astype(F32)
        second = recv_ref[4 * share :, :META].astype(F32)
        first = jnp.sum(jnp.where(lanes == z, first, 0.0), axis=0, keepdims=True)
        second = jnp.sum(jnp.where(lanes == z, second, 0.0), axis=0, keepdims=True)
        tile = jnp.where(lanes == 0, first, jnp.where(lanes == 1, second, 0.0))
        outs[k][rows + 2 * share :, :META] = tile.astype(BF)
        outs[k][rows + 2 * share :, META:] = jnp.zeros((EXTRA, width - META), BF)


def stack_kernel(*refs):
    out_ref, at = refs[-1], 0
    for ref in refs[:-1]:
        if len(ref.shape) == 3:
            out_ref[at : at + ref.shape[0]] = ref[...]
            at += ref.shape[0]
        else:
            out_ref[at] = ref[...]
            at += 1


def stack(name, *parts):
    count = sum(1 if part.ndim == 2 else part.shape[0] for part in parts)
    (out,) = kernel_call(name, stack_kernel, [like((count,) + parts[0].shape[-2:])], parts)
    return out


def slots_kernel(*refs):
    out_ref = refs[4]
    share, width = (refs[0].shape[0] - EXTRA) // 2, refs[0].shape[1]
    lane = lax.broadcasted_iota(jnp.int32, (2 * share, META), 1)
    row = lax.broadcasted_iota(jnp.int32, (2 * share, META), 0)
    for k, ref in enumerate(refs[:4]):
        at = slice(2 * k * share, 2 * (k + 1) * share)
        out_ref[at, :width] = ref[: 2 * share, :]
        codes = ref[2 * share :, :META].astype(F32)
        spread = jnp.where(row < share, codes[:1, :], codes[1:2, :])
        code = jnp.sum(jnp.where(lane == row % share, spread, 0.0), axis=1, keepdims=True)
        out_ref[at, width:] = jnp.broadcast_to(code, (2 * share, META)).astype(BF)


def attend_kernel(per_block, count, plan, *refs):
    x_ref, tag_ref, doc_ref, bias_ref = refs[:4]
    parts = refs[4:8]
    pieces = refs[8 : 8 + count]
    mine_ref, theirs_ref, a_ref, q_ref, kv_ref, mask_ref, stat_ref, scratch, y_ref = refs[
        8 + count :
    ]
    rows, width = x_ref.shape
    local = a_ref.shape[1]
    slots = kv_ref.shape[0] - rows
    step = slots // 4
    me = lax.axis_index("blk")
    core = lax.axis_index("head") % 2
    weight = whole_matrix(pieces, plan, scratch)
    own = dot(x_ref[...], weight[:, : 3 * local]) + bias_ref[:1, : 3 * local]
    q_ref[...] = own[:, 2 * local :].astype(BF)
    kv_ref[slots:, :] = own[:, : 2 * local].astype(BF)
    row_cluster = lax.broadcasted_iota(jnp.int32, (1, rows), 1) // CLUSTER
    wanted = (1 + doc_ref[...] * per_block + row_cluster).astype(F32)
    for k in range(4):
        part = parts[k]
        kv_ref[k * step : (k + 1) * step, :] = (
            dot(part[:, :width], weight[:, : 2 * local]) + bias_ref[:1, : 2 * local]
        ).astype(BF)
        code = part[:, width : width + 1].astype(F32)
        mask_ref[k * step : (k + 1) * step, :] = jnp.where(code == wanted, 0.0, NEG).astype(BF)
    alone = tag_ref[...] != me * per_block + row_cluster
    diagonal = lax.broadcasted_iota(jnp.int32, (rows, rows), 0) == lax.broadcasted_iota(
        jnp.int32, (rows, rows), 1
    )
    mask_ref[slots:, :] = jnp.where(diagonal & alone, 0.0, NEG).astype(BF)
    mask = mask_ref[...].astype(F32)
    stats = []
    for j in range(local // DH):
        cut = slice(j * DH, (j + 1) * DH)
        scores = dot_last(kv_ref[:, cut], q_ref[:, cut]) * SCALE + mask
        top = jnp.max(scores, axis=0, keepdims=True)
        weights = jnp.exp(scores - top)
        inverse = 1.0 / jnp.sum(weights, axis=0, keepdims=True)
        probs = (weights * inverse).astype(BF)
        value = kv_ref[:, local + j * DH : local + (j + 1) * DH]
        a_ref[:, cut] = dot_first(probs, value).astype(BF)
        stats += [top, inverse]
    stat_ref[...] = jnp.concatenate(stats + [jnp.zeros((8 - len(stats), rows), F32)])
    y_ref[...] = dot_last(a_ref[...], weight[:, 3 * local :])
    half = rows // 2
    mine_ref[...] = y_ref[pl.ds(core * half, half), :]
    theirs_ref[...] = y_ref[pl.ds((1 - core) * half, half), :].astype(BF)


def attend_back_kernel(n, count, plan, *refs):
    own_ref, other_ref, q_ref, kv_ref, mask_ref, stat_ref = refs[:6]
    pieces = refs[6 : 6 + count]
    eb_ref, dq_ref, dkv_ref = refs[6 + count : 9 + count]
    back, scratch = refs[9 + count : -1], refs[-1]
    rows, local = q_ref.shape
    slots = kv_ref.shape[0] - rows
    half = rows // 2
    core = lax.axis_index("head") % 2
    weight = whole_matrix(pieces, plan, scratch)
    eb_ref[pl.ds(core * half, half), :] = own_ref[:half, :]
    eb_ref[pl.ds((1 - core) * half, half), :] = other_ref[:half, :]
    da = dot(eb_ref[...], weight[:, 3 * local :]).astype(BF)
    mask = mask_ref[...].astype(F32)
    for j in range(local // DH):
        cut = slice(j * DH, (j + 1) * DH)
        key, query = kv_ref[:, cut], q_ref[:, cut]
        value = kv_ref[:, local + j * DH : local + (j + 1) * DH]
        scores = dot_last(key, query) * SCALE + mask
        probs = jnp.exp(scores - stat_ref[2 * j : 2 * j + 1, :]) * stat_ref[
            2 * j + 1 : 2 * j + 2, :
        ]
        low = probs.astype(BF)
        dkv_ref[:, local + j * DH : local + (j + 1) * DH] = dot(low, da[:, cut]).astype(BF)
        grad = dot_last(value, da[:, cut])
        delta = jnp.sum(low.astype(F32) * grad, axis=0, keepdims=True)
        grad = (probs * (grad - delta)).astype(BF)
        dkv_ref[:, cut] = (dot(grad, query) * SCALE).astype(BF)
        dq_ref[:, cut] = (dot_first(grad, key) * SCALE).astype(BF)
    if back:
        share = slots // 4 // n
        for t in range(2):
            for z in range(4):
                for k in range(4):
                    at = k * slots // 4 + (2 * z + t) * share
                    to = (z * 4 + k) * share
                    back[t][to : to + share, :] = dkv_ref[at : at + share, :]


def back_kernel(room, left_ref, right_ref, keep_ref, send_ref):
    for k in range(left_ref.shape[0] // room):
        out, to = (send_ref if k % 2 else keep_ref), k // 2 * 2 * room
        out[to : to + room, :] = left_ref[k * room : (k + 1) * room, :]
        out[to + room : to + 2 * room, :] = right_ref[k * room : (k + 1) * room, :]


def token_kernel(n, room, per_block, parts, count, plan, *refs):
    tag_ref, dkv_ref, dq_ref = refs[:3]
    back = refs[3 : 3 + parts]
    pieces = refs[3 + parts : 3 + parts + count]
    mine_ref, theirs_ref, scratch, z_ref = refs[3 + parts + count :]
    rows, local = dq_ref.shape
    slots = n * room
    half = rows // 2
    share = room // 4
    group = lax.axis_index("head")
    core = group % 2
    weight = whole_matrix(pieces, plan, scratch)
    target, rank = places(tag_ref[...], n, per_block, rows)
    if parts > 1:
        target = target ^ lax.axis_index("blk")
    place = target * room + ((rank // share) ^ group) * share + rank % share
    total = dkv_ref[slots:, :].astype(F32)
    step = slots // parts
    for k in range(parts):
        pick = lax.broadcasted_iota(jnp.int32, (step, rows), 0) + k * step == place
        total = total + dot_first(pick.astype(F32).astype(BF), back[k][...])
    z_ref[...] = dot_last(total.astype(BF), weight[:, : 2 * local]) + dot_last(
        dq_ref[...], weight[:, 2 * local : 3 * local]
    )
    mine_ref[...] = z_ref[pl.ds(core * half, half), :]
    theirs_ref[...] = z_ref[pl.ds((1 - core) * half, half), :].astype(BF)


def norm_one_kernel(
    chip_ref, recv_ref, x_ref, vec_ref, h_ref, n_ref, r_ref, hb_ref
):
    half = chip_ref.shape[0]
    core = lax.axis_index("head") % 2
    branch = chip_ref[...].astype(F32) + recv_ref[...].astype(F32) + vec_ref[1:2, :]
    value = x_ref[pl.ds(core * half, half), :].astype(F32) + branch
    h, normal, inverse = norm_forward(value, vec_ref[2:3, :], vec_ref[3:4, :])
    h_ref[...] = h
    n_ref[...] = normal
    r_ref[...] = inverse
    hb_ref[...] = h.astype(BF)


def norm_two_kernel(
    chip_ref, recv_ref, h_ref, vec_ref, c_ref, out_ref, e_ref, eb_ref
):
    half = chip_ref.shape[0]
    core = lax.axis_index("head") % 2
    outer = chip_ref[...].astype(F32) + recv_ref[...].astype(F32) + vec_ref[4:5, :]
    gain_row = vec_ref[5:6, :]
    result, normal, inverse = norm_forward(h_ref[...] + outer, gain_row, vec_ref[6:7, :])
    out_ref[...] = result.astype(BF)
    cotangent = c_ref[pl.ds(core * half, half), :].astype(F32)
    grad, gain, shift = norm_backward(cotangent, normal, inverse, gain_row)
    e_ref[...] = grad
    eb_ref[:half, :] = grad.astype(BF)
    eb_ref[half:, :] = extra_rows(gain, shift)


def norm_back_kernel(chip_ref, recv_ref, e_ref, n_ref, r_ref, vec_ref, out_ref, eb_ref):
    half = chip_ref.shape[0]
    grad = e_ref[...] + (chip_ref[...].astype(F32) + recv_ref[...].astype(F32))
    grad, gain, shift = norm_backward(grad, n_ref[...], r_ref[...], vec_ref[2:3, :])
    out_ref[...] = grad
    eb_ref[:half, :] = grad.astype(BF)
    eb_ref[half:, :] = extra_rows(gain, shift)


def inner_kernel(count, plan, *refs):
    own_ref, other_ref, bias_ref = refs[:3]
    pieces = refs[3 : 3 + count]
    g_ref, slope_ref, scratch = refs[3 + count :]
    half = own_ref.shape[0]
    weight = whole_matrix(pieces, plan, scratch)
    for k, part in enumerate((own_ref, other_ref)):
        u = dot(part[...], weight) + bias_ref[7:8, :]
        below = 0.5 * (1.0 + lax.erf(u * math.sqrt(0.5)))
        g_ref[k * half : (k + 1) * half, :] = (u * below).astype(BF)
        density = jnp.exp(-0.5 * u * u) * (1.0 / math.sqrt(2.0 * math.pi))
        slope_ref[k * half : (k + 1) * half, :] = below + u * density


def outer_kernel(count, plan, *refs):
    g_ref = refs[0]
    pieces = refs[1 : 1 + count]
    mine_ref, theirs_ref, scratch = refs[1 + count :]
    half = mine_ref.shape[0]
    weight = whole_matrix(pieces, plan, scratch)
    mine_ref[...] = dot_last(g_ref[:half, :], weight)
    theirs_ref[...] = dot_last(g_ref[half:, :], weight).astype(BF)


def ff_back_kernel(outer_plan, inner_plan, outer_count, inner_count, *refs):
    own_ref, other_ref, slope_ref = refs[:3]
    outer, inner = refs[3 : 3 + outer_count], refs[3 + outer_count :][:inner_count]
    mine_ref, theirs_ref, du_ref, scratch, scratch_two = refs[3 + outer_count + inner_count :]
    half = mine_ref.shape[0]
    outer = whole_matrix(outer, outer_plan, scratch)
    inner = whole_matrix(inner, inner_plan, scratch_two)
    for k, part in ((1, other_ref), (0, own_ref)):
        rows = slice(k * half, (k + 1) * half)
        dg = dot(part[:half, :], outer).astype(BF).astype(F32)
        du_ref[rows, :] = (dg * slope_ref[rows, :]).astype(BF)
        dh = dot_last(du_ref[rows, :], inner)
        if k:
            theirs_ref[...] = dh.astype(BF)
        else:
            mine_ref[...] = dh


def halves(blocks, bit):
    return [b for b in blocks if not b & bit], [b for b in blocks if b & bit]


def split_pieces(total, bit, mine_ref, theirs_ref):
    me = lax.axis_index("blk")
    rows = total.shape[0] // 8
    for out, blocks in zip((mine_ref, theirs_ref), halves(range(8), bit)):
        for k, block in enumerate(blocks):
            out[k * rows : (k + 1) * rows, :] = total[pl.ds((me ^ block) * rows, rows), :].astype(BF)


def ff_weights_kernel(small, own_ref, other_ref, left_ref, *refs):
    half = left_ref.shape[0] // 2
    refs = list(refs)
    total = refs.pop()
    total[...] = dot_first(own_ref[:half, :], left_ref[:half, :]) + dot_first(
        other_ref[:half, :], left_ref[half:, :]
    )
    if small == "outer":
        small_ref = refs.pop()
        norms = own_ref[half:, :].astype(F32) + other_ref[half:, :].astype(F32)
        bias = jnp.sum(own_ref[:half, :].astype(F32), axis=0, keepdims=True) + jnp.sum(
            other_ref[:half, :].astype(F32), axis=0, keepdims=True
        )
        small_ref[...] = jnp.concatenate([norms[:2], bias, jnp.zeros((5, bias.shape[1]), F32)])
    else:
        small_ref = refs.pop()
        bias = jnp.sum(left_ref[...].astype(F32), axis=0, keepdims=True)
        small_ref[...] = jnp.concatenate([bias, jnp.zeros((7, bias.shape[1]), F32)])
    if len(refs) == 1:
        refs[0][...] = total[...]
    else:
        split_pieces(total, 1 if small == "outer" else 2, *refs)


def attend_weights_kernel(*refs):
    x_ref, p0, p1, p2, p3, dkv_ref, dq_ref, eb_ref, a_ref, own_ref, other_ref = refs[:11]
    outer_ref, inner_ref = refs[11:13]
    outs, total = list(refs[13:-1]), refs[-1]
    rows, width = x_ref.shape
    local = dq_ref.shape[1]
    slots = dkv_ref.shape[0] - rows
    step = slots // 4
    sums = dot_first(x_ref[...], dkv_ref[slots:, :])
    for k, part in enumerate((p0, p1, p2, p3)):
        sums = sums + dot_first(part[:, :width], dkv_ref[k * step : (k + 1) * step, :])
    total[:, : 2 * local] = sums
    total[:, 2 * local : 3 * local] = dot_first(x_ref[...], dq_ref[...])
    total[:, 3 * local :] = dot_first(eb_ref[...], a_ref[...])
    half = rows // 2
    norms = own_ref[half:, :].astype(F32) + other_ref[half:, :].astype(F32)
    output_b = jnp.sum(eb_ref[...].astype(F32), axis=0, keepdims=True)
    query_b = jnp.sum(dq_ref[...].astype(F32), axis=0, keepdims=True)
    value_b = jnp.sum(dkv_ref[...].astype(F32), axis=0, keepdims=True)
    last = jnp.concatenate([value_b, query_b, jnp.zeros((1, width - 3 * local), F32)], axis=1)
    small = jnp.concatenate(
        [
            outer_ref[:3, :],
            inner_ref[:1, :],
            norms[:2],
            output_b,
            last,
            jnp.zeros((EXTRA - 8, width), F32),
        ]
    )
    if outs[0].shape == total.shape:
        outs[0][...] = total[...]
        outs[1][...] = small
    else:
        split_pieces(total, 1, *outs)
        body = outs[0].shape[0] - EXTRA
        outs[0][body:, :] = small.astype(BF)
        outs[1][body:, :] = small.astype(BF)


def middle_kernel(extra, blocks, bit, mine_ref, recv_ref, *outs):
    rows = (mine_ref.shape[0] - extra) // len(blocks)
    last = mine_ref.shape[0] - extra
    for out, pieces in zip(outs, halves(blocks, bit)):
        for k, piece in enumerate(pieces):
            at = slice(blocks.index(piece) * rows, (blocks.index(piece) + 1) * rows)
            out[k * rows : (k + 1) * rows, :] = (
                mine_ref[at, :].astype(F32) + recv_ref[at, :].astype(F32)
            ).astype(BF)
        if extra:
            small = mine_ref[last:, :].astype(F32) + recv_ref[last:, :].astype(F32)
            out[len(pieces) * rows :, :] = small.astype(BF)


def pair_kernel(*refs):
    inputs, keeps, send_ref = refs[:4], refs[4:6], refs[6]
    rows = keeps[0].shape[0]
    for k, keep_ref in enumerate(keeps):
        mine_ref, recv_ref = inputs[2 * k : 2 * k + 2]
        total = (mine_ref[...].astype(F32) + recv_ref[...].astype(F32)).astype(BF)
        keep_ref[...] = total[:rows, :]
        send_ref[k * rows : (k + 1) * rows, :] = total[rows:, :]


def last_pair_kernel(first_ref, second_ref, recv_ref, *outs):
    rows = first_ref.shape[0]
    for k, ref in enumerate((first_ref, second_ref)):
        recv = recv_ref[k * rows : (k + 1) * rows, :]
        outs[k][...] = ref[...].astype(F32) + recv.astype(F32)


def last_kernel(left_ref, right_ref, *outs):
    total = left_ref[...].astype(F32) + right_ref[...].astype(F32)
    if len(outs) == 1:
        outs[0][...] = total
        return
    rows, local = outs[0].shape
    for k in range(4):
        outs[k][...] = total[:rows, k * local : (k + 1) * local]
    spread_small(total[rows:, :], local, outs[4:])


def spread_small(small, local, outs):
    for k, out in enumerate(outs[:7]):
        out[...] = small[k, :]
    outs[7][...] = small[7, 2 * local : 3 * local]
    outs[8][...] = small[7, local : 2 * local]


def small_kernel(small_ref, *outs):
    spread_small(small_ref[...], outs[7].shape[0], outs)


def scatter_step(name, mine, recv, blocks, bit, extra=0):
    rows = (mine.shape[0] - extra) // 2 + extra
    return kernel_call(
        name,
        functools.partial(middle_kernel, extra, blocks, bit),
        [like((rows, mine.shape[1]))] * 2,
        [mine, recv],
    )


def chip_sum(mine, theirs, name):
    chip = (mine + swap(theirs, "head", 1, name + "_chip").astype(F32)).astype(BF)
    return chip, swap(chip, "head", 2, name + "_x")


def per_device(
    hidden_in,
    query_w,
    key_w,
    value_w,
    output_w,
    inner_w,
    outer_w,
    query_b,
    value_b,
    output_b,
    inner_b,
    outer_b,
    first_gain,
    first_shift,
    second_gain,
    second_shift,
    key_cluster,
    document,
    cotangent,
):
    rows, width = hidden_in.shape
    n = lax.axis_size("blk")
    groups = lax.axis_size("head")
    assert groups == 4
    local = query_w.shape[1]
    units = inner_w.shape[1]
    per_block = rows // CLUSTER
    room = 2 * rows // n
    slots = n * room
    half = rows // 2
    share = room // groups
    staged = n == 8
    core = lax.axis_index("head") % 2

    tag_row, doc_row = key_cluster.reshape(1, rows), document.reshape(1, rows)

    if staged:
        sends = [like((4 * share + EXTRA, width))] * 2
    else:
        sends = [like((n * share, width + META))]
    pack_args = [key_w, value_w, query_w, output_w, inner_w, outer_w]
    pack_args += [hidden_in, tag_row, doc_row, value_b, query_b, output_b]
    pack_args += [first_gain, first_shift, outer_b, second_gain, second_shift, inner_b]
    *sent, attend_w, ff_w, vectors = kernel_call(
        "pack",
        functools.partial(pack_kernel, n, room, per_block, groups),
        sends
        + [
            like((width // n, 4 * local)),
            like((width // n, 2 * units)),
            like((8, width), F32),
        ],
        [pltpu.with_memory_space_constraint(item, pltpu.HBM) for item in pack_args],
        [pltpu.VMEM(item.shape, item.dtype) for item in pack_args]
        + [pltpu.SemaphoreType.DMA((len(pack_args),))],
        flops=2 * n * share * rows * width,
        space=pltpu.HBM,
    )
    if staged:
        attend_column = [
            swap(attend_w, "blk", bits, f"attend_w_z{bits}") for bits in (2, 4, 6)
        ]
        slots_y = swap(sent[1], "blk", 1, "slots_y")
        messages = kernel_call(
            "route", route_kernel, [like((2 * share + EXTRA, width))] * 4, [sent[0], slots_y]
        )
        arrived = [messages[0]] + [
            swap(messages[k], "blk", 2 * k, f"slots_z{2 * k}") for k in (1, 2, 3)
        ]
        (moved,) = kernel_call("slots", slots_kernel, [like((n * share, width + META))], arrived)
        column = order(attend_column, messages[0])
        column = stack("attend_w_column", attend_w, *column)
        rest = swap(column, "blk", 1, "attend_w_rest")
        attend_p = [attend_w] + attend_column + [rest]
        inner_far = swap(order(inner_w, *attend_column), "blk", 4, "inner_w_far")
        inner_near = swap(stack("inner_w_pair", inner_w, inner_far), "blk", 2, "inner_w_near")
        outer_far = swap(order(outer_w, inner_far), "blk", 4, "outer_w_far")
    else:
        moved = lax.all_to_all(sent[0].reshape(n, share, width + META), "blk", 0, 0)
        moved = moved.reshape(sent[0].shape)
        gather = lambda value: [lax.all_gather(value, "blk", axis=0, tiled=True)]
        attend_p, inner_p, outer_p = gather(attend_w), gather(inner_w), gather(outer_w)
    far = swap(moved, "head", 2, "slots_x")
    parts = [moved, swap(moved, "head", 1, "slots_chip"), far, swap(far, "head", 1, "slots_far")]
    attend_plan = [((0,), 0), ((2,), 0), ((4,), 0), ((6,), 0), ((1, 3, 5, 7), 0)]
    inner_plan = [((0,), 0), ((1,), 0), ((4,), 0), ((2, 6), 0), ((5, 3, 7), 0)]
    outer_plan = [((0,), 0), ((1,), units), ((4,), 0), ((2, 6), 0), ((5, 3, 7), 0)]

    count = len(attend_p)
    mine, theirs, a, q, kv, mask, stat = kernel_call(
        "attend",
        functools.partial(attend_kernel, per_block, count, attend_plan),
        [
            like((half, width), F32),
            like((half, width)),
            like((rows, local)),
            like((rows, local)),
            like((slots + rows, 2 * local)),
            like((slots + rows, rows)),
            like((8, rows), F32),
        ],
        [hidden_in, tag_row, doc_row, vectors] + parts + attend_p,
        [piece_scratch(attend_p, 4 * local), pltpu.VMEM((rows, width), F32)],
        flops=2 * rows * width * local * 9,
    )
    if staged:
        facing = swap(order(ff_w, far), "blk", 1, "facing_w")
        outer_far = order(outer_far, theirs)
        outer_near = swap(stack("outer_w_pair", outer_w, outer_far), "blk", 2, "outer_w_near")
        inner_rest = stack("inner_w_column", inner_far, inner_near)
        inner_rest = swap(inner_rest, "blk", 1, "inner_w_rest")
        outer_rest = stack("outer_w_column", outer_far, outer_near)
        outer_rest = swap(outer_rest, "blk", 1, "outer_w_rest")
        inner_p = [inner_w, facing, inner_far, inner_near, inner_rest]
        outer_p = [outer_w, facing, outer_far, outer_near, outer_rest]
        mine = order(mine, facing, outer_far)
    chip, recv = chip_sum(mine, theirs, "branch")
    if staged:
        recv = order(recv, outer_near)
    h, normal_one, inv_one, hb = kernel_call(
        "norm_one",
        norm_one_kernel,
        [
            like((half, width), F32),
            like((half, width), F32),
            like((half, 1), F32),
            like((half, width)),
        ],
        [chip, recv, hidden_in, vectors],
    )
    hb_other = swap(hb, "head", 1, "hb")

    g, slope = kernel_call(
        "inner",
        functools.partial(inner_kernel, len(inner_p), inner_plan),
        [like((rows, units)), like((rows, units), F32)],
        [hb, hb_other, vectors] + inner_p,
        [piece_scratch(inner_p, units)],
        flops=2 * rows * width * units,
    )
    mine, theirs = kernel_call(
        "outer",
        functools.partial(outer_kernel, len(outer_p), outer_plan),
        [like((half, width), F32), like((half, width))],
        [g] + outer_p,
        [piece_scratch(outer_p, units)],
        flops=2 * rows * width * units,
    )
    chip, recv = chip_sum(mine, theirs, "ff")
    result, e_two, eb_two = kernel_call(
        "norm_two",
        norm_two_kernel,
        [like((half, width)), like((half, width), F32), like((half + EXTRA, width))],
        [chip, recv, h, vectors, cotangent],
    )
    eb_two_other = swap(eb_two, "head", 1, "eb_two")
    mine, theirs, du = kernel_call(
        "ff_back",
        functools.partial(
            ff_back_kernel, outer_plan, inner_plan, len(outer_p), len(inner_p)
        ),
        [like((half, width), F32), like((half, width)), like((rows, units))],
        [eb_two, eb_two_other, slope] + outer_p + inner_p,
        [piece_scratch(outer_p, units), piece_scratch(inner_p, units)],
        flops=4 * rows * width * units,
    )
    if staged:
        grad_outs = [like((width // 2, units)), like((width // 2, units))]
    else:
        grad_outs = [like((width, units), F32)]
    outer_g = kernel_call(
        "outer_grad",
        functools.partial(ff_weights_kernel, "outer"),
        grad_outs + [like((8, width), F32)],
        [eb_two, eb_two_other, g],
        [pltpu.VMEM((width, units), F32)],
        flops=2 * rows * width * units,
    )
    mine = order(mine, outer_g[0])
    chip, recv = chip_sum(mine, theirs, "ff_back")
    inner_g = kernel_call(
        "inner_grad",
        functools.partial(ff_weights_kernel, "inner"),
        grad_outs + [like((8, units), F32)],
        [hb, hb_other, du],
        [pltpu.VMEM((width, units), F32)],
        flops=2 * rows * width * units,
    )
    recv = order(recv, outer_g[0], inner_g[0])
    grad_units = [like((width // n, units), F32)]
    if staged:
        outer_y = swap(outer_g[1], "blk", 1, "outer_g_y")
        inner_near = swap(inner_g[1], "blk", 2, "inner_g_near")
    else:
        grad_outer_w = lax.psum_scatter(outer_g[0], "blk", scatter_dimension=0, tiled=True)
        grad_inner_w = lax.psum_scatter(inner_g[0], "blk", scatter_dimension=0, tiled=True)

    e_one, eb_one = kernel_call(
        "norm_back",
        norm_back_kernel,
        [like((half, width), F32), like((half + EXTRA, width))],
        [chip, recv, e_two, normal_one, inv_one, vectors],
    )
    eb_one_other = swap(eb_one, "head", 1, "eb_one")
    back_outs = [like((slots // 2, 2 * local))] * 2 if staged else []
    eb_full, dq, dkv, *back = kernel_call(
        "attend_back",
        functools.partial(attend_back_kernel, n, count, attend_plan),
        [
            like((rows, width)),
            like((rows, local)),
            like((slots + rows, 2 * local)),
        ]
        + back_outs,
        [eb_one, eb_one_other, q, kv, mask, stat] + attend_p,
        [piece_scratch(attend_p, 4 * local)],
        flops=2 * rows * width * local * 8,
    )
    if staged:
        back_y = swap(back[1], "blk", 1, "back_y")
        outer_k, outer_s = scatter_step("outer_g_one", outer_g[0], outer_y, [0, 2, 4, 6], 2)
        inner_near = order(inner_near, outer_k)
        inner_k, inner_s = scatter_step("inner_g_one", inner_g[0], inner_near, [0, 1, 4, 5], 1)
        dq = order(dq, inner_k, outer_k)
        grad_outs = [like((width // 2 + EXTRA, width))] * 2
    else:
        grad_outs = [like((width, width), F32), like((EXTRA, width), F32)]
    attend_g = kernel_call(
        "attend_grad",
        attend_weights_kernel,
        grad_outs,
        [hidden_in] + parts + [dkv, dq, eb_full, a, eb_one, eb_one_other, outer_g[-1], inner_g[-1]],
        [pltpu.VMEM((width, width), F32)],
        flops=2 * rows * width * local * 8,
    )
    if staged:
        back_y = order(back_y, attend_g[1])
        attend_y = swap(order(attend_g[1], back_y), "blk", 1, "attend_g_y")
        half_slots = [like((slots // 2, 2 * local))] * 2
        back_k, back_s = kernel_call(
            "back_one", functools.partial(back_kernel, room), half_slots, [back[0], back_y]
        )
        back_near = swap(back_s, "blk", 2, "back_near")
        outer_near = swap(order(outer_s, back_near), "blk", 2, "outer_g_near")
        inner_y = swap(inner_s, "blk", 1, "inner_g_y")
        back_k, back_s = kernel_call(
            "back_two", functools.partial(back_kernel, 2 * room), half_slots, [back_k, back_near]
        )
        moved = [back_k, swap(back_s, "blk", 4, "back_far")]
        attend_k, attend_s = scatter_step(
            "attend_g_one", attend_g[0], attend_y, [0, 2, 4, 6], 2, EXTRA
        )
        piece = like((width // n, units))
        inner_k, outer_k, both = kernel_call(
            "pair",
            pair_kernel,
            [piece, piece, like((2 * width // n, units))],
            [inner_k, inner_y, outer_k, outer_near],
        )
        moved[0] = order(moved[0], attend_k)
        both = swap(order(both, moved[1]), "blk", 4, "both_far")
        grad_inner_w, grad_outer_w = kernel_call(
            "pair_last", last_pair_kernel, grad_units * 2, [inner_k, outer_k, both]
        )
    else:
        moved = dkv[:slots].reshape(4, n, share, 2 * local).transpose(1, 0, 2, 3)
        moved = lax.all_to_all(moved, "blk", 0, 0).reshape(slots, 2 * local)
        moved = [moved]
    mine, theirs = kernel_call(
        "token",
        functools.partial(
            token_kernel, n, room, per_block, len(moved), count, attend_plan
        ),
        [like((half, width), F32), like((half, width))],
        [tag_row, dkv, dq] + moved + attend_p,
        [piece_scratch(attend_p, 4 * local), pltpu.VMEM((rows, width), F32)],
        flops=2 * rows * width * local * 4,
    )
    if staged:
        mine = order(mine, inner_k)
    chip, recv = chip_sum(mine, theirs, "last")
    if staged:
        attend_near = swap(attend_s, "blk", 2, "attend_g_near")
        attend_k, attend_s = scatter_step(
            "attend_g_two", attend_k, attend_near, [0, 4], 4, EXTRA
        )
        recv = order(recv, attend_k, grad_inner_w)
    last = e_one + (chip.astype(F32) + recv.astype(F32))
    last_other = swap(last, "head", 1, "last")
    result_other = swap(result, "head", 1, "result")

    def joined(own, other):
        return jnp.where(
            core == 0, jnp.concatenate([own, other]), jnp.concatenate([other, own])
        )

    layer_out = joined(result, result_other)
    grad_input = joined(last, last_other)
    small_outs = [like((width,), F32)] * 7 + [like((local,), F32)] * 2
    if staged:
        attend_far = swap(attend_s, "blk", 4, "attend_g_far")
        attend_far = order(attend_far, grad_input, layer_out)
        grads = kernel_call(
            "attend_g_last",
            last_kernel,
            [like((width // n, local), F32)] * 4 + small_outs,
            [attend_k, attend_far],
        )
        grads, small = grads[:4], grads[4:]
    else:
        summed = lax.psum_scatter(attend_g[0], "blk", scatter_dimension=0, tiled=True)
        grads = [summed[:, k * local : (k + 1) * local] for k in range(4)]
        small = kernel_call("small", small_kernel, small_outs, [lax.psum(attend_g[1], "blk")])
    grad_key_w, grad_value_w, grad_query_w, grad_output_w = grads

    return (
        layer_out,
        grad_input,
        grad_query_w,
        grad_key_w,
        grad_value_w,
        grad_output_w,
        grad_inner_w,
        grad_outer_w,
        small[7],
        small[8],
        small[6],
        small[3],
        small[2],
        small[4],
        small[5],
        small[0],
        small[1],
    )


def solution(mesh):
    matrix = P("blk", "head")
    in_specs = (
        (P("blk", None),)
        + (matrix,) * 6
        + (P("head"), P("head"), P(), P("head"))
        + (P(),) * 5
        + (P("blk"), P("blk"), P("blk", None))
    )
    out_specs = (
        (P("blk", None), P("blk", None))
        + (matrix,) * 6
        + (P("head"), P("head"), P(), P("head"))
        + (P(),) * 5
    )
    return jax.shard_map(
        per_device, mesh=mesh, in_specs=in_specs, out_specs=out_specs, check_vma=False
    )
```

```python
import functools
import math

import jax
import jax.numpy as jnp
from jax import lax
from jax.experimental import pallas as pl
from jax.experimental.pallas import tpu as pltpu
from jax.sharding import PartitionSpec as P

DH = 64
CLUSTER = 128
EPS = 1e-06
NEG = -1e30
SCALE = 1.0 / math.sqrt(DH)
META = 128
EXTRA = 8
VMEM = 16 << 20
BF = jnp.bfloat16
F32 = jnp.float32


def swap(value, axis, bits, name):
    with jax.named_scope(name):
        return lax.ppermute(value, axis, [(i, i ^ bits) for i in range(lax.axis_size(axis))])


def dot(left, right):
    return jnp.dot(left, right, preferred_element_type=F32)


def dot_last(left, right):
    return lax.dot_general(left, right, (((1,), (1,)), ((), ())), preferred_element_type=F32)


def dot_first(left, right):
    return lax.dot_general(left, right, (((0,), (0,)), ((), ())), preferred_element_type=F32)


def kernel_call(name, body, outs, args, scratch=(), flops=0, space=pltpu.VMEM):
    size = sum(math.prod(a.shape) * a.dtype.itemsize for a in list(args) + list(outs))
    whole = pl.BlockSpec(memory_space=pltpu.VMEM)
    return pl.pallas_call(
        body,
        out_shape=tuple(outs),
        in_specs=[pl.BlockSpec(memory_space=space)] * len(args),
        out_specs=tuple([whole] * len(outs)),
        scratch_shapes=list(scratch),
        name=name,
        compiler_params=pltpu.CompilerParams(vmem_limit_bytes=VMEM),
        cost_estimate=pl.CostEstimate(flops=flops, bytes_accessed=size, transcendentals=0),
    )(*args)


def like(shape, dtype=BF):
    return jax.ShapeDtypeStruct(shape, dtype)


def norm_forward(value, gain, shift):
    centered = value - jnp.mean(value, axis=-1, keepdims=True)
    variance = jnp.mean(centered * centered, axis=-1, keepdims=True)
    inv_std = lax.rsqrt(variance + EPS)
    normal_part = centered * inv_std
    return (normal_part * gain + shift, normal_part, inv_std)


def norm_backward(grad_out, normal_part, inv_std, gain):
    scaled = grad_out * gain
    mean_one = jnp.mean(scaled, axis=-1, keepdims=True)
    mean_two = jnp.mean(scaled * normal_part, axis=-1, keepdims=True)
    grad_in = inv_std * (scaled - mean_one - normal_part * mean_two)
    return (
        grad_in,
        jnp.sum(grad_out * normal_part, axis=0, keepdims=True),
        jnp.sum(grad_out, axis=0, keepdims=True),
    )


def extra_rows(*rows):
    width = rows[0].shape[1]
    return jnp.concatenate(list(rows) + [jnp.zeros((EXTRA - len(rows), width), F32)]).astype(BF)


def whole_matrix(pieces, plan, scratch):
    if len(pieces) == 1:
        return pieces[0][...]
    me = lax.axis_index("blk")
    rows, width = scratch.shape[1:]
    for piece, (sources, at) in zip(pieces, plan):
        for k, source in enumerate(sources):
            if len(piece.shape) == 3:
                scratch[me ^ source] = piece[k, :, at : at + width]
            else:
                scratch[me ^ source] = piece[k * rows : (k + 1) * rows, at : at + width]
    return scratch[...].reshape(-1, width)


def order(value, *after):
    return lax.optimization_barrier((value,) + after)[0]


def piece_scratch(pieces, width):
    if len(pieces) == 1:
        return pltpu.VMEM((8, 128), BF)
    return pltpu.VMEM((8, pieces[0].shape[-2], width), BF)


def places(tag_row, n, per_block, rows):
    target = tag_row // per_block
    onehot = lax.broadcasted_iota(jnp.int32, (n, rows), 0) == target
    earlier = lax.broadcasted_iota(jnp.int32, (rows, rows), 0) < lax.broadcasted_iota(
        jnp.int32, (rows, rows), 1
    )
    count = dot(onehot.astype(F32).astype(BF), earlier.astype(F32).astype(BF))
    rank = jnp.sum(jnp.where(onehot, count, 0.0), axis=0, keepdims=True).astype(jnp.int32)
    return target, rank


def fetch(sources, held, sems):
    copies = [
        pltpu.make_async_copy(source, to, sems.at[k])
        for k, (source, to) in enumerate(zip(sources, held))
    ]
    for copy in copies:
        copy.start()
    for copy in copies:
        copy.wait()


def pack_kernel(n, room, per_block, groups, *refs):
    count = 18
    sources, rest = refs[:count], refs[count:]
    held, sems = rest[-count - 1 : -1], rest[-1]
    *sends, attend_ref, ff_ref, vec_ref = rest[: -count - 1]
    fetch(sources, held, sems)
    for out, shards in ((attend_ref, held[:4]), (ff_ref, held[4:6])):
        at = 0
        for shard in shards:
            out[:, at : at + shard.shape[1]] = shard[...]
            at += shard.shape[1]
    x_ref, tag_ref, doc_ref, value_b, query_b, *vectors = held[6:]
    blank = jnp.zeros((1, value_b.shape[0]), F32)
    biases = [blank, value_b[...].reshape(1, -1), query_b[...].reshape(1, -1), blank]
    vec_ref[...] = jnp.concatenate(
        [jnp.concatenate(biases, axis=1)] + [item[...].reshape(1, -1) for item in vectors]
    )
    rows, width = x_ref.shape
    share = room // groups
    target, rank = places(tag_ref[...], n, per_block, rows)
    offset = rank - lax.axis_index("head") * share
    inside = (offset >= 0) & (offset < share)
    code = (1 + doc_ref[...] * per_block + tag_ref[...] % per_block).astype(F32)
    if len(sends) == 1:
        (out_ref,) = sends
        place = jnp.where(inside, target * share + offset, -1)
        pick = lax.broadcasted_iota(jnp.int32, (n * share, rows), 0) == place
        out_ref[:, :width] = dot(pick.astype(F32).astype(BF), x_ref[...]).astype(BF)
        code = jnp.sum(jnp.where(pick, code, 0.0), axis=1, keepdims=True)
        out_ref[:, width:] = jnp.broadcast_to(code, (n * share, META)).astype(BF)
        return
    odd = lax.axis_index("blk") % 2
    for t, out_ref in enumerate(sends):
        there = inside & (target % 2 == odd ^ t)
        place = jnp.where(there, target // 2 * share + offset, -1)
        pick = lax.broadcasted_iota(jnp.int32, (4 * share, rows), 0) == place
        out_ref[: 4 * share, :] = dot(pick.astype(F32).astype(BF), x_ref[...]).astype(BF)
        level = lax.broadcasted_iota(jnp.int32, (EXTRA, rows), 0)
        codes = jnp.where(there & (target // 2 == level), code, 0.0).astype(BF)
        spot = lax.broadcasted_iota(jnp.int32, (META, rows), 0) == offset
        tile = dot_last(codes, spot.astype(F32).astype(BF)).astype(BF)
        out_ref[4 * share :, :META] = tile
        out_ref[4 * share :, META:] = jnp.zeros((EXTRA, width - META), BF)


def route_kernel(keep_ref, recv_ref, *outs):
    level = lax.axis_index("blk") // 2
    rows, share = 0, (keep_ref.shape[0] - EXTRA) // 4
    width = keep_ref.shape[1]
    lanes = lax.broadcasted_iota(jnp.int32, (EXTRA, META), 0)
    for k in range(4):
        z = level ^ k
        for t, ref in enumerate((keep_ref, recv_ref)):
            outs[k][rows + t * share : rows + (t + 1) * share, :] = ref[pl.ds(z * share, share), :]
        first = keep_ref[4 * share :, :META].astype(F32)
        second = recv_ref[4 * share :, :META].astype(F32)
        first = jnp.sum(jnp.where(lanes == z, first, 0.0), axis=0, keepdims=True)
        second = jnp.sum(jnp.where(lanes == z, second, 0.0), axis=0, keepdims=True)
        tile = jnp.where(lanes == 0, first, jnp.where(lanes == 1, second, 0.0))
        outs[k][rows + 2 * share :, :META] = tile.astype(BF)
        outs[k][rows + 2 * share :, META:] = jnp.zeros((EXTRA, width - META), BF)


def stack_kernel(*refs):
    out_ref, at = refs[-1], 0
    for ref in refs[:-1]:
        if len(ref.shape) == 3:
            out_ref[at : at + ref.shape[0]] = ref[...]
            at += ref.shape[0]
        else:
            out_ref[at] = ref[...]
            at += 1


def stack(name, *parts):
    count = sum(1 if part.ndim == 2 else part.shape[0] for part in parts)
    (out,) = kernel_call(name, stack_kernel, [like((count,) + parts[0].shape[-2:])], parts)
    return out


def slots_kernel(*refs):
    out_ref = refs[4]
    share, width = (refs[0].shape[0] - EXTRA) // 2, refs[0].shape[1]
    lane = lax.broadcasted_iota(jnp.int32, (2 * share, META), 1)
    row = lax.broadcasted_iota(jnp.int32, (2 * share, META), 0)
    for k, ref in enumerate(refs[:4]):
        at = slice(2 * k * share, 2 * (k + 1) * share)
        out_ref[at, :width] = ref[: 2 * share, :]
        codes = ref[2 * share :, :META].astype(F32)
        spread = jnp.where(row < share, codes[:1, :], codes[1:2, :])
        code = jnp.sum(jnp.where(lane == row % share, spread, 0.0), axis=1, keepdims=True)
        out_ref[at, width:] = jnp.broadcast_to(code, (2 * share, META)).astype(BF)


def attend_kernel(per_block, count, plan, *refs):
    x_ref, tag_ref, doc_ref, bias_ref = refs[:4]
    parts = refs[4:8]
    pieces = refs[8 : 8 + count]
    mine_ref, theirs_ref, a_ref, q_ref, kv_ref, mask_ref, stat_ref, scratch, y_ref = refs[
        8 + count :
    ]
    rows, width = x_ref.shape
    local = a_ref.shape[1]
    slots = kv_ref.shape[0] - rows
    step = slots // 4
    me = lax.axis_index("blk")
    core = lax.axis_index("head") % 2
    weight = whole_matrix(pieces, plan, scratch)
    own = dot(x_ref[...], weight[:, : 3 * local]) + bias_ref[:1, : 3 * local]
    q_ref[...] = own[:, 2 * local :].astype(BF)
    kv_ref[slots:, :] = own[:, : 2 * local].astype(BF)
    row_cluster = lax.broadcasted_iota(jnp.int32, (1, rows), 1) // CLUSTER
    wanted = (1 + doc_ref[...] * per_block + row_cluster).astype(F32)
    for k in range(4):
        part = parts[k]
        kv_ref[k * step : (k + 1) * step, :] = (
            dot(part[:, :width], weight[:, : 2 * local]) + bias_ref[:1, : 2 * local]
        ).astype(BF)
        code = part[:, width : width + 1].astype(F32)
        mask_ref[k * step : (k + 1) * step, :] = jnp.where(code == wanted, 0.0, NEG).astype(BF)
    alone = tag_ref[...] != me * per_block + row_cluster
    diagonal = lax.broadcasted_iota(jnp.int32, (rows, rows), 0) == lax.broadcasted_iota(
        jnp.int32, (rows, rows), 1
    )
    mask_ref[slots:, :] = jnp.where(diagonal & alone, 0.0, NEG).astype(BF)
    mask = mask_ref[...].astype(F32)
    stats = []
    for j in range(local // DH):
        cut = slice(j * DH, (j + 1) * DH)
        scores = dot_last(kv_ref[:, cut], q_ref[:, cut]) * SCALE + mask
        top = jnp.max(scores, axis=0, keepdims=True)
        weights = jnp.exp(scores - top)
        inverse = 1.0 / jnp.sum(weights, axis=0, keepdims=True)
        probs = (weights * inverse).astype(BF)
        value = kv_ref[:, local + j * DH : local + (j + 1) * DH]
        a_ref[:, cut] = dot_first(probs, value).astype(BF)
        stats += [top, inverse]
    stat_ref[...] = jnp.concatenate(stats + [jnp.zeros((8 - len(stats), rows), F32)])
    y_ref[...] = dot_last(a_ref[...], weight[:, 3 * local :])
    half = rows // 2
    mine_ref[...] = y_ref[pl.ds(core * half, half), :]
    theirs_ref[...] = y_ref[pl.ds((1 - core) * half, half), :].astype(BF)


def attend_back_kernel(n, count, plan, *refs):
    own_ref, other_ref, q_ref, kv_ref, mask_ref, stat_ref = refs[:6]
    pieces = refs[6 : 6 + count]
    eb_ref, dq_ref, dkv_ref = refs[6 + count : 9 + count]
    back, scratch = refs[9 + count : -1], refs[-1]
    rows, local = q_ref.shape
    slots = kv_ref.shape[0] - rows
    half = rows // 2
    core = lax.axis_index("head") % 2
    weight = whole_matrix(pieces, plan, scratch)
    eb_ref[pl.ds(core * half, half), :] = own_ref[:half, :]
    eb_ref[pl.ds((1 - core) * half, half), :] = other_ref[:half, :]
    da = dot(eb_ref[...], weight[:, 3 * local :]).astype(BF)
    mask = mask_ref[...].astype(F32)
    for j in range(local // DH):
        cut = slice(j * DH, (j + 1) * DH)
        key, query = kv_ref[:, cut], q_ref[:, cut]
        value = kv_ref[:, local + j * DH : local + (j + 1) * DH]
        scores = dot_last(key, query) * SCALE + mask
        probs = jnp.exp(scores - stat_ref[2 * j : 2 * j + 1, :]) * stat_ref[
            2 * j + 1 : 2 * j + 2, :
        ]
        low = probs.astype(BF)
        dkv_ref[:, local + j * DH : local + (j + 1) * DH] = dot(low, da[:, cut]).astype(BF)
        grad = dot_last(value, da[:, cut])
        delta = jnp.sum(low.astype(F32) * grad, axis=0, keepdims=True)
        grad = (probs * (grad - delta)).astype(BF)
        dkv_ref[:, cut] = (dot(grad, query) * SCALE).astype(BF)
        dq_ref[:, cut] = (dot_first(grad, key) * SCALE).astype(BF)
    if back:
        share = slots // 4 // n
        for t in range(2):
            for z in range(4):
                for k in range(4):
                    at = k * slots // 4 + (2 * z + t) * share
                    to = (z * 4 + k) * share
                    back[t][to : to + share, :] = dkv_ref[at : at + share, :]


def back_kernel(room, left_ref, right_ref, keep_ref, send_ref):
    for k in range(left_ref.shape[0] // room):
        out, to = (send_ref if k % 2 else keep_ref), k // 2 * 2 * room
        out[to : to + room, :] = left_ref[k * room : (k + 1) * room, :]
        out[to + room : to + 2 * room, :] = right_ref[k * room : (k + 1) * room, :]


def token_kernel(n, room, per_block, parts, count, plan, *refs):
    tag_ref, dkv_ref, dq_ref = refs[:3]
    back = refs[3 : 3 + parts]
    pieces = refs[3 + parts : 3 + parts + count]
    mine_ref, theirs_ref, scratch, z_ref = refs[3 + parts + count :]
    rows, local = dq_ref.shape
    slots = n * room
    half = rows // 2
    share = room // 4
    group = lax.axis_index("head")
    core = group % 2
    weight = whole_matrix(pieces, plan, scratch)
    target, rank = places(tag_ref[...], n, per_block, rows)
    if parts > 1:
        target = target ^ lax.axis_index("blk")
    place = target * room + ((rank // share) ^ group) * share + rank % share
    total = dkv_ref[slots:, :].astype(F32)
    step = slots // parts
    for k in range(parts):
        pick = lax.broadcasted_iota(jnp.int32, (step, rows), 0) + k * step == place
        total = total + dot_first(pick.astype(F32).astype(BF), back[k][...])
    z_ref[...] = dot_last(total.astype(BF), weight[:, : 2 * local]) + dot_last(
        dq_ref[...], weight[:, 2 * local : 3 * local]
    )
    mine_ref[...] = z_ref[pl.ds(core * half, half), :]
    theirs_ref[...] = z_ref[pl.ds((1 - core) * half, half), :].astype(BF)


def norm_one_kernel(
    chip_ref, recv_ref, x_ref, vec_ref, h_ref, n_ref, r_ref, hb_ref
):
    half = chip_ref.shape[0]
    core = lax.axis_index("head") % 2
    branch = chip_ref[...].astype(F32) + recv_ref[...].astype(F32) + vec_ref[1:2, :]
    value = x_ref[pl.ds(core * half, half), :].astype(F32) + branch
    h, normal, inverse = norm_forward(value, vec_ref[2:3, :], vec_ref[3:4, :])
    h_ref[...] = h
    n_ref[...] = normal
    r_ref[...] = inverse
    hb_ref[...] = h.astype(BF)


def norm_two_kernel(
    chip_ref, recv_ref, h_ref, vec_ref, c_ref, out_ref, e_ref, eb_ref
):
    half = chip_ref.shape[0]
    core = lax.axis_index("head") % 2
    outer = chip_ref[...].astype(F32) + recv_ref[...].astype(F32) + vec_ref[4:5, :]
    gain_row = vec_ref[5:6, :]
    result, normal, inverse = norm_forward(h_ref[...] + outer, gain_row, vec_ref[6:7, :])
    out_ref[...] = result.astype(BF)
    cotangent = c_ref[pl.ds(core * half, half), :].astype(F32)
    grad, gain, shift = norm_backward(cotangent, normal, inverse, gain_row)
    e_ref[...] = grad
    eb_ref[:half, :] = grad.astype(BF)
    eb_ref[half:, :] = extra_rows(gain, shift)


def norm_back_kernel(chip_ref, recv_ref, e_ref, n_ref, r_ref, vec_ref, out_ref, eb_ref):
    half = chip_ref.shape[0]
    grad = e_ref[...] + (chip_ref[...].astype(F32) + recv_ref[...].astype(F32))
    grad, gain, shift = norm_backward(grad, n_ref[...], r_ref[...], vec_ref[2:3, :])
    out_ref[...] = grad
    eb_ref[:half, :] = grad.astype(BF)
    eb_ref[half:, :] = extra_rows(gain, shift)


def inner_kernel(count, plan, *refs):
    own_ref, other_ref, bias_ref = refs[:3]
    pieces = refs[3 : 3 + count]
    g_ref, slope_ref, scratch = refs[3 + count :]
    half = own_ref.shape[0]
    weight = whole_matrix(pieces, plan, scratch)
    for k, part in enumerate((own_ref, other_ref)):
        u = dot(part[...], weight) + bias_ref[7:8, :]
        below = 0.5 * (1.0 + lax.erf(u * math.sqrt(0.5)))
        g_ref[k * half : (k + 1) * half, :] = (u * below).astype(BF)
        density = jnp.exp(-0.5 * u * u) * (1.0 / math.sqrt(2.0 * math.pi))
        slope_ref[k * half : (k + 1) * half, :] = below + u * density


def outer_kernel(count, plan, *refs):
    g_ref = refs[0]
    pieces = refs[1 : 1 + count]
    mine_ref, theirs_ref, scratch = refs[1 + count :]
    half = mine_ref.shape[0]
    weight = whole_matrix(pieces, plan, scratch)
    mine_ref[...] = dot_last(g_ref[:half, :], weight)
    theirs_ref[...] = dot_last(g_ref[half:, :], weight).astype(BF)


def ff_back_kernel(outer_plan, inner_plan, outer_count, inner_count, *refs):
    own_ref, other_ref, slope_ref = refs[:3]
    outer, inner = refs[3 : 3 + outer_count], refs[3 + outer_count :][:inner_count]
    mine_ref, theirs_ref, du_ref, scratch, scratch_two = refs[3 + outer_count + inner_count :]
    half = mine_ref.shape[0]
    outer = whole_matrix(outer, outer_plan, scratch)
    inner = whole_matrix(inner, inner_plan, scratch_two)
    for k, part in ((1, other_ref), (0, own_ref)):
        rows = slice(k * half, (k + 1) * half)
        dg = dot(part[:half, :], outer).astype(BF).astype(F32)
        du_ref[rows, :] = (dg * slope_ref[rows, :]).astype(BF)
        dh = dot_last(du_ref[rows, :], inner)
        if k:
            theirs_ref[...] = dh.astype(BF)
        else:
            mine_ref[...] = dh


def halves(blocks, bit):
    return [b for b in blocks if not b & bit], [b for b in blocks if b & bit]


def split_pieces(total, bit, mine_ref, theirs_ref):
    me = lax.axis_index("blk")
    rows = total.shape[0] // 8
    for out, blocks in zip((mine_ref, theirs_ref), halves(range(8), bit)):
        for k, block in enumerate(blocks):
            out[k * rows : (k + 1) * rows, :] = total[pl.ds((me ^ block) * rows, rows), :].astype(BF)


def ff_weights_kernel(small, own_ref, other_ref, left_ref, *refs):
    half = left_ref.shape[0] // 2
    refs = list(refs)
    total = refs.pop()
    total[...] = dot_first(own_ref[:half, :], left_ref[:half, :]) + dot_first(
        other_ref[:half, :], left_ref[half:, :]
    )
    if small == "outer":
        small_ref = refs.pop()
        norms = own_ref[half:, :].astype(F32) + other_ref[half:, :].astype(F32)
        bias = jnp.sum(own_ref[:half, :].astype(F32), axis=0, keepdims=True) + jnp.sum(
            other_ref[:half, :].astype(F32), axis=0, keepdims=True
        )
        small_ref[...] = jnp.concatenate([norms[:2], bias, jnp.zeros((5, bias.shape[1]), F32)])
    else:
        small_ref = refs.pop()
        bias = jnp.sum(left_ref[...].astype(F32), axis=0, keepdims=True)
        small_ref[...] = jnp.concatenate([bias, jnp.zeros((7, bias.shape[1]), F32)])
    if len(refs) == 1:
        refs[0][...] = total[...]
    else:
        split_pieces(total, 1 if small == "outer" else 2, *refs)


def attend_weights_kernel(*refs):
    x_ref, p0, p1, p2, p3, dkv_ref, dq_ref, eb_ref, a_ref, own_ref, other_ref = refs[:11]
    outer_ref, inner_ref = refs[11:13]
    outs, total = list(refs[13:-1]), refs[-1]
    rows, width = x_ref.shape
    local = dq_ref.shape[1]
    slots = dkv_ref.shape[0] - rows
    step = slots // 4
    sums = dot_first(x_ref[...], dkv_ref[slots:, :])
    for k, part in enumerate((p0, p1, p2, p3)):
        sums = sums + dot_first(part[:, :width], dkv_ref[k * step : (k + 1) * step, :])
    total[:, : 2 * local] = sums
    total[:, 2 * local : 3 * local] = dot_first(x_ref[...], dq_ref[...])
    total[:, 3 * local :] = dot_first(eb_ref[...], a_ref[...])
    half = rows // 2
    norms = own_ref[half:, :].astype(F32) + other_ref[half:, :].astype(F32)
    output_b = jnp.sum(eb_ref[...].astype(F32), axis=0, keepdims=True)
    query_b = jnp.sum(dq_ref[...].astype(F32), axis=0, keepdims=True)
    value_b = jnp.sum(dkv_ref[...].astype(F32), axis=0, keepdims=True)
    last = jnp.concatenate([value_b, query_b, jnp.zeros((1, width - 3 * local), F32)], axis=1)
    small = jnp.concatenate(
        [
            outer_ref[:3, :],
            inner_ref[:1, :],
            norms[:2],
            output_b,
            last,
        ]
    )
    if outs[0].shape == total.shape:
        outs[0][...] = total[...]
        outs[1][...] = small
    else:
        split_pieces(total, 1, *outs)
        body = outs[0].shape[0] - EXTRA
        outs[0][body:, :] = small.astype(BF)
        outs[1][body:, :] = small.astype(BF)


def middle_kernel(extra, blocks, bit, mine_ref, recv_ref, *outs):
    rows = (mine_ref.shape[0] - extra) // len(blocks)
    last = mine_ref.shape[0] - extra
    for out, pieces in zip(outs, halves(blocks, bit)):
        for k, piece in enumerate(pieces):
            at = slice(blocks.index(piece) * rows, (blocks.index(piece) + 1) * rows)
            out[k * rows : (k + 1) * rows, :] = (
                mine_ref[at, :].astype(F32) + recv_ref[at, :].astype(F32)
            ).astype(BF)
        if extra:
            small = mine_ref[last:, :].astype(F32) + recv_ref[last:, :].astype(F32)
            out[len(pieces) * rows :, :] = small.astype(BF)


def pair_kernel(*refs):
    inputs, keeps, send_ref = refs[:4], refs[4:6], refs[6]
    rows = keeps[0].shape[0]
    for k, keep_ref in enumerate(keeps):
        mine_ref, recv_ref = inputs[2 * k : 2 * k + 2]
        total = (mine_ref[...].astype(F32) + recv_ref[...].astype(F32)).astype(BF)
        keep_ref[...] = total[:rows, :]
        send_ref[k * rows : (k + 1) * rows, :] = total[rows:, :]


def last_pair_kernel(first_ref, second_ref, recv_ref, *outs):
    rows = first_ref.shape[0]
    for k, ref in enumerate((first_ref, second_ref)):
        recv = recv_ref[k * rows : (k + 1) * rows, :]
        outs[k][...] = ref[...].astype(F32) + recv.astype(F32)


def last_kernel(left_ref, right_ref, *outs):
    total = left_ref[...].astype(F32) + right_ref[...].astype(F32)
    if len(outs) == 1:
        outs[0][...] = total
        return
    rows, local = outs[0].shape
    for k in range(4):
        outs[k][...] = total[:rows, k * local : (k + 1) * local]
    spread_small(total[rows:, :], local, outs[4:])


def spread_small(small, local, outs):
    for k, out in enumerate(outs[:7]):
        out[...] = small[k, :]
    outs[7][...] = small[7, 2 * local : 3 * local]
    outs[8][...] = small[7, local : 2 * local]


def small_kernel(small_ref, *outs):
    spread_small(small_ref[...], outs[7].shape[0], outs)


def scatter_step(name, mine, recv, blocks, bit, extra=0):
    rows = (mine.shape[0] - extra) // 2 + extra
    return kernel_call(
        name,
        functools.partial(middle_kernel, extra, blocks, bit),
        [like((rows, mine.shape[1]))] * 2,
        [mine, recv],
    )


def chip_sum(mine, theirs, name):
    chip = (mine + swap(theirs, "head", 1, name + "_chip").astype(F32)).astype(BF)
    return chip, swap(chip, "head", 2, name + "_x")


def per_device(
    hidden_in,
    query_w,
    key_w,
    value_w,
    output_w,
    inner_w,
    outer_w,
    query_b,
    value_b,
    output_b,
    inner_b,
    outer_b,
    first_gain,
    first_shift,
    second_gain,
    second_shift,
    key_cluster,
    document,
    cotangent,
):
    rows, width = hidden_in.shape
    n = lax.axis_size("blk")
    groups = lax.axis_size("head")
    assert groups == 4
    local = query_w.shape[1]
    units = inner_w.shape[1]
    per_block = rows // CLUSTER
    room = 2 * rows // n
    slots = n * room
    half = rows // 2
    share = room // groups
    staged = n == 8
    core = lax.axis_index("head") % 2

    tag_row, doc_row = key_cluster.reshape(1, rows), document.reshape(1, rows)

    if staged:
        sends = [like((4 * share + EXTRA, width))] * 2
    else:
        sends = [like((n * share, width + META))]
    pack_args = [key_w, value_w, query_w, output_w, inner_w, outer_w]
    pack_args += [hidden_in, tag_row, doc_row, value_b, query_b, output_b]
    pack_args += [first_gain, first_shift, outer_b, second_gain, second_shift, inner_b]
    *sent, attend_w, ff_w, vectors = kernel_call(
        "pack",
        functools.partial(pack_kernel, n, room, per_block, groups),
        sends
        + [
            like((width // n, 4 * local)),
            like((width // n, 2 * units)),
            like((8, width), F32),
        ],
        [pltpu.with_memory_space_constraint(item, pltpu.HBM) for item in pack_args],
        [pltpu.VMEM(item.shape, item.dtype) for item in pack_args]
        + [pltpu.SemaphoreType.DMA((len(pack_args),))],
        flops=2 * n * share * rows * width,
        space=pltpu.HBM,
    )
    if staged:
        attend_column = [
            swap(attend_w, "blk", bits, f"attend_w_z{bits}") for bits in (2, 4, 6)
        ]
        slots_y = swap(sent[1], "blk", 1, "slots_y")
        messages = kernel_call(
            "route", route_kernel, [like((2 * share + EXTRA, width))] * 4, [sent[0], slots_y]
        )
        arrived = [messages[0]] + [
            swap(messages[k], "blk", 2 * k, f"slots_z{2 * k}") for k in (1, 2, 3)
        ]
        (moved,) = kernel_call("slots", slots_kernel, [like((n * share, width + META))], arrived)
        column = order(attend_column, messages[0])
        column = stack("attend_w_column", attend_w, *column)
        rest = swap(column, "blk", 1, "attend_w_rest")
        attend_p = [attend_w] + attend_column + [rest]
        inner_far = swap(order(inner_w, *attend_column), "blk", 4, "inner_w_far")
        inner_near = swap(stack("inner_w_pair", inner_w, inner_far), "blk", 2, "inner_w_near")
        outer_far = swap(order(outer_w, inner_far), "blk", 4, "outer_w_far")
    else:
        moved = lax.all_to_all(sent[0].reshape(n, share, width + META), "blk", 0, 0)
        moved = moved.reshape(sent[0].shape)
        gather = lambda value: [lax.all_gather(value, "blk", axis=0, tiled=True)]
        attend_p, inner_p, outer_p = gather(attend_w), gather(inner_w), gather(outer_w)
    far = swap(moved, "head", 2, "slots_x")
    parts = [moved, swap(moved, "head", 1, "slots_chip"), far, swap(far, "head", 1, "slots_far")]
    attend_plan = [((0,), 0), ((2,), 0), ((4,), 0), ((6,), 0), ((1, 3, 5, 7), 0)]
    inner_plan = [((0,), 0), ((1,), 0), ((4,), 0), ((2, 6), 0), ((5, 3, 7), 0)]
    outer_plan = [((0,), 0), ((1,), units), ((4,), 0), ((2, 6), 0), ((5, 3, 7), 0)]

    count = len(attend_p)
    mine, theirs, a, q, kv, mask, stat = kernel_call(
        "attend",
        functools.partial(attend_kernel, per_block, count, attend_plan),
        [
            like((half, width), F32),
            like((half, width)),
            like((rows, local)),
            like((rows, local)),
            like((slots + rows, 2 * local)),
            like((slots + rows, rows)),
            like((8, rows), F32),
        ],
        [hidden_in, tag_row, doc_row, vectors] + parts + attend_p,
        [piece_scratch(attend_p, 4 * local), pltpu.VMEM((rows, width), F32)],
        flops=2 * rows * width * local * 9,
    )
    if staged:
        facing = swap(order(ff_w, far), "blk", 1, "facing_w")
        outer_far = order(outer_far, theirs)
        outer_near = swap(stack("outer_w_pair", outer_w, outer_far), "blk", 2, "outer_w_near")
        inner_rest = stack("inner_w_column", inner_far, inner_near)
        inner_rest = swap(inner_rest, "blk", 1, "inner_w_rest")
        outer_rest = stack("outer_w_column", outer_far, outer_near)
        outer_rest = swap(outer_rest, "blk", 1, "outer_w_rest")
        inner_p = [inner_w, facing, inner_far, inner_near, inner_rest]
        outer_p = [outer_w, facing, outer_far, outer_near, outer_rest]
        mine = order(mine, facing, outer_far)
    chip, recv = chip_sum(mine, theirs, "branch")
    if staged:
        recv = order(recv, outer_near)
    h, normal_one, inv_one, hb = kernel_call(
        "norm_one",
        norm_one_kernel,
        [
            like((half, width), F32),
            like((half, width), F32),
            like((half, 1), F32),
            like((half, width)),
        ],
        [chip, recv, hidden_in, vectors],
    )
    hb_other = swap(hb, "head", 1, "hb")

    g, slope = kernel_call(
        "inner",
        functools.partial(inner_kernel, len(inner_p), inner_plan),
        [like((rows, units)), like((rows, units), F32)],
        [hb, hb_other, vectors] + inner_p,
        [piece_scratch(inner_p, units)],
        flops=2 * rows * width * units,
    )
    mine, theirs = kernel_call(
        "outer",
        functools.partial(outer_kernel, len(outer_p), outer_plan),
        [like((half, width), F32), like((half, width))],
        [g] + outer_p,
        [piece_scratch(outer_p, units)],
        flops=2 * rows * width * units,
    )
    chip, recv = chip_sum(mine, theirs, "ff")
    result, e_two, eb_two = kernel_call(
        "norm_two",
        norm_two_kernel,
        [like((half, width)), like((half, width), F32), like((half + EXTRA, width))],
        [chip, recv, h, vectors, cotangent],
    )
    eb_two_other = swap(eb_two, "head", 1, "eb_two")
    mine, theirs, du = kernel_call(
        "ff_back",
        functools.partial(
            ff_back_kernel, outer_plan, inner_plan, len(outer_p), len(inner_p)
        ),
        [like((half, width), F32), like((half, width)), like((rows, units))],
        [eb_two, eb_two_other, slope] + outer_p + inner_p,
        [piece_scratch(outer_p, units), piece_scratch(inner_p, units)],
        flops=4 * rows * width * units,
    )
    if staged:
        grad_outs = [like((width // 2, units)), like((width // 2, units))]
    else:
        grad_outs = [like((width, units), F32)]
    outer_g = kernel_call(
        "outer_grad",
        functools.partial(ff_weights_kernel, "outer"),
        grad_outs + [like((8, width), F32)],
        [eb_two, eb_two_other, g],
        [pltpu.VMEM((width, units), F32)],
        flops=2 * rows * width * units,
    )
    mine = order(mine, outer_g[0])
    chip, recv = chip_sum(mine, theirs, "ff_back")
    inner_g = kernel_call(
        "inner_grad",
        functools.partial(ff_weights_kernel, "inner"),
        grad_outs + [like((8, units), F32)],
        [hb, hb_other, du],
        [pltpu.VMEM((width, units), F32)],
        flops=2 * rows * width * units,
    )
    recv = order(recv, outer_g[0], inner_g[0])
    grad_units = [like((width // n, units), F32)]
    if staged:
        outer_y = swap(outer_g[1], "blk", 1, "outer_g_y")
        inner_near = swap(inner_g[1], "blk", 2, "inner_g_near")
    else:
        grad_outer_w = lax.psum_scatter(outer_g[0], "blk", scatter_dimension=0, tiled=True)
        grad_inner_w = lax.psum_scatter(inner_g[0], "blk", scatter_dimension=0, tiled=True)

    e_one, eb_one = kernel_call(
        "norm_back",
        norm_back_kernel,
        [like((half, width), F32), like((half + EXTRA, width))],
        [chip, recv, e_two, normal_one, inv_one, vectors],
    )
    eb_one_other = swap(eb_one, "head", 1, "eb_one")
    back_outs = [like((slots // 2, 2 * local))] * 2 if staged else []
    eb_full, dq, dkv, *back = kernel_call(
        "attend_back",
        functools.partial(attend_back_kernel, n, count, attend_plan),
        [
            like((rows, width)),
            like((rows, local)),
            like((slots + rows, 2 * local)),
        ]
        + back_outs,
        [eb_one, eb_one_other, q, kv, mask, stat] + attend_p,
        [piece_scratch(attend_p, 4 * local)],
        flops=2 * rows * width * local * 8,
    )
    if staged:
        back_y = swap(back[1], "blk", 1, "back_y")
        outer_k, outer_s = scatter_step("outer_g_one", outer_g[0], outer_y, [0, 2, 4, 6], 2)
        inner_near = order(inner_near, outer_k)
        inner_k, inner_s = scatter_step("inner_g_one", inner_g[0], inner_near, [0, 1, 4, 5], 1)
        dq = order(dq, inner_k, outer_k)
        grad_outs = [like((width // 2 + EXTRA, width))] * 2
    else:
        grad_outs = [like((width, width), F32), like((EXTRA, width), F32)]
    attend_g = kernel_call(
        "attend_grad",
        attend_weights_kernel,
        grad_outs,
        [hidden_in] + parts + [dkv, dq, eb_full, a, eb_one, eb_one_other, outer_g[-1], inner_g[-1]],
        [pltpu.VMEM((width, width), F32)],
        flops=2 * rows * width * local * 8,
    )
    if staged:
        back_y = order(back_y, attend_g[1])
        attend_y = swap(order(attend_g[1], back_y), "blk", 1, "attend_g_y")
        half_slots = [like((slots // 2, 2 * local))] * 2
        back_k, back_s = kernel_call(
            "back_one", functools.partial(back_kernel, room), half_slots, [back[0], back_y]
        )
        back_near = swap(back_s, "blk", 2, "back_near")
        outer_near = swap(order(outer_s, back_near), "blk", 2, "outer_g_near")
        inner_y = swap(inner_s, "blk", 1, "inner_g_y")
        back_k, back_s = kernel_call(
            "back_two", functools.partial(back_kernel, 2 * room), half_slots, [back_k, back_near]
        )
        moved = [back_k, swap(back_s, "blk", 4, "back_far")]
        attend_k, attend_s = scatter_step(
            "attend_g_one", attend_g[0], attend_y, [0, 2, 4, 6], 2, EXTRA
        )
        piece = like((width // n, units))
        inner_k, outer_k, both = kernel_call(
            "pair",
            pair_kernel,
            [piece, piece, like((2 * width // n, units))],
            [inner_k, inner_y, outer_k, outer_near],
        )
        moved[0] = order(moved[0], attend_k)
        both = swap(order(both, moved[1]), "blk", 4, "both_far")
        grad_inner_w, grad_outer_w = kernel_call(
            "pair_last", last_pair_kernel, grad_units * 2, [inner_k, outer_k, both]
        )
    else:
        moved = dkv[:slots].reshape(4, n, share, 2 * local).transpose(1, 0, 2, 3)
        moved = lax.all_to_all(moved, "blk", 0, 0).reshape(slots, 2 * local)
        moved = [moved]
    mine, theirs = kernel_call(
        "token",
        functools.partial(
            token_kernel, n, room, per_block, len(moved), count, attend_plan
        ),
        [like((half, width), F32), like((half, width))],
        [tag_row, dkv, dq] + moved + attend_p,
        [piece_scratch(attend_p, 4 * local), pltpu.VMEM((rows, width), F32)],
        flops=2 * rows * width * local * 4,
    )
    if staged:
        mine = order(mine, inner_k)
    chip, recv = chip_sum(mine, theirs, "last")
    if staged:
        attend_near = swap(attend_s, "blk", 2, "attend_g_near")
        attend_k, attend_s = scatter_step(
            "attend_g_two", attend_k, attend_near, [0, 4], 4, EXTRA
        )
        recv = order(recv, attend_k, grad_inner_w)
    last = e_one + (chip.astype(F32) + recv.astype(F32))
    last_other = swap(last, "head", 1, "last")
    result_other = swap(result, "head", 1, "result")

    def joined(own, other):
        return jnp.where(
            core == 0, jnp.concatenate([own, other]), jnp.concatenate([other, own])
        )

    layer_out = joined(result, result_other)
    grad_input = joined(last, last_other)
    small_outs = [like((width,), F32)] * 7 + [like((local,), F32)] * 2
    if staged:
        attend_far = swap(attend_s, "blk", 4, "attend_g_far")
        attend_far = order(attend_far, grad_input, layer_out)
        grads = kernel_call(
            "attend_g_last",
            last_kernel,
            [like((width // n, local), F32)] * 4 + small_outs,
            [attend_k, attend_far],
        )
        grads, small = grads[:4], grads[4:]
    else:
        summed = lax.psum_scatter(attend_g[0], "blk", scatter_dimension=0, tiled=True)
        grads = [summed[:, k * local : (k + 1) * local] for k in range(4)]
        small = kernel_call("small", small_kernel, small_outs, [lax.psum(attend_g[1], "blk")])
    grad_key_w, grad_value_w, grad_query_w, grad_output_w = grads

    return (
        layer_out,
        grad_input,
        grad_query_w,
        grad_key_w,
        grad_value_w,
        grad_output_w,
        grad_inner_w,
        grad_outer_w,
        small[7],
        small[8],
        small[6],
        small[3],
        small[2],
        small[4],
        small[5],
        small[0],
        small[1],
    )


def solution(mesh):
    matrix = P("blk", "head")
    in_specs = (
        (P("blk", None),)
        + (matrix,) * 6
        + (P("head"), P("head"), P(), P("head"))
        + (P(),) * 5
        + (P("blk"), P("blk"), P("blk", None))
    )
    out_specs = (
        (P("blk", None), P("blk", None))
        + (matrix,) * 6
        + (P("head"), P("head"), P(), P("head"))
        + (P(),) * 5
    )
    return jax.shard_map(
        per_device, mesh=mesh, in_specs=in_specs, out_specs=out_specs, check_vma=False
    )
```

```python
import functools
import math

import jax
import jax.numpy as jnp
from jax import lax
from jax.experimental import pallas as pl
from jax.experimental.pallas import tpu as pltpu
from jax.sharding import PartitionSpec as P

DH = 64
CLUSTER = 128
EPS = 1e-06
NEG = -1e30
SCALE = 1.0 / math.sqrt(DH)
META = 128
EXTRA = 8
VMEM = 16 << 20
BF = jnp.bfloat16
F32 = jnp.float32


def swap(value, axis, bits, name):
    with jax.named_scope(name):
        return lax.ppermute(value, axis, [(i, i ^ bits) for i in range(lax.axis_size(axis))])


def dot(left, right):
    return jnp.dot(left, right, preferred_element_type=F32)


def dot_last(left, right):
    return lax.dot_general(left, right, (((1,), (1,)), ((), ())), preferred_element_type=F32)


def dot_first(left, right):
    return lax.dot_general(left, right, (((0,), (0,)), ((), ())), preferred_element_type=F32)


def kernel_call(name, body, outs, args, scratch=(), flops=0, space=pltpu.VMEM):
    size = sum(math.prod(a.shape) * a.dtype.itemsize for a in list(args) + list(outs))
    whole = pl.BlockSpec(memory_space=pltpu.VMEM)
    return pl.pallas_call(
        body,
        out_shape=tuple(outs),
        in_specs=[pl.BlockSpec(memory_space=space)] * len(args),
        out_specs=tuple([whole] * len(outs)),
        scratch_shapes=list(scratch),
        name=name,
        compiler_params=pltpu.CompilerParams(vmem_limit_bytes=VMEM),
        cost_estimate=pl.CostEstimate(flops=flops, bytes_accessed=size, transcendentals=0),
    )(*args)


def like(shape, dtype=BF):
    return jax.ShapeDtypeStruct(shape, dtype)


def norm_forward(value, gain, shift):
    centered = value - jnp.mean(value, axis=-1, keepdims=True)
    variance = jnp.mean(centered * centered, axis=-1, keepdims=True)
    inv_std = lax.rsqrt(variance + EPS)
    normal_part = centered * inv_std
    return (normal_part * gain + shift, normal_part, inv_std)


def norm_backward(grad_out, normal_part, inv_std, gain):
    scaled = grad_out * gain
    mean_one = jnp.mean(scaled, axis=-1, keepdims=True)
    mean_two = jnp.mean(scaled * normal_part, axis=-1, keepdims=True)
    grad_in = inv_std * (scaled - mean_one - normal_part * mean_two)
    return (
        grad_in,
        jnp.sum(grad_out * normal_part, axis=0, keepdims=True),
        jnp.sum(grad_out, axis=0, keepdims=True),
    )


def extra_rows(*rows):
    width = rows[0].shape[1]
    return jnp.concatenate(list(rows) + [jnp.zeros((EXTRA - len(rows), width), F32)]).astype(BF)


def whole_matrix(pieces, plan, scratch):
    if len(pieces) == 1:
        return pieces[0][...]
    me = lax.axis_index("blk")
    rows, width = scratch.shape[1:]
    for piece, (sources, at) in zip(pieces, plan):
        for k, source in enumerate(sources):
            if len(piece.shape) == 3:
                scratch[me ^ source] = piece[k, :, at : at + width]
            else:
                scratch[me ^ source] = piece[k * rows : (k + 1) * rows, at : at + width]
    return scratch[...].reshape(-1, width)


def order(value, *after):
    return lax.optimization_barrier((value,) + after)[0]


def piece_scratch(pieces, width):
    if len(pieces) == 1:
        return pltpu.VMEM((8, 128), BF)
    return pltpu.VMEM((8, pieces[0].shape[-2], width), BF)


def places(tag_row, n, per_block, rows):
    target = tag_row // per_block
    onehot = lax.broadcasted_iota(jnp.int32, (n, rows), 0) == target
    earlier = lax.broadcasted_iota(jnp.int32, (rows, rows), 0) < lax.broadcasted_iota(
        jnp.int32, (rows, rows), 1
    )
    count = dot(onehot.astype(F32).astype(BF), earlier.astype(F32).astype(BF))
    rank = jnp.sum(jnp.where(onehot, count, 0.0), axis=0, keepdims=True).astype(jnp.int32)
    return target, rank


def fetch(sources, held, sems):
    copies = [
        pltpu.make_async_copy(source, to, sems.at[k])
        for k, (source, to) in enumerate(zip(sources, held))
    ]
    for copy in copies:
        copy.start()
    for copy in copies:
        copy.wait()


def pack_kernel(n, room, per_block, groups, *refs):
    count = 18
    sources, rest = refs[:count], refs[count:]
    held, sems = rest[-count - 1 : -1], rest[-1]
    *sends, attend_ref, ff_ref, vec_ref = rest[: -count - 1]
    fetch(sources, held, sems)
    for out, shards in ((attend_ref, held[:4]), (ff_ref, held[4:6])):
        at = 0
        for shard in shards:
            out[:, at : at + shard.shape[1]] = shard[...]
            at += shard.shape[1]
    x_ref, tag_ref, doc_ref, value_b, query_b, *vectors = held[6:]
    blank = jnp.zeros((1, value_b.shape[0]), F32)
    biases = [blank, value_b[...].reshape(1, -1), query_b[...].reshape(1, -1), blank]
    vec_ref[...] = jnp.concatenate(
        [jnp.concatenate(biases, axis=1)] + [item[...].reshape(1, -1) for item in vectors]
    )
    rows, width = x_ref.shape
    share = room // groups
    target, rank = places(tag_ref[...], n, per_block, rows)
    offset = rank - lax.axis_index("head") * share
    inside = (offset >= 0) & (offset < share)
    code = (1 + doc_ref[...] * per_block + tag_ref[...] % per_block).astype(F32)
    if len(sends) == 1:
        (out_ref,) = sends
        place = jnp.where(inside, target * share + offset, -1)
        pick = lax.broadcasted_iota(jnp.int32, (n * share, rows), 0) == place
        out_ref[:, :width] = dot(pick.astype(F32).astype(BF), x_ref[...]).astype(BF)
        code = jnp.sum(jnp.where(pick, code, 0.0), axis=1, keepdims=True)
        out_ref[:, width:] = jnp.broadcast_to(code, (n * share, META)).astype(BF)
        return
    odd = lax.axis_index("blk") % 2
    for t, out_ref in enumerate(sends):
        there = inside & (target % 2 == odd ^ t)
        place = jnp.where(there, target // 2 * share + offset, -1)
        pick = lax.broadcasted_iota(jnp.int32, (4 * share, rows), 0) == place
        out_ref[: 4 * share, :] = dot(pick.astype(F32).astype(BF), x_ref[...]).astype(BF)
        level = lax.broadcasted_iota(jnp.int32, (EXTRA, rows), 0)
        codes = jnp.where(there & (target // 2 == level), code, 0.0).astype(BF)
        spot = lax.broadcasted_iota(jnp.int32, (META, rows), 0) == offset
        tile = dot_last(codes, spot.astype(F32).astype(BF)).astype(BF)
        out_ref[4 * share :, :META] = tile
        out_ref[4 * share :, META:] = jnp.zeros((EXTRA, width - META), BF)


def route_kernel(keep_ref, recv_ref, *outs):
    level = lax.axis_index("blk") // 2
    rows, share = 0, (keep_ref.shape[0] - EXTRA) // 4
    width = keep_ref.shape[1]
    lanes = lax.broadcasted_iota(jnp.int32, (EXTRA, META), 0)
    for k in range(4):
        z = level ^ k
        for t, ref in enumerate((keep_ref, recv_ref)):
            outs[k][rows + t * share : rows + (t + 1) * share, :] = ref[pl.ds(z * share, share), :]
        first = keep_ref[4 * share :, :META].astype(F32)
        second = recv_ref[4 * share :, :META].astype(F32)
        first = jnp.sum(jnp.where(lanes == z, first, 0.0), axis=0, keepdims=True)
        second = jnp.sum(jnp.where(lanes == z, second, 0.0), axis=0, keepdims=True)
        tile = jnp.where(lanes == 0, first, jnp.where(lanes == 1, second, 0.0))
        outs[k][rows + 2 * share :, :META] = tile.astype(BF)
        outs[k][rows + 2 * share :, META:] = jnp.zeros((EXTRA, width - META), BF)


def stack_kernel(*refs):
    out_ref, at = refs[-1], 0
    for ref in refs[:-1]:
        if len(ref.shape) == 3:
            out_ref[at : at + ref.shape[0]] = ref[...]
            at += ref.shape[0]
        else:
            out_ref[at] = ref[...]
            at += 1


def stack(name, *parts):
    count = sum(1 if part.ndim == 2 else part.shape[0] for part in parts)
    (out,) = kernel_call(name, stack_kernel, [like((count,) + parts[0].shape[-2:])], parts)
    return out


def slots_kernel(*refs):
    out_ref = refs[4]
    share, width = (refs[0].shape[0] - EXTRA) // 2, refs[0].shape[1]
    lane = lax.broadcasted_iota(jnp.int32, (2 * share, META), 1)
    row = lax.broadcasted_iota(jnp.int32, (2 * share, META), 0)
    for k, ref in enumerate(refs[:4]):
        at = slice(2 * k * share, 2 * (k + 1) * share)
        out_ref[at, :width] = ref[: 2 * share, :]
        codes = ref[2 * share :, :META].astype(F32)
        spread = jnp.where(row < share, codes[:1, :], codes[1:2, :])
        code = jnp.sum(jnp.where(lane == row % share, spread, 0.0), axis=1, keepdims=True)
        out_ref[at, width:] = jnp.broadcast_to(code, (2 * share, META)).astype(BF)


def attend_kernel(per_block, count, plan, *refs):
    x_ref, tag_ref, doc_ref, bias_ref = refs[:4]
    parts = refs[4:8]
    pieces = refs[8 : 8 + count]
    mine_ref, theirs_ref, a_ref, q_ref, kv_ref, mask_ref, stat_ref, scratch, y_ref = refs[
        8 + count :
    ]
    rows, width = x_ref.shape
    local = a_ref.shape[1]
    slots = kv_ref.shape[0] - rows
    step = slots // 4
    me = lax.axis_index("blk")
    core = lax.axis_index("head") % 2
    weight = whole_matrix(pieces, plan, scratch)
    own = dot(x_ref[...], weight[:, : 3 * local]) + bias_ref[:1, : 3 * local]
    q_ref[...] = own[:, 2 * local :].astype(BF)
    kv_ref[slots:, :] = own[:, : 2 * local].astype(BF)
    row_cluster = lax.broadcasted_iota(jnp.int32, (1, rows), 1) // CLUSTER
    wanted = (1 + doc_ref[...] * per_block + row_cluster).astype(F32)
    for k in range(4):
        part = parts[k]
        kv_ref[k * step : (k + 1) * step, :] = (
            dot(part[:, :width], weight[:, : 2 * local]) + bias_ref[:1, : 2 * local]
        ).astype(BF)
        code = part[:, width : width + 1].astype(F32)
        mask_ref[k * step : (k + 1) * step, :] = jnp.where(code == wanted, 0.0, NEG).astype(BF)
    alone = tag_ref[...] != me * per_block + row_cluster
    diagonal = lax.broadcasted_iota(jnp.int32, (rows, rows), 0) == lax.broadcasted_iota(
        jnp.int32, (rows, rows), 1
    )
    mask_ref[slots:, :] = jnp.where(diagonal & alone, 0.0, NEG).astype(BF)
    mask = mask_ref[...].astype(F32)
    stats = []
    for j in range(local // DH):
        cut = slice(j * DH, (j + 1) * DH)
        scores = dot_last(kv_ref[:, cut], q_ref[:, cut]) * SCALE + mask
        top = jnp.max(scores, axis=0, keepdims=True)
        weights = jnp.exp(scores - top)
        inverse = 1.0 / jnp.sum(weights, axis=0, keepdims=True)
        probs = (weights * inverse).astype(BF)
        value = kv_ref[:, local + j * DH : local + (j + 1) * DH]
        a_ref[:, cut] = dot_first(probs, value).astype(BF)
        stats += [top, inverse]
    stat_ref[...] = jnp.concatenate(stats + [jnp.zeros((8 - len(stats), rows), F32)])
    y_ref[...] = dot_last(a_ref[...], weight[:, 3 * local :])
    half = rows // 2
    mine_ref[...] = y_ref[pl.ds(core * half, half), :]
    theirs_ref[...] = y_ref[pl.ds((1 - core) * half, half), :].astype(BF)


def attend_back_kernel(n, count, plan, *refs):
    own_ref, other_ref, q_ref, kv_ref, mask_ref, stat_ref = refs[:6]
    pieces = refs[6 : 6 + count]
    eb_ref, dq_ref, dkv_ref = refs[6 + count : 9 + count]
    back, scratch = refs[9 + count : -1], refs[-1]
    rows, local = q_ref.shape
    slots = kv_ref.shape[0] - rows
    half = rows // 2
    core = lax.axis_index("head") % 2
    weight = whole_matrix(pieces, plan, scratch)
    eb_ref[pl.ds(core * half, half), :] = own_ref[:half, :]
    eb_ref[pl.ds((1 - core) * half, half), :] = other_ref[:half, :]
    da = dot(eb_ref[...], weight[:, 3 * local :]).astype(BF)
    mask = mask_ref[...].astype(F32)
    for j in range(local // DH):
        cut = slice(j * DH, (j + 1) * DH)
        key, query = kv_ref[:, cut], q_ref[:, cut]
        value = kv_ref[:, local + j * DH : local + (j + 1) * DH]
        scores = dot_last(key, query) * SCALE + mask
        probs = jnp.exp(scores - stat_ref[2 * j : 2 * j + 1, :]) * stat_ref[
            2 * j + 1 : 2 * j + 2, :
        ]
        low = probs.astype(BF)
        dkv_ref[:, local + j * DH : local + (j + 1) * DH] = dot(low, da[:, cut]).astype(BF)
        grad = dot_last(value, da[:, cut])
        delta = jnp.sum(low.astype(F32) * grad, axis=0, keepdims=True)
        grad = (probs * (grad - delta)).astype(BF)
        dkv_ref[:, cut] = (dot(grad, query) * SCALE).astype(BF)
        dq_ref[:, cut] = (dot_first(grad, key) * SCALE).astype(BF)
    if back:
        share = slots // 4 // n
        for t in range(2):
            for z in range(4):
                for k in range(4):
                    at = k * slots // 4 + (2 * z + t) * share
                    to = (z * 4 + k) * share
                    back[t][to : to + share, :] = dkv_ref[at : at + share, :]


def back_kernel(room, left_ref, right_ref, keep_ref, send_ref):
    for k in range(left_ref.shape[0] // room):
        out, to = (send_ref if k % 2 else keep_ref), k // 2 * 2 * room
        out[to : to + room, :] = left_ref[k * room : (k + 1) * room, :]
        out[to + room : to + 2 * room, :] = right_ref[k * room : (k + 1) * room, :]


def token_kernel(n, room, per_block, parts, count, plan, *refs):
    tag_ref, dkv_ref, dq_ref = refs[:3]
    back = refs[3 : 3 + parts]
    pieces = refs[3 + parts : 3 + parts + count]
    mine_ref, theirs_ref, scratch, z_ref = refs[3 + parts + count :]
    rows, local = dq_ref.shape
    slots = n * room
    half = rows // 2
    share = room // 4
    group = lax.axis_index("head")
    core = group % 2
    weight = whole_matrix(pieces, plan, scratch)
    target, rank = places(tag_ref[...], n, per_block, rows)
    if parts > 1:
        target = target ^ lax.axis_index("blk")
    place = target * room + ((rank // share) ^ group) * share + rank % share
    total = dkv_ref[slots:, :].astype(F32)
    step = slots // parts
    for k in range(parts):
        pick = lax.broadcasted_iota(jnp.int32, (step, rows), 0) + k * step == place
        total = total + dot_first(pick.astype(F32).astype(BF), back[k][...])
    z_ref[...] = dot_last(total.astype(BF), weight[:, : 2 * local]) + dot_last(
        dq_ref[...], weight[:, 2 * local : 3 * local]
    )
    mine_ref[...] = z_ref[pl.ds(core * half, half), :]
    theirs_ref[...] = z_ref[pl.ds((1 - core) * half, half), :].astype(BF)


def norm_one_kernel(
    chip_ref, recv_ref, x_ref, vec_ref, h_ref, n_ref, r_ref, hb_ref
):
    half = chip_ref.shape[0]
    core = lax.axis_index("head") % 2
    branch = chip_ref[...].astype(F32) + recv_ref[...].astype(F32) + vec_ref[1:2, :]
    value = x_ref[pl.ds(core * half, half), :].astype(F32) + branch
    h, normal, inverse = norm_forward(value, vec_ref[2:3, :], vec_ref[3:4, :])
    h_ref[...] = h
    n_ref[...] = normal
    r_ref[...] = inverse
    hb_ref[...] = h.astype(BF)


def norm_two_kernel(
    chip_ref, recv_ref, h_ref, vec_ref, c_ref, out_ref, e_ref, eb_ref
):
    half = chip_ref.shape[0]
    core = lax.axis_index("head") % 2
    outer = chip_ref[...].astype(F32) + recv_ref[...].astype(F32) + vec_ref[4:5, :]
    gain_row = vec_ref[5:6, :]
    result, normal, inverse = norm_forward(h_ref[...] + outer, gain_row, vec_ref[6:7, :])
    out_ref[...] = result.astype(BF)
    cotangent = c_ref[pl.ds(core * half, half), :].astype(F32)
    grad, gain, shift = norm_backward(cotangent, normal, inverse, gain_row)
    e_ref[...] = grad
    eb_ref[:half, :] = grad.astype(BF)
    eb_ref[half:, :] = extra_rows(gain, shift)


def norm_back_kernel(chip_ref, recv_ref, e_ref, n_ref, r_ref, vec_ref, out_ref, eb_ref):
    half = chip_ref.shape[0]
    grad = e_ref[...] + (chip_ref[...].astype(F32) + recv_ref[...].astype(F32))
    grad, gain, shift = norm_backward(grad, n_ref[...], r_ref[...], vec_ref[2:3, :])
    out_ref[...] = grad
    eb_ref[:half, :] = grad.astype(BF)
    eb_ref[half:, :] = extra_rows(gain, shift)


def inner_kernel(count, plan, *refs):
    own_ref, other_ref, bias_ref = refs[:3]
    pieces = refs[3 : 3 + count]
    g_ref, slope_ref, scratch = refs[3 + count :]
    half = own_ref.shape[0]
    weight = whole_matrix(pieces, plan, scratch)
    for k, part in enumerate((own_ref, other_ref)):
        u = dot(part[...], weight) + bias_ref[7:8, :]
        below = 0.5 * (1.0 + lax.erf(u * math.sqrt(0.5)))
        g_ref[k * half : (k + 1) * half, :] = (u * below).astype(BF)
        density = jnp.exp(-0.5 * u * u) * (1.0 / math.sqrt(2.0 * math.pi))
        slope_ref[k * half : (k + 1) * half, :] = below + u * density


def outer_kernel(count, plan, *refs):
    g_ref = refs[0]
    pieces = refs[1 : 1 + count]
    mine_ref, theirs_ref, scratch = refs[1 + count :]
    half = mine_ref.shape[0]
    weight = whole_matrix(pieces, plan, scratch)
    mine_ref[...] = dot_last(g_ref[:half, :], weight)
    theirs_ref[...] = dot_last(g_ref[half:, :], weight).astype(BF)


def ff_back_kernel(outer_plan, inner_plan, outer_count, inner_count, *refs):
    own_ref, other_ref, slope_ref = refs[:3]
    outer, inner = refs[3 : 3 + outer_count], refs[3 + outer_count :][:inner_count]
    mine_ref, theirs_ref, du_ref, scratch, scratch_two = refs[3 + outer_count + inner_count :]
    half = mine_ref.shape[0]
    outer = whole_matrix(outer, outer_plan, scratch)
    inner = whole_matrix(inner, inner_plan, scratch_two)
    for k, part in ((1, other_ref), (0, own_ref)):
        rows = slice(k * half, (k + 1) * half)
        dg = dot(part[:half, :], outer).astype(BF).astype(F32)
        du_ref[rows, :] = (dg * slope_ref[rows, :]).astype(BF)
        dh = dot_last(du_ref[rows, :], inner)
        if k:
            theirs_ref[...] = dh.astype(BF)
        else:
            mine_ref[...] = dh


def halves(blocks, bit):
    return [b for b in blocks if not b & bit], [b for b in blocks if b & bit]


def split_pieces(total, bit, mine_ref, theirs_ref):
    me = lax.axis_index("blk")
    rows = total.shape[0] // 8
    for out, blocks in zip((mine_ref, theirs_ref), halves(range(8), bit)):
        for k, block in enumerate(blocks):
            out[k * rows : (k + 1) * rows, :] = total[pl.ds((me ^ block) * rows, rows), :].astype(BF)


def ff_weights_kernel(small, own_ref, other_ref, left_ref, *refs):
    half = left_ref.shape[0] // 2
    refs = list(refs)
    total = refs.pop()
    total[...] = dot_first(own_ref[:half, :], left_ref[:half, :]) + dot_first(
        other_ref[:half, :], left_ref[half:, :]
    )
    if small == "outer":
        small_ref = refs.pop()
        norms = own_ref[half:, :].astype(F32) + other_ref[half:, :].astype(F32)
        bias = jnp.sum(own_ref[:half, :].astype(F32), axis=0, keepdims=True) + jnp.sum(
            other_ref[:half, :].astype(F32), axis=0, keepdims=True
        )
        small_ref[...] = jnp.concatenate([norms[:2], bias, jnp.zeros((5, bias.shape[1]), F32)])
    else:
        small_ref = refs.pop()
        bias = jnp.sum(left_ref[...].astype(F32), axis=0, keepdims=True)
        small_ref[...] = jnp.concatenate([bias, jnp.zeros((7, bias.shape[1]), F32)])
    if len(refs) == 1:
        refs[0][...] = total[...]
    else:
        split_pieces(total, 1 if small == "outer" else 2, *refs)


def attend_weights_kernel(*refs):
    x_ref, p0, p1, p2, p3, dkv_ref, dq_ref, eb_ref, a_ref, own_ref, other_ref = refs[:11]
    outer_ref, inner_ref = refs[11:13]
    outs, total = list(refs[13:-1]), refs[-1]
    rows, width = x_ref.shape
    local = dq_ref.shape[1]
    slots = dkv_ref.shape[0] - rows
    step = slots // 4
    sums = dot_first(x_ref[...], dkv_ref[slots:, :])
    for k, part in enumerate((p0, p1, p2, p3)):
        sums = sums + dot_first(part[:, :width], dkv_ref[k * step : (k + 1) * step, :])
    total[:, : 2 * local] = sums
    total[:, 2 * local : 3 * local] = dot_first(x_ref[...], dq_ref[...])
    total[:, 3 * local :] = dot_first(eb_ref[...], a_ref[...])
    half = rows // 2
    norms = own_ref[half:, :].astype(F32) + other_ref[half:, :].astype(F32)
    output_b = jnp.sum(eb_ref[...].astype(F32), axis=0, keepdims=True)
    query_b = jnp.sum(dq_ref[...].astype(F32), axis=0, keepdims=True)
    value_b = jnp.sum(dkv_ref[...].astype(F32), axis=0, keepdims=True)
    last = jnp.concatenate([value_b, query_b, jnp.zeros((1, width - 3 * local), F32)], axis=1)
    small = jnp.concatenate(
        [
            outer_ref[:3, :],
            inner_ref[:1, :],
            norms[:2],
            output_b,
            last,
        ]
    )
    if outs[0].shape == total.shape:
        outs[0][...] = total[...]
        outs[1][...] = small
    else:
        split_pieces(total, 1, *outs)
        body = outs[0].shape[0] - EXTRA
        outs[0][body:, :] = small.astype(BF)
        outs[1][body:, :] = small.astype(BF)


def middle_kernel(extra, blocks, bit, mine_ref, recv_ref, *outs):
    rows = (mine_ref.shape[0] - extra) // len(blocks)
    last = mine_ref.shape[0] - extra
    for out, pieces in zip(outs, halves(blocks, bit)):
        for k, piece in enumerate(pieces):
            at = slice(blocks.index(piece) * rows, (blocks.index(piece) + 1) * rows)
            out[k * rows : (k + 1) * rows, :] = (
                mine_ref[at, :].astype(F32) + recv_ref[at, :].astype(F32)
            ).astype(BF)
        if extra:
            small = mine_ref[last:, :].astype(F32) + recv_ref[last:, :].astype(F32)
            out[len(pieces) * rows :, :] = small.astype(BF)


def pair_kernel(*refs):
    inputs, keeps, send_ref = refs[:4], refs[4:6], refs[6]
    rows = keeps[0].shape[0]
    for k, keep_ref in enumerate(keeps):
        mine_ref, recv_ref = inputs[2 * k : 2 * k + 2]
        total = (mine_ref[...].astype(F32) + recv_ref[...].astype(F32)).astype(BF)
        keep_ref[...] = total[:rows, :]
        send_ref[k * rows : (k + 1) * rows, :] = total[rows:, :]


def last_pair_kernel(first_ref, second_ref, recv_ref, *outs):
    rows = first_ref.shape[0]
    for k, ref in enumerate((first_ref, second_ref)):
        recv = recv_ref[k * rows : (k + 1) * rows, :]
        outs[k][...] = ref[...].astype(F32) + recv.astype(F32)


def last_kernel(left_ref, right_ref, *outs):
    total = left_ref[...].astype(F32) + right_ref[...].astype(F32)
    if len(outs) == 1:
        outs[0][...] = total
        return
    rows, local = outs[0].shape
    for k in range(4):
        outs[k][...] = total[:rows, k * local : (k + 1) * local]
    spread_small(total[rows:, :], local, outs[4:])


def spread_small(small, local, outs):
    for k, out in enumerate(outs[:7]):
        out[...] = small[k, :]
    outs[7][...] = small[7, 2 * local : 3 * local]
    outs[8][...] = small[7, local : 2 * local]


def small_kernel(small_ref, *outs):
    spread_small(small_ref[...], outs[7].shape[0], outs)


def scatter_step(name, mine, recv, blocks, bit, extra=0):
    rows = (mine.shape[0] - extra) // 2 + extra
    return kernel_call(
        name,
        functools.partial(middle_kernel, extra, blocks, bit),
        [like((rows, mine.shape[1]))] * 2,
        [mine, recv],
    )


def chip_sum(mine, theirs, name):
    chip = (mine + swap(theirs, "head", 1, name + "_chip").astype(F32)).astype(BF)
    return chip, swap(chip, "head", 2, name + "_x")


def per_device(
    hidden_in,
    query_w,
    key_w,
    value_w,
    output_w,
    inner_w,
    outer_w,
    query_b,
    value_b,
    output_b,
    inner_b,
    outer_b,
    first_gain,
    first_shift,
    second_gain,
    second_shift,
    key_cluster,
    document,
    cotangent,
):
    rows, width = hidden_in.shape
    n = lax.axis_size("blk")
    groups = lax.axis_size("head")
    assert groups == 4
    local = query_w.shape[1]
    units = inner_w.shape[1]
    per_block = rows // CLUSTER
    room = 2 * rows // n
    slots = n * room
    half = rows // 2
    share = room // groups
    staged = n == 8
    core = lax.axis_index("head") % 2

    tag_row, doc_row = key_cluster.reshape(1, rows), document.reshape(1, rows)

    if staged:
        sends = [like((4 * share + EXTRA, width))] * 2
    else:
        sends = [like((n * share, width + META))]
    pack_args = [key_w, value_w, query_w, output_w, inner_w, outer_w]
    pack_args += [hidden_in, tag_row, doc_row, value_b, query_b, output_b]
    pack_args += [first_gain, first_shift, outer_b, second_gain, second_shift, inner_b]
    *sent, attend_w, ff_w, vectors = kernel_call(
        "pack",
        functools.partial(pack_kernel, n, room, per_block, groups),
        sends
        + [
            like((width // n, 4 * local)),
            like((width // n, 2 * units)),
            like((8, width), F32),
        ],
        [pltpu.with_memory_space_constraint(item, pltpu.HBM) for item in pack_args],
        [pltpu.VMEM(item.shape, item.dtype) for item in pack_args]
        + [pltpu.SemaphoreType.DMA((len(pack_args),))],
        flops=2 * n * share * rows * width,
        space=pltpu.HBM,
    )
    if staged:
        attend_column = [
            swap(attend_w, "blk", bits, f"attend_w_z{bits}") for bits in (2, 4, 6)
        ]
        slots_y = swap(sent[1], "blk", 1, "slots_y")
        messages = kernel_call(
            "route", route_kernel, [like((2 * share + EXTRA, width))] * 4, [sent[0], slots_y]
        )
        arrived = [messages[0]] + [
            swap(messages[k], "blk", 2 * k, f"slots_z{2 * k}") for k in (1, 2, 3)
        ]
        (moved,) = kernel_call("slots", slots_kernel, [like((n * share, width + META))], arrived)
        column = order(attend_column, messages[0])
        column = stack("attend_w_column", attend_w, *column)
        rest = swap(column, "blk", 1, "attend_w_rest")
        attend_p = [attend_w] + attend_column + [rest]
        inner_far = swap(order(inner_w, *attend_column), "blk", 4, "inner_w_far")
        inner_near = swap(stack("inner_w_pair", inner_w, inner_far), "blk", 2, "inner_w_near")
        outer_far = swap(order(outer_w, inner_far), "blk", 4, "outer_w_far")
    else:
        moved = lax.all_to_all(sent[0].reshape(n, share, width + META), "blk", 0, 0)
        moved = moved.reshape(sent[0].shape)
        gather = lambda value: [lax.all_gather(value, "blk", axis=0, tiled=True)]
        attend_p, inner_p, outer_p = gather(attend_w), gather(inner_w), gather(outer_w)
    far = swap(moved, "head", 2, "slots_x")
    parts = [moved, swap(moved, "head", 1, "slots_chip"), far, swap(far, "head", 1, "slots_far")]
    attend_plan = [((0,), 0), ((2,), 0), ((4,), 0), ((6,), 0), ((1, 3, 5, 7), 0)]
    inner_plan = [((0,), 0), ((1,), 0), ((4,), 0), ((2, 6), 0), ((5, 3, 7), 0)]
    outer_plan = [((0,), 0), ((1,), units), ((4,), 0), ((2, 6), 0), ((5, 3, 7), 0)]

    count = len(attend_p)
    mine, theirs, a, q, kv, mask, stat = kernel_call(
        "attend",
        functools.partial(attend_kernel, per_block, count, attend_plan),
        [
            like((half, width), F32),
            like((half, width)),
            like((rows, local)),
            like((rows, local)),
            like((slots + rows, 2 * local)),
            like((slots + rows, rows)),
            like((8, rows), F32),
        ],
        [hidden_in, tag_row, doc_row, vectors] + parts + attend_p,
        [piece_scratch(attend_p, 4 * local), pltpu.VMEM((rows, width), F32)],
        flops=2 * rows * width * local * 9,
    )
    if staged:
        facing = swap(order(ff_w, far), "blk", 1, "facing_w")
        outer_far = order(outer_far, theirs)
        outer_near = swap(stack("outer_w_pair", outer_w, outer_far), "blk", 2, "outer_w_near")
        inner_rest = stack("inner_w_column", inner_far, inner_near)
        inner_rest = swap(inner_rest, "blk", 1, "inner_w_rest")
        outer_rest = stack("outer_w_column", outer_far, outer_near)
        outer_rest = swap(outer_rest, "blk", 1, "outer_w_rest")
        inner_p = [inner_w, facing, inner_far, inner_near, inner_rest]
        outer_p = [outer_w, facing, outer_far, outer_near, outer_rest]
        mine = order(mine, facing, outer_far)
    chip, recv = chip_sum(mine, theirs, "branch")
    if staged:
        recv = order(recv, outer_near)
    h, normal_one, inv_one, hb = kernel_call(
        "norm_one",
        norm_one_kernel,
        [
            like((half, width), F32),
            like((half, width), F32),
            like((half, 1), F32),
            like((half, width)),
        ],
        [chip, recv, hidden_in, vectors],
    )
    hb_other = swap(hb, "head", 1, "hb")

    g, slope = kernel_call(
        "inner",
        functools.partial(inner_kernel, len(inner_p), inner_plan),
        [like((rows, units)), like((rows, units), F32)],
        [hb, hb_other, vectors] + inner_p,
        [piece_scratch(inner_p, units)],
        flops=2 * rows * width * units,
    )
    mine, theirs = kernel_call(
        "outer",
        functools.partial(outer_kernel, len(outer_p), outer_plan),
        [like((half, width), F32), like((half, width))],
        [g] + outer_p,
        [piece_scratch(outer_p, units)],
        flops=2 * rows * width * units,
    )
    chip, recv = chip_sum(mine, theirs, "ff")
    result, e_two, eb_two = kernel_call(
        "norm_two",
        norm_two_kernel,
        [like((half, width)), like((half, width), F32), like((half + EXTRA, width))],
        [chip, recv, h, vectors, cotangent],
    )
    eb_two_other = swap(eb_two, "head", 1, "eb_two")
    mine, theirs, du = kernel_call(
        "ff_back",
        functools.partial(
            ff_back_kernel, outer_plan, inner_plan, len(outer_p), len(inner_p)
        ),
        [like((half, width), F32), like((half, width)), like((rows, units))],
        [eb_two, eb_two_other, slope] + outer_p + inner_p,
        [piece_scratch(outer_p, units), piece_scratch(inner_p, units)],
        flops=4 * rows * width * units,
    )
    if staged:
        grad_outs = [like((width // 2, units)), like((width // 2, units))]
    else:
        grad_outs = [like((width, units), F32)]
    outer_g = kernel_call(
        "outer_grad",
        functools.partial(ff_weights_kernel, "outer"),
        grad_outs + [like((8, width), F32)],
        [eb_two, eb_two_other, g],
        [pltpu.VMEM((width, units), F32)],
        flops=2 * rows * width * units,
    )
    mine = order(mine, outer_g[0])
    chip, recv = chip_sum(mine, theirs, "ff_back")
    inner_g = kernel_call(
        "inner_grad",
        functools.partial(ff_weights_kernel, "inner"),
        grad_outs + [like((8, units), F32)],
        [hb, hb_other, du],
        [pltpu.VMEM((width, units), F32)],
        flops=2 * rows * width * units,
    )
    recv = order(recv, outer_g[0], inner_g[0])
    grad_units = [like((width // n, units), F32)]
    if staged:
        outer_y = swap(outer_g[1], "blk", 1, "outer_g_y")
        inner_near = swap(inner_g[1], "blk", 2, "inner_g_near")
    else:
        grad_outer_w = lax.psum_scatter(outer_g[0], "blk", scatter_dimension=0, tiled=True)
        grad_inner_w = lax.psum_scatter(inner_g[0], "blk", scatter_dimension=0, tiled=True)

    e_one, eb_one = kernel_call(
        "norm_back",
        norm_back_kernel,
        [like((half, width), F32), like((half + EXTRA, width))],
        [chip, recv, e_two, normal_one, inv_one, vectors],
    )
    eb_one_other = swap(eb_one, "head", 1, "eb_one")
    back_outs = [like((slots // 2, 2 * local))] * 2 if staged else []
    eb_full, dq, dkv, *back = kernel_call(
        "attend_back",
        functools.partial(attend_back_kernel, n, count, attend_plan),
        [
            like((rows, width)),
            like((rows, local)),
            like((slots + rows, 2 * local)),
        ]
        + back_outs,
        [eb_one, eb_one_other, q, kv, mask, stat] + attend_p,
        [piece_scratch(attend_p, 4 * local)],
        flops=2 * rows * width * local * 8,
    )
    if staged:
        back_y = swap(back[1], "blk", 1, "back_y")
        outer_k, outer_s = scatter_step("outer_g_one", outer_g[0], outer_y, [0, 2, 4, 6], 2)
        inner_near = order(inner_near, outer_k)
        inner_k, inner_s = scatter_step("inner_g_one", inner_g[0], inner_near, [0, 1, 4, 5], 1)
        dq = order(dq, inner_k, outer_k)
        grad_outs = [like((width // 2 + EXTRA, width))] * 2
    else:
        grad_outs = [like((width, width), F32), like((EXTRA, width), F32)]
    attend_g = kernel_call(
        "attend_grad",
        attend_weights_kernel,
        grad_outs,
        [hidden_in] + parts + [dkv, dq, eb_full, a, eb_one, eb_one_other, outer_g[-1], inner_g[-1]],
        [pltpu.VMEM((width, width), F32)],
        flops=2 * rows * width * local * 8,
    )
    if staged:
        back_y = order(back_y, attend_g[1])
        attend_y = swap(order(attend_g[1], back_y), "blk", 1, "attend_g_y")
        half_slots = [like((slots // 2, 2 * local))] * 2
        back_k, back_s = kernel_call(
            "back_one", functools.partial(back_kernel, room), half_slots, [back[0], back_y]
        )
        back_near = swap(back_s, "blk", 2, "back_near")
        outer_near = swap(order(outer_s, back_near), "blk", 2, "outer_g_near")
        inner_y = swap(inner_s, "blk", 1, "inner_g_y")
        back_k, back_s = kernel_call(
            "back_two", functools.partial(back_kernel, 2 * room), half_slots, [back_k, back_near]
        )
        moved = [back_k, swap(back_s, "blk", 4, "back_far")]
        attend_k, attend_s = scatter_step(
            "attend_g_one", attend_g[0], attend_y, [0, 2, 4, 6], 2, EXTRA
        )
        piece = like((width // n, units))
        inner_k, outer_k, both = kernel_call(
            "pair",
            pair_kernel,
            [piece, piece, like((2 * width // n, units))],
            [inner_k, inner_y, outer_k, outer_near],
        )
        moved[0] = order(moved[0], attend_k)
        both = swap(order(both, moved[1]), "blk", 4, "both_far")
        grad_inner_w, grad_outer_w = kernel_call(
            "pair_last", last_pair_kernel, grad_units * 2, [inner_k, outer_k, both]
        )
    else:
        moved = dkv[:slots].reshape(4, n, share, 2 * local).transpose(1, 0, 2, 3)
        moved = lax.all_to_all(moved, "blk", 0, 0).reshape(slots, 2 * local)
        moved = [moved]
    mine, theirs = kernel_call(
        "token",
        functools.partial(
            token_kernel, n, room, per_block, len(moved), count, attend_plan
        ),
        [like((half, width), F32), like((half, width))],
        [tag_row, dkv, dq] + moved + attend_p,
        [piece_scratch(attend_p, 4 * local), pltpu.VMEM((rows, width), F32)],
        flops=2 * rows * width * local * 4,
    )
    if staged:
        mine = order(mine, inner_k)
    result_other = swap(result, "head", 1, "result")

    def joined(own, other):
        return jnp.where(
            core == 0, jnp.concatenate([own, other]), jnp.concatenate([other, own])
        )

    layer_out = joined(result, result_other)
    chip, recv = chip_sum(mine, theirs, "last")
    if staged:
        attend_near = swap(attend_s, "blk", 2, "attend_g_near")
        attend_k, attend_s = scatter_step(
            "attend_g_two", attend_k, attend_near, [0, 4], 4, EXTRA
        )
        recv = order(recv, attend_k, grad_inner_w, layer_out)
    last = e_one + (chip.astype(F32) + recv.astype(F32))
    last_other = swap(last, "head", 1, "last")
    grad_input = joined(last, last_other)
    small_outs = [like((width,), F32)] * 7 + [like((local,), F32)] * 2
    if staged:
        attend_far = swap(attend_s, "blk", 4, "attend_g_far")
        attend_far = order(attend_far, grad_input)
        grads = kernel_call(
            "attend_g_last",
            last_kernel,
            [like((width // n, local), F32)] * 4 + small_outs,
            [attend_k, attend_far],
        )
        grads, small = grads[:4], grads[4:]
    else:
        summed = lax.psum_scatter(attend_g[0], "blk", scatter_dimension=0, tiled=True)
        grads = [summed[:, k * local : (k + 1) * local] for k in range(4)]
        small = kernel_call("small", small_kernel, small_outs, [lax.psum(attend_g[1], "blk")])
    grad_key_w, grad_value_w, grad_query_w, grad_output_w = grads

    return (
        layer_out,
        grad_input,
        grad_query_w,
        grad_key_w,
        grad_value_w,
        grad_output_w,
        grad_inner_w,
        grad_outer_w,
        small[7],
        small[8],
        small[6],
        small[3],
        small[2],
        small[4],
        small[5],
        small[0],
        small[1],
    )


def solution(mesh):
    matrix = P("blk", "head")
    in_specs = (
        (P("blk", None),)
        + (matrix,) * 6
        + (P("head"), P("head"), P(), P("head"))
        + (P(),) * 5
        + (P("blk"), P("blk"), P("blk", None))
    )
    out_specs = (
        (P("blk", None), P("blk", None))
        + (matrix,) * 6
        + (P("head"), P("head"), P(), P("head"))
        + (P(),) * 5
    )
    return jax.shard_map(
        per_device, mesh=mesh, in_specs=in_specs, out_specs=out_specs, check_vma=False
    )
```
